256 devices in a mesh: gx: 16 (over y_lo, z), gy: 8 (over x, core), gz: 2 (over y_hi).
Axes of the slice: x: 4, y: 4 (y_hi: 2, y_lo: 2; y = y_hi * 2 + y_lo), z: 8, core: 2. Of those that a mesh axis runs over, the one named last changes fastest.
Arguments:
- features: bfloat16 [32, 64, 256, 256], P(None, 'gx', 'gy', 'gz'), may hold values from -6 to 6
- conv_weight: bfloat16 [32, 32, 3, 3, 3], replicated, may hold values from -0.21875 to 0.21875
- conv_bias: float32 [32], replicated, may hold values from -3 to 3
- head_weight: bfloat16 [3, 32], replicated, may hold values from -1 to 1
- head_bias: float32 [3], replicated, may hold values from 1.5 to 3
- mask: int32 [64, 256, 256], P('gx', 'gy', 'gz'), may hold values 0 or 1
- seeds: int32 [64, 256, 256], P('gx', 'gy', 'gz'), may hold values from 0 to 15, as said below
Outputs:
- affinity: bfloat16 [3, 64, 256, 256], P(None, 'gx', 'gy', 'gz')
- propagated: float32 [64, 256, 256], P('gx', 'gy', 'gz')
The draws below stay inside these ranges and needn't reach their ends.
Inputs may be any that keep to these rules, and one draw needn't show every extreme that they name: `seeds`: seed value of a voxel; 0 where the voxel holds no seed.
All inputs are finite; a program needn't handle non-finite values. No bound on the sum of `mask` on one device may be relied on, other than what follows from the above.
Results may differ from the reference program's by a relative error of at most 0.0026.
Values may be sent and summed in bfloat16 or wider, within the bound.
No kernel may reach another device: no remote copies, remote signals or barrier semaphores. Data moves between devices by JAX's collectives and lax.ppermute only.
A program may use at most 128 MiB of HBM per device.

```python
import jax
import jax.numpy as jnp
from jax import lax

CH = 32
ROUNDS = 4
CX = 4
NX = 64
NY = 256
NZ = 256
N_GX = 16


def draw_seeds(key, part):
    first_key, second_key, third_key = jax.random.split(jax.random.fold_in(key, 7), 3)
    present = jax.random.randint(first_key, (NX, NY, NZ), 0, 32) == 0
    levels = jax.random.randint(second_key, (NX, NY, NZ), 1, 16)
    seed_grid = jnp.where(present, levels, 0).astype(jnp.int32).reshape(-1)
    position = jax.random.randint(third_key, (), 0, NX * NY * NZ)
    seed_grid = seed_grid.at[position].set(15)
    return seed_grid.reshape(NX, NY, NZ).astype(jnp.int32)


def with_ends(values, stream_key, smallest, high):
    place = [jax.random.randint(jax.random.fold_in(stream_key, axis), (), 0, length) for axis, length in enumerate(values.shape)]
    longest = values.shape.index(max(values.shape))
    next_to = place[:longest] + [(place[longest] + 1) % values.shape[longest]] + place[longest + 1:]
    return values.at[tuple(place)].set(smallest).at[tuple(next_to)].set(high)


def steps_of(rng, shape, cuts, smallest, high):
    def one(dim, blocks):
        steps = jax.random.uniform(jax.random.fold_in(jax.random.fold_in(rng, 6), dim), (blocks,), jnp.float32, smallest / len(cuts), high / len(cuts))
        return jnp.repeat(jnp.exp(steps), shape[dim] // blocks).reshape((-1,) + (1,) * (len(shape) - dim - 1))

    factor_of = one(*cuts[0])
    for cut in cuts[1:]:
        factor_of = factor_of * one(*cut)
    return factor_of


def scatter_about(key, dims, deviation, bound, pieces=(), kind=jnp.bfloat16):
    drawn = deviation * jax.random.normal(key, dims, jnp.float32)
    if pieces:
        drawn = drawn * steps_of(key, dims, pieces, -0.22, 0.18)
    return jnp.clip(drawn, -bound, bound).astype(kind)


def setup_inputs(seed: int = 0) -> dict:
    key_of = jax.random.split(jax.random.key(seed), 8)
    features = scatter_about(key_of[0], (CH, NX, NY, NZ), 1.0, 6.0, ((1, 16), (2, 8), (3, 2)))
    conv_weight = scatter_about(key_of[1], (CH, CH, 3, 3, 3), (CH * 27) ** -0.5, 0.21875)
    conv_bias = scatter_about(key_of[2], (CH,), 0.5, 3.0, (), jnp.float32)
    head_weight = scatter_about(key_of[3], (3, CH), CH ** -0.5, 1.0)
    head_bias = jnp.clip(jax.random.uniform(key_of[4], (3,), jnp.float32, 1.5, 3.0), 1.5, 3.0)
    mask = with_ends((jax.random.randint(key_of[5], (NX, NY, NZ), 0, 4) < 3).astype(jnp.int32), jax.random.fold_in(key_of[5], 1), 0, 1)
    seeds = draw_seeds(jax.random.fold_in(key_of[7], 71), 0)
    return {"features": features, "conv_weight": conv_weight, "conv_bias": conv_bias, "head_weight": head_weight, "head_bias": head_bias, "mask": mask, "seeds": seeds}


def affinities(window, conv_weight, conv_bias, head_weight, head_bias):
    conv_out = lax.conv_general_dilated(window[None], conv_weight, (1, 1, 1), "VALID", dimension_numbers=("NCDHW", "OIDHW", "NCDHW"), preferred_element_type=jnp.float32)[0]
    hidden = jnp.maximum(conv_out + conv_bias[:, None, None, None], 0.0).astype(jnp.bfloat16)
    hidden_shape = hidden.shape
    logits = jnp.dot(head_weight, hidden.reshape(hidden_shape[0], -1), preferred_element_type=jnp.float32) + head_bias[:, None]
    return jax.nn.sigmoid(logits).astype(jnp.bfloat16).reshape((3,) + hidden_shape[1:])


def propagate(initial, foreground, own_edges, next_x, next_y, next_z):
    strength = initial
    for round_index in range(ROUNDS):
        padded = jnp.pad(strength, 1)
        highest = strength
        highest = jnp.maximum(highest, jnp.minimum(padded[:-2, 1:-1, 1:-1], own_edges[0]))
        highest = jnp.maximum(highest, jnp.minimum(padded[2:, 1:-1, 1:-1], next_x))
        highest = jnp.maximum(highest, jnp.minimum(padded[1:-1, :-2, 1:-1], own_edges[1]))
        highest = jnp.maximum(highest, jnp.minimum(padded[1:-1, 2:, 1:-1], next_y))
        highest = jnp.maximum(highest, jnp.minimum(padded[1:-1, 1:-1, :-2], own_edges[2]))
        highest = jnp.maximum(highest, jnp.minimum(padded[1:-1, 1:-1, 2:], next_z))
        strength = foreground * highest
    return strength


def reference(features, conv_weight, conv_bias, head_weight, head_bias, mask, seeds):
    padded = jnp.pad(features, ((0, 0), (1, 1), (1, 1), (1, 1)))

    def slab(slab_index):
        window = lax.dynamic_slice_in_dim(padded, slab_index * CX, CX + 2, 1)
        return affinities(window, conv_weight, conv_bias, head_weight, head_bias)

    slabs = lax.map(slab, jnp.arange(N_GX, dtype=jnp.int32))
    affinity = jnp.transpose(slabs, (1, 0, 2, 3, 4)).reshape(3, NX, NY, NZ)
    own_edges = affinity.astype(jnp.float32)
    next_x = jnp.pad(own_edges[0], ((0, 1), (0, 0), (0, 0)))[1:]
    next_y = jnp.pad(own_edges[1], ((0, 0), (0, 1), (0, 0)))[:, 1:]
    next_z = jnp.pad(own_edges[2], ((0, 0), (0, 0), (0, 1)))[:, :, 1:]
    foreground = mask.astype(jnp.float32)
    initial = foreground * (seeds.astype(jnp.float32) / 15.0)
    propagated = propagate(initial, foreground, own_edges, next_x, next_y, next_z)
    return affinity, propagated
```

```python
import jax
import jax.numpy as jnp
from jax import lax
from jax.experimental import pallas as pl
from jax.experimental.pallas import tpu as pltpu
from jax.sharding import PartitionSpec as P

ROUNDS = 4
F32 = jnp.float32
BF16 = jnp.bfloat16
VMEM = pl.BlockSpec(memory_space=pltpu.VMEM)
SMEM = pl.BlockSpec(memory_space=pltpu.SMEM)
PARAMS = pltpu.CompilerParams(vmem_limit_bytes=48 * 2**20)


def swaps(axis):
    count = lax.axis_size(axis)

    def pairs(first):
        return [p for i in range(first, count - 1, 2) for p in ((i, i + 1), (i + 1, i))]

    return pairs(0), pairs(1)


def iota(shape, dim):
    return lax.broadcasted_iota(jnp.int32, shape, dim)


def pack_kernel(where_ref, x_ref, m_ref, s_ref, v_ref, zs_ref):
    gz = where_ref[2]
    for x in range(4):
        v_ref[x, 5:37] = jnp.swapaxes(x_ref[:, x], 0, 1)
    lane = iota((128, 128), 1)
    row = iota((128, 128), 0)
    base = jnp.where(gz == 0, 120, 0)
    hit = row == base + lane % 8
    acc = jnp.zeros((256, 128), F32)
    for y in range(16):
        sel = jnp.where(hit & (lane // 8 == y), 1.0, 0.0).astype(BF16)
        lhs = jnp.concatenate(
            [v_ref[x, 5 + 16 * half + y] for x in range(4) for half in range(2)], axis=0
        )
        acc = acc + jnp.dot(lhs, sel, preferred_element_type=F32)
    zs_ref[0:256] = acc.astype(BF16)
    lane = iota((32, 128), 1)
    edge = (lane >= jnp.where(gz == 0, 124, 0)) & (lane < jnp.where(gz == 0, 128, 4))
    packed = jnp.zeros((32, 128), F32)
    for x in range(4):
        mask = m_ref[x].astype(F32)
        seed = mask * s_ref[x].astype(F32)
        for slot, value in ((x, mask), (4 + x, seed)):
            value = jnp.where(edge, value, 0.0)
            packed = packed + (pltpu.roll(value, 8 * slot, 1) if slot else value)
    zs_ref[256:288] = packed.astype(BF16)


def unpack_ext(packed, slot, gz):
    lane = iota(packed.shape, 1)
    inside = (lane >= jnp.where(gz == 0, 0, 124)) & (lane < jnp.where(gz == 0, 4, 128))
    value = pltpu.roll(packed, (128 - 8 * slot) % 128, 1) if slot else packed
    return jnp.where(inside, value, 0.0)


def yface_kernel(where_ref, v_ref, zs_ref, zr_ref, m_ref, s_ref, pt_ref, ye_ref, yo_ref, ms_ref):
    odd = where_ref[1] % 2
    gz = where_ref[2]
    lane = iota((256, 128), 1) % 8
    own = pltpu.roll(zs_ref[0:256].astype(F32), jnp.where(gz == 0, 122, 5), 1)
    other = pltpu.roll(zr_ref[0:256].astype(F32), jnp.where(gz == 0, 2, 125), 1)
    own_from = jnp.where(gz == 0, 0, 5)
    other_from = jnp.where(gz == 0, 2, 0)
    packed = jnp.where((lane >= own_from) & (lane < own_from + 2), own, 0.0)
    packed = jnp.where((lane >= other_from) & (lane < other_from + 5), other, packed)
    packed = packed.astype(BF16).reshape(4, 2, 32, 128)
    pt_ref[...] = packed
    zmask = zr_ref[256:288].astype(F32)
    for x in range(4):
        mask = m_ref[x].astype(F32)
        seed = mask * s_ref[x].astype(F32)
        fields = (mask, seed, unpack_ext(zmask, x, gz), unpack_ext(zmask, 4 + x, gz))
        for f, value in enumerate(fields):
            ms_ref[0, x, 4 * f : 4 * f + 4] = value[28:32]
            ms_ref[1, x, 4 * f : 4 * f + 4] = value[0:4]

    def write(dst_ref, up):
        for x in range(4):
            first = 32 if up else 5
            for j in range(5):
                dst_ref[x, 32 * j : 32 * j + 32] = v_ref[x, first + j]
            dst_ref[x, 160:192] = pt_ref[x, 1 if up else 0]
            dst_ref[x, 192:208] = ms_ref[0 if up else 1, x].astype(BF16)

    @pl.when(odd == 0)
    def _():
        write(ye_ref, True)
        write(yo_ref, False)

    @pl.when(odd == 1)
    def _():
        write(ye_ref, False)
        write(yo_ref, True)


def xface_kernel(where_ref, v_in_ref, pt_ref, ye_ref, yo_ref, v_ref, xe_ref, xo_ref):
    odd_x = where_ref[0] % 2
    odd_y = where_ref[1] % 2

    def fill(low_ref, high_ref):
        for x in range(4):
            for j in range(5):
                v_ref[x, j] = low_ref[x, 32 * j : 32 * j + 32]
                v_ref[x, 37 + j] = high_ref[x, 32 * j : 32 * j + 32]
            v_ref[x, 42] = low_ref[x, 160:192]
            v_ref[x, 43] = pt_ref[x, 0]
            v_ref[x, 44] = pt_ref[x, 1]
            v_ref[x, 45] = high_ref[x, 160:192]

    @pl.when(odd_y == 0)
    def _():
        fill(yo_ref, ye_ref)

    @pl.when(odd_y == 1)
    def _():
        fill(ye_ref, yo_ref)

    even_face = jnp.where(odd_x == 0, 3, 0)
    xe_ref[...] = v_ref[even_face]
    xo_ref[...] = v_ref[3 - even_face]


def head(hidden, head_ref, head_bias):
    logits = jnp.dot(head_ref, hidden, preferred_element_type=F32) + head_bias
    return jax.nn.sigmoid(logits).astype(BF16).astype(F32)


def conv_slice(gz, refs, w, wp, bias, hw, hb, hwp, hbp, out_ref, ext_ref, x):
    lane = iota((32, 128), 1)

    def pair(t0, t1):
        cols = []
        for t in (t0, t1):
            cols.append(
                jnp.concatenate([r[pl.ds(t - 1, 3)].reshape(96, 128) for r in refs], axis=0)
            )
        part = jnp.dot(w, jnp.concatenate(cols, axis=1), preferred_element_type=F32)
        rows = []
        for i in range(2):
            one = part[:, 128 * i : 128 * i + 128]
            left = jnp.where(lane == 0, 0.0, pltpu.roll(one[0:32], 1, 1))
            right = jnp.where(lane == 127, 0.0, pltpu.roll(one[64:96], 127, 1))
            rows.append(jnp.maximum(one[32:64] + left + right + bias, 0.0).astype(BF16))
        return rows

    def group(starts, row):
        rows = []
        for t in starts:
            rows += pair(t, t + 1)
        value = head(jnp.concatenate(rows, axis=0), hw, hb)
        for c in range(3):
            out_ref[x, c, pl.ds(row, 8)] = value[8 * c : 8 * c + 8]

    @pl.loop(0, 4)
    def _(g):
        row = pl.multiple_of(8 * g, 8)
        group([row + 5 + 2 * i for i in range(4)], row)

    group([37, 39, 1, 3], 32)

    cols = [
        jnp.concatenate([r[42 + q] for r in refs], axis=0) for q in range(4)
    ]
    part = jnp.dot(wp, jnp.concatenate(cols, axis=1), preferred_element_type=F32)
    total = jnp.zeros((32, 512), F32)
    for dy in range(3):
        for dz in range(3):
            k = 3 * dy + dz
            shift = (-(8 * (dy - 1) + dz - 1)) % 512
            one = part[32 * k : 32 * k + 32]
            total = total + (pltpu.roll(one, shift, 1) if shift else one)
    hidden = jnp.maximum(total + bias[:, 0:1], 0.0).astype(BF16)
    value = head(hidden, hwp, hbp)
    row = iota((40, 512), 0)
    at = iota((40, 512), 1)
    mine = at // 8 - 16 == jnp.where(row < 36, row, row - 40)
    lhs = jnp.concatenate(
        [jnp.where(mine, jnp.broadcast_to(value[c : c + 1], (40, 512)), 0.0) for c in range(3)],
        axis=0,
    ).astype(BF16)
    k = iota((512, 128), 0) % 8
    to = iota((512, 128), 1)
    goal = jnp.where(gz == 0, (k + 126) % 128, (k + 123) % 128)
    first = jnp.where((k >= 1) & (k <= 5) & (to == goal), 1.0, 0.0).astype(BF16)
    spread = jnp.dot(lhs, first, preferred_element_type=F32)
    lane = iota((40, 128), 1)
    fixed = lane == jnp.where(gz == 0, 127, 0)
    for c in range(3):
        one = spread[40 * c : 40 * c + 40]
        out_ref[x, c] = jnp.where(fixed, one, out_ref[x, c])
        ext_ref[x, c] = jnp.where(fixed, 0.0, one)


def inner_kernel(where_ref, v_ref, w_ref, wp_ref, b_ref, hw_ref, hb_ref, hwp_ref, hbp_ref, out_ref, ext_ref):
    gz = where_ref[2]
    for x in range(2):
        refs = [v_ref.at[x + d] for d in range(3)]
        conv_slice(
            gz, refs, w_ref[...], wp_ref[...], b_ref[...], hw_ref[...], hb_ref[...], hwp_ref[...],
            hbp_ref[...], out_ref, ext_ref, x,
        )


def border_kernel(
    where_ref, v_ref, xe_ref, xo_ref, in_ref, in_ext_ref, ye_ref, yo_ref, zr_ref, m_ref, s_ref,
    w_ref, wp_ref, b_ref, hw_ref, hb_ref, hwp_ref, hbp_ref,
    aff_ref, e_ref, ext_ref, se_ref, so_ref,
    low_ref, high_ref, out_ref, oext_ref, mask_ref, mext_ref,
):
    odd_x = where_ref[0] % 2
    odd_y = where_ref[1] % 2
    gz = where_ref[2]

    @pl.when(odd_x == 0)
    def _():
        low_ref[...] = xo_ref[...]
        high_ref[...] = xe_ref[...]

    @pl.when(odd_x == 1)
    def _():
        low_ref[...] = xe_ref[...]
        high_ref[...] = xo_ref[...]

    for x, refs in (
        (0, [low_ref, v_ref.at[0], v_ref.at[1]]),
        (1, [v_ref.at[2], v_ref.at[3], high_ref]),
    ):
        conv_slice(
            gz, refs, w_ref[...], wp_ref[...], b_ref[...], hw_ref[...], hb_ref[...], hwp_ref[...],
            hbp_ref[...], out_ref, oext_ref, x,
        )

    zmask = zr_ref[256:288].astype(F32)
    for x in range(4):
        mask = m_ref[x].astype(F32)
        mask_ref[0, x, 0:32] = mask
        mask_ref[1, x, 0:32] = mask * s_ref[x].astype(F32)
        mext_ref[0, x, 0:32] = unpack_ext(zmask, x, gz)
        mext_ref[1, x, 0:32] = unpack_ext(zmask, 4 + x, gz)

    def fill(lower_ref, upper_ref):
        for x in range(4):
            lower = lower_ref[x, 192:208].astype(F32)
            upper = upper_ref[x, 192:208].astype(F32)
            for f in range(2):
                mask_ref[f, x, 32:36] = upper[4 * f : 4 * f + 4]
                mask_ref[f, x, 36:40] = lower[4 * f : 4 * f + 4]
                mext_ref[f, x, 32:36] = upper[8 + 4 * f : 12 + 4 * f]
                mext_ref[f, x, 36:40] = lower[8 + 4 * f : 12 + 4 * f]

    @pl.when(odd_y == 0)
    def _():
        fill(yo_ref, ye_ref)

    @pl.when(odd_y == 1)
    def _():
        fill(ye_ref, yo_ref)

    lane = iota((40, 128), 1)
    row = iota((40, 128), 0)

    def shift_y(value):
        return jnp.where(row == 36, 0.0, pltpu.roll(value, 1, 0))

    for x in range(4):
        main, ext = mask_ref[0, x], mext_ref[0, x]
        rolled, rolled_ext = pltpu.roll(main, 1, 1), pltpu.roll(ext, 1, 1)
        z_main = main * jnp.where(lane == 0, rolled_ext, rolled)
        z_ext = ext * jnp.where(lane == 0, rolled, rolled_ext)
        y_main, y_ext = main * shift_y(main), ext * shift_y(ext)
        x_main = main * mask_ref[0, x - 1] if x else main
        x_ext = ext * mext_ref[0, x - 1] if x else ext
        if 0 < x < 3:
            a = [in_ref[x - 1, c] for c in range(3)]
            aext = [in_ext_ref[x - 1, c] for c in range(3)]
        else:
            a = [out_ref[x // 3, c] for c in range(3)]
            aext = [oext_ref[x // 3, c] for c in range(3)]
        for c in range(3):
            aff_ref[c, x] = a[c][0:32].astype(BF16)
        slots = jnp.zeros((40, 128), F32)
        for f, (keep, keep_ext) in enumerate(((x_main, x_ext), (y_main, y_ext), (z_main, z_ext))):
            e_ref[x, f] = a[f] * keep
            ext_ref[x, f] = aext[f] * keep_ext
        e_ref[x, 3] = mask_ref[1, x]
        ext_ref[x, 3] = mext_ref[1, x]

    def send(dst_ref, order, last):
        packed = jnp.zeros((40, 128), F32)
        for j, x in enumerate(order):
            for f in range(4):
                value = ext_ref[x, f]
                slot = 4 * j + f
                packed = packed + (pltpu.roll(value, 8 * slot, 1) if slot else value)
                if j < 3:
                    dst_ref[slot] = e_ref[x, f].astype(BF16)
        dst_ref[12] = e_ref[order[3], 3].astype(BF16)
        dst_ref[13] = e_ref[order[3], 0].astype(BF16)
        dst_ref[14] = packed.astype(BF16)

    def send_up(dst_ref):
        send(dst_ref, (3, 2, 1, 0), None)

    def send_down(dst_ref):
        send(dst_ref, (0, 1, 2, 3), None)

    @pl.when(odd_x == 0)
    def _():
        send_up(se_ref)
        send_down(so_ref)

    @pl.when(odd_x == 1)
    def _():
        send_down(se_ref)
        send_up(so_ref)


def rounds_kernel(where_ref, e_ref, ext_ref, re_ref, ro_ref, m_ref, out_ref, all_ref, s_ref):
    odd_x = where_ref[0] % 2
    gz = where_ref[2]

    def place(src_ref, places, keep_last):
        packed = src_ref[14].astype(F32)
        for j, at in enumerate(places):
            for f in range(4):
                scale = (lambda v: v / 15.0) if f == 3 else (lambda v: v)
                ext = scale(unpack_ext(packed, 4 * j + f, gz))
                if j < 3:
                    main = scale(src_ref[4 * j + f].astype(F32))
                elif f == 3:
                    main = scale(src_ref[12].astype(F32))
                elif f == 0 and keep_last:
                    main = src_ref[13].astype(F32)
                else:
                    main, ext = jnp.zeros_like(packed), jnp.zeros_like(packed)
                if f == 3:
                    s_ref[0, at, 0] = main
                    s_ref[0, at, 1] = ext
                else:
                    all_ref[at, f, 0] = main
                    all_ref[at, f, 1] = ext

    @pl.when(odd_x == 0)
    def _():
        place(ro_ref, (3, 2, 1, 0), False)
        place(re_ref, (8, 9, 10, 11), True)

    @pl.when(odd_x == 1)
    def _():
        place(re_ref, (3, 2, 1, 0), False)
        place(ro_ref, (8, 9, 10, 11), True)

    for x in range(4):
        for f in range(3):
            all_ref[4 + x, f, 0] = e_ref[x, f]
            all_ref[4 + x, f, 1] = ext_ref[x, f]
        s_ref[0, 4 + x, 0] = e_ref[x, 3] / 15.0
        s_ref[0, 4 + x, 1] = ext_ref[x, 3] / 15.0

    lane = iota((40, 128), 1)

    def down(pair):
        a, b = pltpu.roll(pair[0], 1, 1), pltpu.roll(pair[1], 1, 1)
        return jnp.where(lane == 0, b, a), jnp.where(lane == 0, a, b)

    def up(pair):
        a, b = pltpu.roll(pair[0], 127, 1), pltpu.roll(pair[1], 127, 1)
        return jnp.where(lane == 127, b, a), jnp.where(lane == 127, a, b)

    for r in range(ROUNDS):
        src, dst = r % 2, (r + 1) % 2

        @pl.loop(r + 1, 11 - r)
        def _(x):
            here = (s_ref[src, x, 0], s_ref[src, x, 1])
            best = list(here)
            ez = (all_ref[x, 2, 0], all_ref[x, 2, 1])
            z_low = down(here)
            z_high = up(tuple(jnp.minimum(here[i], ez[i]) for i in range(2)))
            for i in range(2):
                ey = all_ref[x, 1, i]
                value = here[i]
                value = jnp.maximum(value, jnp.minimum(s_ref[src, x - 1, i], all_ref[x, 0, i]))
                value = jnp.maximum(value, jnp.minimum(s_ref[src, x + 1, i], all_ref[x + 1, 0, i]))
                value = jnp.maximum(value, jnp.minimum(pltpu.roll(here[i], 1, 0), ey))
                value = jnp.maximum(value, pltpu.roll(jnp.minimum(here[i], ey), 39, 0))
                value = jnp.maximum(value, jnp.minimum(z_low[i], ez[i]))
                value = jnp.maximum(value, z_high[i])
                s_ref[dst, x, i] = value

    for x in range(4):
        out_ref[x] = s_ref[ROUNDS % 2, 4 + x, 0, 0:32] * m_ref[x].astype(F32)


def call(kernel, shapes, args, scratch=(), aliases={}):
    return pl.pallas_call(
        kernel,
        out_shape=[jax.ShapeDtypeStruct(s, d) for s, d in shapes],
        in_specs=[SMEM] + [VMEM] * (len(args) - 1),
        out_specs=[VMEM] * len(shapes),
        scratch_shapes=[pltpu.VMEM(s, d) for s, d in scratch],
        input_output_aliases=aliases,
        compiler_params=PARAMS,
    )(*args)


def body(features, conv_weight, conv_bias, head_weight, head_bias, mask, seeds):
    where = jnp.stack([lax.axis_index(a) for a in ("gx", "gy", "gz")]).astype(jnp.int32)
    taps = jnp.transpose(conv_weight, (2, 3, 4, 0, 1))
    w = jnp.transpose(taps, (2, 3, 0, 1, 4)).reshape(96, 288)
    wp = jnp.transpose(taps, (1, 2, 3, 0, 4)).reshape(288, 96)
    bias = jnp.broadcast_to(conv_bias[:, None], (32, 128))
    eye = jnp.eye(8, dtype=BF16)
    hw = (head_weight[:, None, None, :] * eye[None, :, :, None]).reshape(24, 256)
    hb = jnp.broadcast_to(jnp.repeat(head_bias, 8)[:, None], (24, 128))
    hwp = jnp.zeros((8, 32), BF16).at[0:3].set(head_weight)
    hbp = jnp.zeros((8, 512), F32).at[0:3].set(jnp.broadcast_to(head_bias[:, None], (3, 512)))
    weights = (w, wp, bias, hw, hb, hwp, hbp)

    v, zs = call(
        pack_kernel, [((4, 46, 32, 128), BF16), ((288, 128), BF16)], (where, features, mask, seeds)
    )
    zr = lax.ppermute(zs, "gz", [(0, 1), (1, 0)])
    pt, ye, yo = call(
        yface_kernel,
        [((4, 2, 32, 128), BF16), ((4, 208, 128), BF16), ((4, 208, 128), BF16)],
        (where, v, zs, zr, mask, seeds),
        scratch=[((2, 4, 16, 128), F32)],
    )
    even, odd = swaps("gy")
    yo = lax.ppermute(yo, "gy", odd)
    ye = lax.ppermute(ye, "gy", even)
    v, xe, xo = call(
        xface_kernel,
        [((4, 46, 32, 128), BF16), ((46, 32, 128), BF16), ((46, 32, 128), BF16)],
        (where, v, pt, ye, yo),
        aliases={1: 0},
    )
    even, odd = swaps("gx")
    xo = lax.ppermute(xo, "gx", odd)
    xe = lax.ppermute(xe, "gx", even)
    inner, inner_ext = call(
        inner_kernel, [((2, 3, 40, 128), F32), ((2, 3, 40, 128), F32)], (where, v) + weights
    )
    affinity, e, ext, se, so = call(
        border_kernel,
        [
            ((3, 4, 32, 128), BF16),
            ((4, 4, 40, 128), F32),
            ((4, 4, 40, 128), F32),
            ((15, 40, 128), BF16),
            ((15, 40, 128), BF16),
        ],
        (where, v, xe, xo, inner, inner_ext, ye, yo, zr, mask, seeds) + weights,
        scratch=[
            ((46, 32, 128), BF16),
            ((46, 32, 128), BF16),
            ((2, 3, 40, 128), F32),
            ((2, 3, 40, 128), F32),
            ((2, 4, 40, 128), F32),
            ((2, 4, 40, 128), F32),
        ],
    )
    so = lax.ppermute(so, "gx", odd)
    se = lax.ppermute(se, "gx", even)
    (strength,) = call(
        rounds_kernel,
        [((4, 32, 128), F32)],
        (where, e, ext, se, so, mask),
        scratch=[((12, 3, 2, 40, 128), F32), ((2, 12, 2, 40, 128), F32)],
    )
    return (affinity, strength)


def solution(mesh):
    in_specs = (
        P(None, "gx", "gy", "gz"),
        P(),
        P(),
        P(),
        P(),
        P("gx", "gy", "gz"),
        P("gx", "gy", "gz"),
    )
    out_specs = (P(None, "gx", "gy", "gz"), P("gx", "gy", "gz"))
    return jax.shard_map(body, mesh=mesh, in_specs=in_specs, out_specs=out_specs, check_vma=False)
```

```python
import jax
import jax.numpy as jnp
from jax import lax
from jax.experimental import pallas as pl
from jax.experimental.pallas import tpu as pltpu
from jax.sharding import PartitionSpec as P

ROUNDS = 4
F32 = jnp.float32
BF16 = jnp.bfloat16
VMEM = pl.BlockSpec(memory_space=pltpu.VMEM)
SMEM = pl.BlockSpec(memory_space=pltpu.SMEM)
HBM = pl.BlockSpec(memory_space=pltpu.HBM)
PARAMS = pltpu.CompilerParams(vmem_limit_bytes=12 * 2**20)


def swaps(axis):
    count = lax.axis_size(axis)

    def pairs(first):
        return [
            p
            for i in range(first, count + first, 2)
            for p in ((i % count, (i + 1) % count), ((i + 1) % count, i % count))
        ]

    return pairs(0), pairs(1)


def iota(shape, dim):
    return lax.broadcasted_iota(jnp.int32, shape, dim)


def pack_kernel(where_ref, x_hbm, m_hbm, s_hbm, v_ref, zs_ref, ms_ref, x_ref, m_ref, s_ref, sems):
    gz = where_ref[2]
    copies = [pltpu.make_async_copy(x_hbm.at[:, x], x_ref.at[x], sems.at[x]) for x in range(4)]
    copies += [
        pltpu.make_async_copy(m_hbm, m_ref, sems.at[4]),
        pltpu.make_async_copy(s_hbm, s_ref, sems.at[5]),
    ]
    for copy in copies:
        copy.start()
    lane = iota((128, 128), 1)
    row = iota((128, 128), 0)
    base = jnp.where(gz == 0, 120, 0)
    hit = row == base + lane % 8
    sels = [jnp.where(hit & (lane // 8 == y), 1.0, 0.0).astype(BF16) for y in range(16)]
    for x in range(4):
        copies[x].wait()
        v_ref[x, 5:37] = jnp.swapaxes(x_ref[x], 0, 1)
    acc = jnp.zeros((256, 128), F32)
    for y in range(16):
        lhs = jnp.concatenate(
            [v_ref[x, 5 + 16 * half + y] for x in range(4) for half in range(2)], axis=0
        )
        acc = acc + jnp.dot(lhs, sels[y], preferred_element_type=F32)
    zs_ref[0:256] = acc.astype(BF16)
    copies[4].wait()
    copies[5].wait()
    lane = iota((32, 128), 1)
    edge = (lane >= jnp.where(gz == 0, 124, 0)) & (lane < jnp.where(gz == 0, 128, 4))
    packed = jnp.zeros((32, 128), F32)
    for x in range(4):
        mask = m_ref[x].astype(F32)
        seed = mask * s_ref[x].astype(F32)
        ms_ref[0, x] = mask
        ms_ref[1, x] = seed
        for slot, value in ((x, mask), (4 + x, seed)):
            value = jnp.where(edge, value, 0.0)
            packed = packed + (pltpu.roll(value, 8 * slot, 1) if slot else value)
    zs_ref[256:288] = packed.astype(BF16)


def weights_kernel(
    t_hbm, b_hbm, h_hbm, hb_hbm, w_ref, wp_ref, bias_ref, hw_ref, hbias_ref, hwp_ref, hbp_ref,
    t_ref, b_ref, h_ref, hb_ref, sems,
):
    copies = [
        pltpu.make_async_copy(src, dst, sems.at[i])
        for i, (src, dst) in enumerate(
            ((t_hbm, t_ref), (b_hbm, b_ref), (h_hbm, h_ref), (hb_hbm, hb_ref))
        )
    ]
    for copy in copies:
        copy.start()
    for copy in copies:
        copy.wait()
    for dz in range(3):
        w_ref[32 * dz : 32 * dz + 32] = jnp.concatenate(
            [t_ref[3 * k + dz] for k in range(9)], axis=1
        )
    for k in range(9):
        wp_ref[32 * k : 32 * k + 32] = jnp.concatenate(
            [t_ref[9 * dx + k] for dx in range(3)], axis=1
        )
    across = jnp.broadcast_to(b_ref[...], (32, 32))
    diagonal = iota((32, 32), 0) == iota((32, 32), 1)
    column = jnp.sum(jnp.where(diagonal, across, 0.0), axis=1, keepdims=True)
    bias_ref[...] = jnp.broadcast_to(column, (32, 128))
    same = iota((8, 256), 0) == iota((8, 256), 1) // 32
    few = iota((8, 128), 0)
    hwp = jnp.zeros((8, 32), F32)
    hbp = jnp.zeros((8, 128), F32)
    heads = h_ref[...].astype(F32)
    for c in range(3):
        line = jnp.concatenate([heads[c : c + 1]] * 8, axis=1)
        hw_ref[8 * c : 8 * c + 8] = jnp.where(same, jnp.broadcast_to(line, (8, 256)), 0.0)
        hbias_ref[8 * c : 8 * c + 8] = jnp.full((8, 128), hb_ref[c], F32)
        hwp = jnp.where(few[:, 0:32] == c, jnp.broadcast_to(heads[c : c + 1], (8, 32)), hwp)
        hbp = jnp.where(few == c, hb_ref[c], hbp)
    hwp_ref[...] = hwp
    hbp_ref[...] = hbp


def unpack_ext(packed, slot, gz):
    lane = iota(packed.shape, 1)
    inside = (lane >= jnp.where(gz == 0, 0, 124)) & (lane < jnp.where(gz == 0, 4, 128))
    value = pltpu.roll(packed, (128 - 8 * slot) % 128, 1) if slot else packed
    return jnp.where(inside, value, 0.0)


def yface_kernel(where_ref, v_ref, zs_ref, zr_ref, ms_ref, pt_ref, ye_ref, yo_ref, block_ref):
    odd = where_ref[1] % 2
    gz = where_ref[2]
    lane = iota((256, 128), 1) % 8
    own = pltpu.roll(zs_ref[0:256].astype(F32), jnp.where(gz == 0, 122, 5), 1)
    other = pltpu.roll(zr_ref[0:256].astype(F32), jnp.where(gz == 0, 2, 125), 1)
    own_from = jnp.where(gz == 0, 0, 5)
    other_from = jnp.where(gz == 0, 2, 0)
    packed = jnp.where((lane >= own_from) & (lane < own_from + 2), own, 0.0)
    packed = jnp.where((lane >= other_from) & (lane < other_from + 5), other, packed)
    packed = packed.astype(BF16).reshape(4, 2, 32, 128)
    pt_ref[...] = packed
    zmask = zr_ref[256:288].astype(F32)
    for x in range(4):
        fields = (ms_ref[0, x], ms_ref[1, x], unpack_ext(zmask, x, gz), unpack_ext(zmask, 4 + x, gz))
        for f, value in enumerate(fields):
            block_ref[0, x, 4 * f : 4 * f + 4] = value[28:32]
            block_ref[1, x, 4 * f : 4 * f + 4] = value[0:4]

    def write(dst_ref, up):
        for x in range(4):
            first = 32 if up else 5
            for j in range(5):
                dst_ref[x, 32 * j : 32 * j + 32] = v_ref[x, first + j]
            dst_ref[x, 160:192] = pt_ref[x, 1 if up else 0]
            dst_ref[x, 192:208] = block_ref[0 if up else 1, x].astype(BF16)

    @pl.when(odd == 0)
    def _():
        write(ye_ref, True)
        write(yo_ref, False)

    @pl.when(odd == 1)
    def _():
        write(ye_ref, False)
        write(yo_ref, True)


def xface_kernel(where_ref, v_in_ref, pt_ref, ye_ref, yo_ref, v_ref, xe_ref, xo_ref):
    odd_x = where_ref[0] % 2
    odd_y = where_ref[1] % 2

    gy = where_ref[1]
    for x in range(4):
        v_ref[x, 5:37] = v_in_ref[x, 5:37]

    def fill(low_ref, high_ref):
        for x in range(4):
            for j in range(5):
                v_ref[x, j] = low_ref[x, 32 * j : 32 * j + 32]
                v_ref[x, 37 + j] = high_ref[x, 32 * j : 32 * j + 32]
            v_ref[x, 42] = low_ref[x, 160:192]
            v_ref[x, 43] = pt_ref[x, 0]
            v_ref[x, 44] = pt_ref[x, 1]
            v_ref[x, 45] = high_ref[x, 160:192]

    @pl.when(odd_y == 0)
    def _():
        fill(yo_ref, ye_ref)

    @pl.when(odd_y == 1)
    def _():
        fill(ye_ref, yo_ref)

    zero = jnp.zeros((32, 128), BF16)

    @pl.when(gy == 0)
    def _():
        for x in range(4):
            for tile in (0, 1, 2, 3, 4, 42):
                v_ref[x, tile] = zero

    @pl.when(gy == 7)
    def _():
        for x in range(4):
            for tile in (37, 38, 39, 40, 41, 45):
                v_ref[x, tile] = zero

    even_face = jnp.where(odd_x == 0, 3, 0)
    xe_ref[...] = v_ref[even_face]
    xo_ref[...] = v_ref[3 - even_face]


def head(hidden, head_ref, bias_ref):
    logits = jnp.dot(head_ref[...].astype(BF16), hidden, preferred_element_type=F32)
    logits = logits + jnp.tile(bias_ref[...], (1, logits.shape[1] // 128))
    return jax.nn.sigmoid(logits).astype(BF16).astype(F32)


def tile_of(row):
    return row + 5 if row < 36 else row - 35


def spread_matrix(gz):
    k = iota((512, 128), 0) % 8
    to = iota((512, 128), 1)
    goal = jnp.where(gz == 0, (k + 126) % 128, (k + 123) % 128)
    return jnp.where((k >= 1) & (k <= 5) & (to == goal), 1.0, 0.0).astype(BF16)


def conv_main(refs, weights, hid_ref, rows):
    lane = iota((32, 128), 1)
    first, last = lane == 0, lane == 127
    w, bias = weights[0][...], weights[2][...]
    for pair in zip(rows[0::2], rows[1::2]):
        cols = []
        for row in pair:
            t = tile_of(row)
            cols.append(
                jnp.concatenate([r[t - 1 : t + 2].reshape(96, 128) for r in refs], axis=0)
            )
        part = jnp.dot(w, jnp.concatenate(cols, axis=1), preferred_element_type=F32)
        for i, row in enumerate(pair):
            one = part[:, 128 * i : 128 * i + 128]
            left = jnp.where(first, 0.0, pltpu.roll(one[0:32], 1, 1))
            right = jnp.where(last, 0.0, pltpu.roll(one[64:96], 127, 1))
            hid = jnp.maximum(one[32:64] + left + right + bias, 0.0)
            hid_ref[32 * row : 32 * row + 32] = hid.astype(BF16)


def conv_packed(refs, weights, spread):
    _, wp_ref, b_ref, _, _, hwp_ref, hbp_ref = weights
    cols = [jnp.concatenate([r[42 + q] for r in refs], axis=0) for q in range(4)]
    part = jnp.dot(wp_ref[...], jnp.concatenate(cols, axis=1), preferred_element_type=F32)
    total = jnp.tile(b_ref[...], (1, 4))
    for dy in range(3):
        for dz in range(3):
            k = 3 * dy + dz
            shift = (-(8 * (dy - 1) + dz - 1)) % 512
            one = part[32 * k : 32 * k + 32]
            total = total + (pltpu.roll(one, shift, 1) if shift else one)
    value = head(jnp.maximum(total, 0.0).astype(BF16), hwp_ref, hbp_ref)
    row = iota((40, 512), 0)
    at = iota((40, 512), 1)
    mine = at // 8 - 16 == jnp.where(row < 36, row, row - 40)
    lhs = jnp.concatenate(
        [jnp.where(mine, jnp.broadcast_to(value[c : c + 1], (40, 512)), 0.0) for c in range(3)],
        axis=0,
    ).astype(BF16)
    return jnp.dot(lhs, spread, preferred_element_type=F32)


def conv_slice(gz, refs, weights, spread, hid_ref):
    conv_main(refs, weights, hid_ref, range(40))
    border = conv_packed(refs, weights, spread)
    hidden = jnp.concatenate([hid_ref[256 * g : 256 * g + 256] for g in range(5)], axis=1)
    value = head(hidden, weights[3], weights[4])
    fixed = iota((40, 128), 1) == jnp.where(gz == 0, 127, 0)
    out = []
    for c in range(3):
        main = jnp.concatenate(
            [value[8 * c : 8 * c + 8, 128 * g : 128 * g + 128] for g in range(5)], axis=0
        )
        one = border[40 * c : 40 * c + 40]
        out.append((jnp.where(fixed, one, main), jnp.where(fixed, 0.0, one)))
    return out


def inner_kernel(
    where_ref, v_ref, ye_ref, yo_ref, zr_ref, ms_ref, w_ref, wp_ref, b_ref, hw_ref, hb_ref, hwp_ref, hbp_ref,
    a_ref, e_ref, ext_ref, hid_ref, mask_ref, mext_ref,
):
    gy = where_ref[1]
    odd_y = gy % 2
    gz = where_ref[2]
    zmask = zr_ref[256:288].astype(F32)
    for x in range(4):
        for f in range(2):
            mask_ref[f, x, 0:32] = ms_ref[f, x]
            mext_ref[f, x, 0:32] = unpack_ext(zmask, 4 * f + x, gz)

    def fill(lower_ref, upper_ref):
        has_lower = jnp.where(gy == 0, 0.0, 1.0)
        has_upper = jnp.where(gy == 7, 0.0, 1.0)
        for x in range(4):
            lower = lower_ref[x, 192:208].astype(F32) * has_lower
            upper = upper_ref[x, 192:208].astype(F32) * has_upper
            for f in range(2):
                mask_ref[f, x, 32:36] = upper[4 * f : 4 * f + 4]
                mask_ref[f, x, 36:40] = lower[4 * f : 4 * f + 4]
                mext_ref[f, x, 32:36] = upper[8 + 4 * f : 12 + 4 * f]
                mext_ref[f, x, 36:40] = lower[8 + 4 * f : 12 + 4 * f]

    @pl.when(odd_y == 0)
    def _():
        fill(yo_ref, ye_ref)

    @pl.when(odd_y == 1)
    def _():
        fill(ye_ref, yo_ref)

    lane = iota((40, 128), 1)
    row = iota((40, 128), 0)

    def shift_y(value):
        return jnp.where(row == 36, 0.0, pltpu.roll(value, 1, 0))

    weights = (w_ref, wp_ref, b_ref, hw_ref, hb_ref, hwp_ref, hbp_ref)
    spread = spread_matrix(gz)
    for x in range(4):
        main, ext = mask_ref[0, x], mext_ref[0, x]
        rolled, rolled_ext = pltpu.roll(main, 1, 1), pltpu.roll(ext, 1, 1)
        z_main = main * jnp.where(lane == 0, rolled_ext, rolled)
        z_ext = ext * jnp.where(lane == 0, rolled, rolled_ext)
        y_main, y_ext = main * shift_y(main), ext * shift_y(ext)
        x_main = main * mask_ref[0, x - 1] if x else main
        x_ext = ext * mext_ref[0, x - 1] if x else ext
        keep = ((x_main, x_ext), (y_main, y_ext), (z_main, z_ext))
        if 0 < x < 3:
            refs = [v_ref.at[x - 1 + d] for d in range(3)]
            a = conv_slice(gz, refs, weights, spread, hid_ref.at[x - 1])
            for f in range(3):
                a_ref[f, x] = a[f][0][0:32].astype(BF16)
                e_ref[x, f] = a[f][0] * keep[f][0]
                ext_ref[x, f] = a[f][1] * keep[f][1]
        else:
            for f in range(3):
                e_ref[x, f] = keep[f][0]
                ext_ref[x, f] = keep[f][1]
        e_ref[x, 3] = mask_ref[1, x]
        ext_ref[x, 3] = mext_ref[1, x]


def border_kernel(
    where_ref, v_ref, xe_ref, xo_ref, a_in, e_in, ext_in, w_ref, wp_ref, b_ref, hw_ref, hb_ref, hwp_ref, hbp_ref,
    a_ref, e_ref, ext_ref, se_ref, so_ref, low_ref, high_ref, hid_ref,
):
    gx = where_ref[0]
    odd_x = gx % 2
    gz = where_ref[2]

    @pl.when(odd_x == 0)
    def _():
        low_ref[...] = xo_ref[...]
        high_ref[...] = xe_ref[...]

    @pl.when(odd_x == 1)
    def _():
        low_ref[...] = xe_ref[...]
        high_ref[...] = xo_ref[...]

    @pl.when(gx == 0)
    def _():
        low_ref[...] = jnp.zeros_like(low_ref)

    @pl.when(gx == 15)
    def _():
        high_ref[...] = jnp.zeros_like(high_ref)

    for x in (1, 2):
        a_ref[:, x] = a_in[:, x]
        e_ref[x] = e_in[x]
        ext_ref[x] = ext_in[x]
    for x in (0, 3):
        e_ref[x, 3] = e_in[x, 3]
        ext_ref[x, 3] = ext_in[x, 3]

    weights = (w_ref, wp_ref, b_ref, hw_ref, hb_ref, hwp_ref, hbp_ref)
    spread = spread_matrix(gz)
    for x, refs in (
        (0, [low_ref, v_ref.at[0], v_ref.at[1]]),
        (3, [v_ref.at[2], v_ref.at[3], high_ref]),
    ):
        a = conv_slice(gz, refs, weights, spread, hid_ref.at[x // 3])
        for f in range(3):
            a_ref[f, x] = a[f][0][0:32].astype(BF16)
            e_ref[x, f] = a[f][0] * e_in[x, f]
            ext_ref[x, f] = a[f][1] * ext_in[x, f]

    def send(dst_ref, order):
        packed = jnp.zeros((40, 128), F32)
        for j, x in enumerate(order):
            for f in range(4):
                value = ext_ref[x, f]
                slot = 4 * j + f
                packed = packed + (pltpu.roll(value, 8 * slot, 1) if slot else value)
                if j < 3:
                    dst_ref[slot] = e_ref[x, f].astype(BF16)
        dst_ref[12] = e_ref[order[3], 3].astype(BF16)
        dst_ref[13] = e_ref[order[3], 0].astype(BF16)
        dst_ref[14] = packed.astype(BF16)

    @pl.when(odd_x == 0)
    def _():
        send(se_ref, (3, 2, 1, 0))
        send(so_ref, (0, 1, 2, 3))

    @pl.when(odd_x == 1)
    def _():
        send(se_ref, (0, 1, 2, 3))
        send(so_ref, (3, 2, 1, 0))


def rounds_kernel(where_ref, e_ref, ext_ref, re_ref, ro_ref, ms_ref, out_ref, all_ref, s_ref):
    gx = where_ref[0]
    odd_x = gx % 2
    has_low = jnp.where(gx == 0, 0.0, 1.0)
    has_high = jnp.where(gx == 15, 0.0, 1.0)
    gz = where_ref[2]

    def place(src_ref, places, keep_last):
        has = has_high if keep_last else has_low
        packed = src_ref[14].astype(F32) * has
        for j, at in enumerate(places):
            for f in range(4):
                scale = (lambda v: v / 15.0) if f == 3 else (lambda v: v)
                ext = scale(unpack_ext(packed, 4 * j + f, gz))
                if j < 3:
                    main = scale(src_ref[4 * j + f].astype(F32) * has)
                elif f == 3:
                    main = scale(src_ref[12].astype(F32) * has)
                elif f == 0 and keep_last:
                    main = src_ref[13].astype(F32) * has
                else:
                    main, ext = jnp.zeros_like(packed), jnp.zeros_like(packed)
                if f == 3:
                    s_ref[0, at, 0] = main
                    s_ref[0, at, 1] = ext
                else:
                    all_ref[at, f, 0] = main
                    all_ref[at, f, 1] = ext

    @pl.when(odd_x == 0)
    def _():
        place(ro_ref, (3, 2, 1, 0), False)
        place(re_ref, (8, 9, 10, 11), True)

    @pl.when(odd_x == 1)
    def _():
        place(re_ref, (3, 2, 1, 0), False)
        place(ro_ref, (8, 9, 10, 11), True)

    for x in range(4):
        for f in range(3):
            all_ref[4 + x, f, 0] = e_ref[x, f]
            all_ref[4 + x, f, 1] = ext_ref[x, f]
        s_ref[0, 4 + x, 0] = e_ref[x, 3] / 15.0
        s_ref[0, 4 + x, 1] = ext_ref[x, 3] / 15.0

    lane = iota((40, 128), 1)

    def down(pair):
        a, b = pltpu.roll(pair[0], 1, 1), pltpu.roll(pair[1], 1, 1)
        return jnp.where(lane == 0, b, a), jnp.where(lane == 0, a, b)

    def up(pair):
        a, b = pltpu.roll(pair[0], 127, 1), pltpu.roll(pair[1], 127, 1)
        return jnp.where(lane == 127, b, a), jnp.where(lane == 127, a, b)

    for r in range(ROUNDS):
        src, dst = r % 2, (r + 1) % 2

        for x in range(r + 1, 11 - r):
            here = (s_ref[src, x, 0], s_ref[src, x, 1])
            best = list(here)
            ez = (all_ref[x, 2, 0], all_ref[x, 2, 1])
            z_low = down(here)
            z_high = up(tuple(jnp.minimum(here[i], ez[i]) for i in range(2)))
            for i in range(2):
                ey = all_ref[x, 1, i]
                value = here[i]
                value = jnp.maximum(value, jnp.minimum(s_ref[src, x - 1, i], all_ref[x, 0, i]))
                value = jnp.maximum(value, jnp.minimum(s_ref[src, x + 1, i], all_ref[x + 1, 0, i]))
                value = jnp.maximum(value, jnp.minimum(pltpu.roll(here[i], 1, 0), ey))
                value = jnp.maximum(value, pltpu.roll(jnp.minimum(here[i], ey), 39, 0))
                value = jnp.maximum(value, jnp.minimum(z_low[i], ez[i]))
                value = jnp.maximum(value, z_high[i])
                s_ref[dst, x, i] = value

    for x in range(4):
        out_ref[x] = s_ref[ROUNDS % 2, 4 + x, 0, 0:32] * ms_ref[0, x]


def stay(value):
    return pltpu.with_memory_space_constraint(value, pltpu.HBM)


def call(kernel, shapes, args, scratch=(), aliases={}, specs=None):
    return pl.pallas_call(
        kernel,
        out_shape=[jax.ShapeDtypeStruct(s, d) for s, d in shapes],
        in_specs=specs or [SMEM] + [VMEM] * (len(args) - 1),
        out_specs=[VMEM] * len(shapes),
        scratch_shapes=[pltpu.VMEM(*s) if isinstance(s[0], tuple) else s[0](*s[1:]) for s in scratch],
        input_output_aliases=aliases,
        compiler_params=PARAMS,
    )(*args)


def body(features, conv_weight, conv_bias, head_weight, head_bias, mask, seeds):
    where = jnp.stack([lax.axis_index(a) for a in ("gx", "gy", "gz")]).astype(jnp.int32)

    v, zs, ms = call(
        pack_kernel,
        [((4, 46, 32, 128), BF16), ((288, 128), BF16), ((2, 4, 32, 128), F32)],
        (where, *(stay(a) for a in (features, mask, seeds))),
        scratch=[
            ((4, 32, 32, 128), BF16),
            ((4, 32, 128), jnp.int32),
            ((4, 32, 128), jnp.int32),
            (pltpu.SemaphoreType.DMA, (6,)),
        ],
        specs=[SMEM, HBM, HBM, HBM],
    )
    zs, conv_weight, conv_bias, head_weight, head_bias = lax.optimization_barrier(
        (zs, conv_weight, conv_bias, head_weight, head_bias)
    )
    zr = lax.ppermute(zs, "gz", [(0, 1), (1, 0)])
    taps = jnp.transpose(conv_weight, (2, 3, 4, 0, 1)).reshape(27, 32, 32)
    forms = call(
        weights_kernel,
        [
            ((96, 288), BF16),
            ((288, 96), BF16),
            ((32, 128), F32),
            ((24, 256), F32),
            ((24, 128), F32),
            ((8, 32), F32),
            ((8, 128), F32),
        ],
        tuple(stay(a) for a in (taps, conv_bias.reshape(1, 32), head_weight, head_bias)),
        scratch=[
            ((27, 32, 32), BF16),
            ((1, 32), F32),
            ((3, 32), BF16),
            (pltpu.SMEM, (3,), F32),
            (pltpu.SemaphoreType.DMA, (4,)),
        ],
        specs=[HBM] * 4,
    )
    zr, *weights = lax.optimization_barrier((zr, *forms))
    weights = tuple(weights)
    pt, ye, yo = call(
        yface_kernel,
        [((4, 2, 32, 128), BF16), ((4, 208, 128), BF16), ((4, 208, 128), BF16)],
        (where, v, zs, zr, ms),
        scratch=[((2, 4, 16, 128), F32)],
    )
    even, odd = swaps("gy")
    yo = lax.ppermute(yo, "gy", odd)
    ye = lax.ppermute(ye, "gy", even)
    v, xe, xo = call(
        xface_kernel,
        [((4, 46, 32, 128), BF16), ((46, 32, 128), BF16), ((46, 32, 128), BF16)],
        (where, v, pt, ye, yo),
    )
    even, odd = swaps("gx")
    xo = lax.ppermute(xo, "gx", odd)
    xe = lax.ppermute(xe, "gx", even)
    affinity, e, ext = call(
        inner_kernel,
        [((3, 4, 32, 128), BF16), ((4, 4, 40, 128), F32), ((4, 4, 40, 128), F32)],
        (where, v, ye, yo, zr, ms) + weights,
        scratch=[((2, 1280, 128), BF16), ((2, 4, 40, 128), F32), ((2, 4, 40, 128), F32)],
    )
    affinity, e, ext, se, so = call(
        border_kernel,
        [
            ((3, 4, 32, 128), BF16),
            ((4, 4, 40, 128), F32),
            ((4, 4, 40, 128), F32),
            ((15, 40, 128), BF16),
            ((15, 40, 128), BF16),
        ],
        (where, v, xe, xo, affinity, e, ext) + weights,
        scratch=[((46, 32, 128), BF16), ((46, 32, 128), BF16), ((2, 1280, 128), BF16)],
    )
    so = lax.ppermute(so, "gx", odd)
    se = lax.ppermute(se, "gx", even)
    (strength,) = call(
        rounds_kernel,
        [((4, 32, 128), F32)],
        (where, e, ext, se, so, ms),
        scratch=[((12, 3, 2, 40, 128), F32), ((2, 12, 2, 40, 128), F32)],
    )
    return (affinity, strength)


def solution(mesh):
    in_specs = (
        P(None, "gx", "gy", "gz"),
        P(),
        P(),
        P(),
        P(),
        P("gx", "gy", "gz"),
        P("gx", "gy", "gz"),
    )
    out_specs = (P(None, "gx", "gy", "gz"), P("gx", "gy", "gz"))
    return jax.shard_map(body, mesh=mesh, in_specs=in_specs, out_specs=out_specs, check_vma=False)
```

```python
import jax
import jax.numpy as jnp
from jax import lax
from jax.experimental import pallas as pl
from jax.experimental.pallas import tpu as pltpu
from jax.sharding import PartitionSpec as P

ROUNDS = 4
F32 = jnp.float32
BF16 = jnp.bfloat16
VMEM = pl.BlockSpec(memory_space=pltpu.VMEM)
HBM = pl.BlockSpec(memory_space=pltpu.HBM)
PARAMS = pltpu.CompilerParams(vmem_limit_bytes=12 * 2**20)


def swaps(axis):
    count = lax.axis_size(axis)

    def pairs(first):
        return [
            p
            for i in range(first, count + first, 2)
            for p in ((i % count, (i + 1) % count), ((i + 1) % count, i % count))
        ]

    return pairs(0), pairs(1)


def iota(shape, dim):
    return lax.broadcasted_iota(jnp.int32, shape, dim)


def pack_kernel(x_hbm, m_hbm, s_hbm, v_ref, zs_ref, ms_ref, x_ref, m_ref, s_ref, sems):
    gz = lax.axis_index("gz")
    copies = [pltpu.make_async_copy(x_hbm.at[:, x], x_ref.at[x], sems.at[x]) for x in range(4)]
    copies += [
        pltpu.make_async_copy(m_hbm, m_ref, sems.at[4]),
        pltpu.make_async_copy(s_hbm, s_ref, sems.at[5]),
    ]
    for copy in copies:
        copy.start()
    lane = iota((128, 128), 1)
    row = iota((128, 128), 0)
    base = jnp.where(gz == 0, 120, 0)
    hit = row == base + lane % 8
    sels = [jnp.where(hit & (lane // 8 == y), 1.0, 0.0).astype(BF16) for y in range(16)]
    for x in range(4):
        copies[x].wait()
        v_ref[x, 5:37] = jnp.swapaxes(x_ref[x], 0, 1)
    acc = jnp.zeros((256, 128), F32)
    for y in range(16):
        lhs = jnp.concatenate(
            [v_ref[x, 5 + 16 * half + y] for x in range(4) for half in range(2)], axis=0
        )
        acc = acc + jnp.dot(lhs, sels[y], preferred_element_type=F32)
    zs_ref[0:256] = acc.astype(BF16)
    copies[4].wait()
    copies[5].wait()
    lane = iota((32, 128), 1)
    edge = (lane >= jnp.where(gz == 0, 124, 0)) & (lane < jnp.where(gz == 0, 128, 4))
    packed = jnp.zeros((32, 128), F32)
    for x in range(4):
        mask = m_ref[x].astype(F32)
        seed = mask * s_ref[x].astype(F32)
        ms_ref[0, x] = mask
        ms_ref[1, x] = seed
        for slot, value in ((x, mask), (4 + x, seed)):
            value = jnp.where(edge, value, 0.0)
            packed = packed + (pltpu.roll(value, 8 * slot, 1) if slot else value)
    zs_ref[256:288] = packed.astype(BF16)


def weights_kernel(
    t_hbm, b_hbm, h_hbm, hb_hbm, w_ref, wp_ref, bias_ref, hw_ref, hbias_ref, hwp_ref, hbp_ref,
    t_ref, b_ref, h_ref, hb_ref, sems,
):
    copies = [
        pltpu.make_async_copy(src, dst, sems.at[i])
        for i, (src, dst) in enumerate(
            ((t_hbm, t_ref), (b_hbm, b_ref), (h_hbm, h_ref), (hb_hbm, hb_ref))
        )
    ]
    for copy in copies:
        copy.start()
    for copy in copies:
        copy.wait()
    for dz in range(3):
        w_ref[32 * dz : 32 * dz + 32] = jnp.concatenate(
            [t_ref[3 * k + dz] for k in range(9)], axis=1
        )
    for k in range(9):
        wp_ref[32 * k : 32 * k + 32] = jnp.concatenate(
            [t_ref[9 * dx + k] for dx in range(3)], axis=1
        )
    across = jnp.broadcast_to(b_ref[...], (32, 32))
    diagonal = iota((32, 32), 0) == iota((32, 32), 1)
    column = jnp.sum(jnp.where(diagonal, across, 0.0), axis=1, keepdims=True)
    bias_ref[...] = jnp.broadcast_to(column, (32, 128))
    same = iota((8, 256), 0) == iota((8, 256), 1) // 32
    few = iota((8, 128), 0)
    hwp = jnp.zeros((8, 32), F32)
    hbp = jnp.zeros((8, 128), F32)
    heads = h_ref[...].astype(F32)
    for c in range(3):
        line = jnp.concatenate([heads[c : c + 1]] * 8, axis=1)
        hw_ref[8 * c : 8 * c + 8] = jnp.where(same, jnp.broadcast_to(line, (8, 256)), 0.0)
        hbias_ref[8 * c : 8 * c + 8] = jnp.full((8, 128), hb_ref[c], F32)
        hwp = jnp.where(few[:, 0:32] == c, jnp.broadcast_to(heads[c : c + 1], (8, 32)), hwp)
        hbp = jnp.where(few == c, hb_ref[c], hbp)
    hwp_ref[...] = hwp
    hbp_ref[...] = hbp


def unpack_ext(packed, slot, gz):
    lane = iota(packed.shape, 1)
    inside = (lane >= jnp.where(gz == 0, 0, 124)) & (lane < jnp.where(gz == 0, 4, 128))
    value = pltpu.roll(packed, (128 - 8 * slot) % 128, 1) if slot else packed
    return jnp.where(inside, value, 0.0)


def yface_kernel(v_ref, zs_ref, zr_ref, ms_ref, pt_ref, ye_ref, yo_ref, block_ref):
    odd = lax.axis_index("gy") % 2
    gz = lax.axis_index("gz")
    lane = iota((256, 128), 1) % 8
    own = pltpu.roll(zs_ref[0:256].astype(F32), jnp.where(gz == 0, 122, 5), 1)
    other = pltpu.roll(zr_ref[0:256].astype(F32), jnp.where(gz == 0, 2, 125), 1)
    own_from = jnp.where(gz == 0, 0, 5)
    other_from = jnp.where(gz == 0, 2, 0)
    packed = jnp.where((lane >= own_from) & (lane < own_from + 2), own, 0.0)
    packed = jnp.where((lane >= other_from) & (lane < other_from + 5), other, packed)
    packed = packed.astype(BF16).reshape(4, 2, 32, 128)
    pt_ref[...] = packed
    zmask = zr_ref[256:288].astype(F32)
    for x in range(4):
        fields = (ms_ref[0, x], ms_ref[1, x], unpack_ext(zmask, x, gz), unpack_ext(zmask, 4 + x, gz))
        for f, value in enumerate(fields):
            block_ref[0, x, 4 * f : 4 * f + 4] = value[28:32]
            block_ref[1, x, 4 * f : 4 * f + 4] = value[0:4]

    def write(dst_ref, up):
        for x in range(4):
            first = 32 if up else 5
            for j in range(5):
                dst_ref[x, 32 * j : 32 * j + 32] = v_ref[x, first + j]
            dst_ref[x, 160:192] = pt_ref[x, 1 if up else 0]
            dst_ref[x, 192:208] = block_ref[0 if up else 1, x].astype(BF16)

    @pl.when(odd == 0)
    def _():
        write(ye_ref, True)
        write(yo_ref, False)

    @pl.when(odd == 1)
    def _():
        write(ye_ref, False)
        write(yo_ref, True)


def xface_kernel(v_in_ref, pt_ref, ye_ref, yo_ref, v_ref, xe_ref, xo_ref):
    odd_x = lax.axis_index("gx") % 2
    odd_y = lax.axis_index("gy") % 2

    gy = lax.axis_index("gy")
    for x in range(4):
        v_ref[x, 5:37] = v_in_ref[x, 5:37]

    def fill(low_ref, high_ref):
        for x in range(4):
            for j in range(5):
                v_ref[x, j] = low_ref[x, 32 * j : 32 * j + 32]
                v_ref[x, 37 + j] = high_ref[x, 32 * j : 32 * j + 32]
            v_ref[x, 42] = low_ref[x, 160:192]
            v_ref[x, 43] = pt_ref[x, 0]
            v_ref[x, 44] = pt_ref[x, 1]
            v_ref[x, 45] = high_ref[x, 160:192]

    @pl.when(odd_y == 0)
    def _():
        fill(yo_ref, ye_ref)

    @pl.when(odd_y == 1)
    def _():
        fill(ye_ref, yo_ref)

    zero = jnp.zeros((32, 128), BF16)

    @pl.when(gy == 0)
    def _():
        for x in range(4):
            for tile in (0, 1, 2, 3, 4, 42):
                v_ref[x, tile] = zero

    @pl.when(gy == 7)
    def _():
        for x in range(4):
            for tile in (37, 38, 39, 40, 41, 45):
                v_ref[x, tile] = zero

    even_face = jnp.where(odd_x == 0, 3, 0)
    xe_ref[...] = v_ref[even_face]
    xo_ref[...] = v_ref[3 - even_face]


def head(hidden, head_ref, bias_ref):
    logits = jnp.dot(head_ref[...].astype(BF16), hidden, preferred_element_type=F32)
    logits = logits + jnp.tile(bias_ref[...], (1, logits.shape[1] // 128))
    return jax.nn.sigmoid(logits).astype(BF16).astype(F32)


def tile_of(row):
    return row + 5 if row < 36 else row - 35


def spread_matrix(gz):
    k = iota((512, 128), 0) % 8
    to = iota((512, 128), 1)
    goal = jnp.where(gz == 0, (k + 126) % 128, (k + 123) % 128)
    return jnp.where((k >= 1) & (k <= 5) & (to == goal), 1.0, 0.0).astype(BF16)


def conv_main(refs, weights, hid_ref, rows):
    lane = iota((32, 128), 1)
    first, last = lane == 0, lane == 127
    w, bias = weights[0][...], weights[2][...]
    for pair in zip(rows[0::2], rows[1::2]):
        cols = []
        for row in pair:
            t = tile_of(row)
            cols.append(
                jnp.concatenate([r[t - 1 : t + 2].reshape(96, 128) for r in refs], axis=0)
            )
        part = jnp.dot(w, jnp.concatenate(cols, axis=1), preferred_element_type=F32)
        for i, row in enumerate(pair):
            one = part[:, 128 * i : 128 * i + 128]
            left = jnp.where(first, 0.0, pltpu.roll(one[0:32], 1, 1))
            right = jnp.where(last, 0.0, pltpu.roll(one[64:96], 127, 1))
            hid = jnp.maximum(one[32:64] + left + right + bias, 0.0)
            hid_ref[32 * row : 32 * row + 32] = hid.astype(BF16)


def conv_packed(refs, weights, spread):
    _, wp_ref, b_ref, _, _, hwp_ref, hbp_ref = weights
    cols = [jnp.concatenate([r[42 + q] for r in refs], axis=0) for q in range(4)]
    part = jnp.dot(wp_ref[...], jnp.concatenate(cols, axis=1), preferred_element_type=F32)
    total = jnp.tile(b_ref[...], (1, 4))
    for dy in range(3):
        for dz in range(3):
            k = 3 * dy + dz
            shift = (-(8 * (dy - 1) + dz - 1)) % 512
            one = part[32 * k : 32 * k + 32]
            total = total + (pltpu.roll(one, shift, 1) if shift else one)
    value = head(jnp.maximum(total, 0.0).astype(BF16), hwp_ref, hbp_ref)
    row = iota((40, 512), 0)
    at = iota((40, 512), 1)
    mine = at // 8 - 16 == jnp.where(row < 36, row, row - 40)
    lhs = jnp.concatenate(
        [jnp.where(mine, jnp.broadcast_to(value[c : c + 1], (40, 512)), 0.0) for c in range(3)],
        axis=0,
    ).astype(BF16)
    return jnp.dot(lhs, spread, preferred_element_type=F32)


def conv_slice(gz, refs, weights, spread, hid_ref):
    conv_main(refs, weights, hid_ref, range(40))
    border = conv_packed(refs, weights, spread)
    hidden = jnp.concatenate([hid_ref[256 * g : 256 * g + 256] for g in range(5)], axis=1)
    value = head(hidden, weights[3], weights[4])
    fixed = iota((40, 128), 1) == jnp.where(gz == 0, 127, 0)
    out = []
    for c in range(3):
        main = jnp.concatenate(
            [value[8 * c : 8 * c + 8, 128 * g : 128 * g + 128] for g in range(5)], axis=0
        )
        one = border[40 * c : 40 * c + 40]
        out.append((jnp.where(fixed, one, main), jnp.where(fixed, 0.0, one)))
    return out


def inner_kernel(
    v_ref, ye_ref, yo_ref, zr_ref, ms_ref, w_ref, wp_ref, b_ref, hw_ref, hb_ref, hwp_ref, hbp_ref,
    a_ref, e_ref, ext_ref, hid_ref, mask_ref, mext_ref,
):
    gy = lax.axis_index("gy")
    odd_y = gy % 2
    gz = lax.axis_index("gz")
    zmask = zr_ref[256:288].astype(F32)
    for x in range(4):
        for f in range(2):
            mask_ref[f, x, 0:32] = ms_ref[f, x]
            mext_ref[f, x, 0:32] = unpack_ext(zmask, 4 * f + x, gz)

    def fill(lower_ref, upper_ref):
        has_lower = jnp.where(gy == 0, 0.0, 1.0)
        has_upper = jnp.where(gy == 7, 0.0, 1.0)
        for x in range(4):
            lower = lower_ref[x, 192:208].astype(F32) * has_lower
            upper = upper_ref[x, 192:208].astype(F32) * has_upper
            for f in range(2):
                mask_ref[f, x, 32:36] = upper[4 * f : 4 * f + 4]
                mask_ref[f, x, 36:40] = lower[4 * f : 4 * f + 4]
                mext_ref[f, x, 32:36] = upper[8 + 4 * f : 12 + 4 * f]
                mext_ref[f, x, 36:40] = lower[8 + 4 * f : 12 + 4 * f]

    @pl.when(odd_y == 0)
    def _():
        fill(yo_ref, ye_ref)

    @pl.when(odd_y == 1)
    def _():
        fill(ye_ref, yo_ref)

    lane = iota((40, 128), 1)
    row = iota((40, 128), 0)

    def shift_y(value):
        return jnp.where(row == 36, 0.0, pltpu.roll(value, 1, 0))

    weights = (w_ref, wp_ref, b_ref, hw_ref, hb_ref, hwp_ref, hbp_ref)
    spread = spread_matrix(gz)
    for x in range(4):
        main, ext = mask_ref[0, x], mext_ref[0, x]
        rolled, rolled_ext = pltpu.roll(main, 1, 1), pltpu.roll(ext, 1, 1)
        z_main = main * jnp.where(lane == 0, rolled_ext, rolled)
        z_ext = ext * jnp.where(lane == 0, rolled, rolled_ext)
        y_main, y_ext = main * shift_y(main), ext * shift_y(ext)
        x_main = main * mask_ref[0, x - 1] if x else main
        x_ext = ext * mext_ref[0, x - 1] if x else ext
        keep = ((x_main, x_ext), (y_main, y_ext), (z_main, z_ext))
        if 0 < x < 3:
            refs = [v_ref.at[x - 1 + d] for d in range(3)]
            a = conv_slice(gz, refs, weights, spread, hid_ref.at[x - 1])
            for f in range(3):
                a_ref[f, x] = a[f][0][0:32].astype(BF16)
                e_ref[x, f] = a[f][0] * keep[f][0]
                ext_ref[x, f] = a[f][1] * keep[f][1]
        else:
            for f in range(3):
                e_ref[x, f] = keep[f][0]
                ext_ref[x, f] = keep[f][1]
        e_ref[x, 3] = mask_ref[1, x]
        ext_ref[x, 3] = mext_ref[1, x]


def border_kernel(
    v_ref, xe_ref, xo_ref, a_in, e_in, ext_in, w_ref, wp_ref, b_ref, hw_ref, hb_ref, hwp_ref, hbp_ref,
    a_ref, e_ref, ext_ref, se_ref, so_ref, low_ref, high_ref, hid_ref,
):
    gx = lax.axis_index("gx")
    odd_x = gx % 2
    gz = lax.axis_index("gz")

    @pl.when(odd_x == 0)
    def _():
        low_ref[...] = xo_ref[...]
        high_ref[...] = xe_ref[...]

    @pl.when(odd_x == 1)
    def _():
        low_ref[...] = xe_ref[...]
        high_ref[...] = xo_ref[...]

    @pl.when(gx == 0)
    def _():
        low_ref[...] = jnp.zeros_like(low_ref)

    @pl.when(gx == 15)
    def _():
        high_ref[...] = jnp.zeros_like(high_ref)

    for x in (1, 2):
        a_ref[:, x] = a_in[:, x]
        e_ref[x] = e_in[x]
        ext_ref[x] = ext_in[x]
    for x in (0, 3):
        e_ref[x, 3] = e_in[x, 3]
        ext_ref[x, 3] = ext_in[x, 3]

    weights = (w_ref, wp_ref, b_ref, hw_ref, hb_ref, hwp_ref, hbp_ref)
    spread = spread_matrix(gz)
    for x, refs in (
        (0, [low_ref, v_ref.at[0], v_ref.at[1]]),
        (3, [v_ref.at[2], v_ref.at[3], high_ref]),
    ):
        a = conv_slice(gz, refs, weights, spread, hid_ref.at[x // 3])
        for f in range(3):
            a_ref[f, x] = a[f][0][0:32].astype(BF16)
            e_ref[x, f] = a[f][0] * e_in[x, f]
            ext_ref[x, f] = a[f][1] * ext_in[x, f]

    def send(dst_ref, order):
        packed = jnp.zeros((40, 128), F32)
        for j, x in enumerate(order):
            for f in range(4):
                value = ext_ref[x, f]
                slot = 4 * j + f
                packed = packed + (pltpu.roll(value, 8 * slot, 1) if slot else value)
                if j < 3:
                    dst_ref[slot] = e_ref[x, f].astype(BF16)
        dst_ref[12] = e_ref[order[3], 3].astype(BF16)
        dst_ref[13] = e_ref[order[3], 0].astype(BF16)
        dst_ref[14] = packed.astype(BF16)

    @pl.when(odd_x == 0)
    def _():
        send(se_ref, (3, 2, 1, 0))
        send(so_ref, (0, 1, 2, 3))

    @pl.when(odd_x == 1)
    def _():
        send(se_ref, (0, 1, 2, 3))
        send(so_ref, (3, 2, 1, 0))


def rounds_kernel(e_ref, ext_ref, re_ref, ro_ref, ms_ref, out_ref, all_ref, s_ref):
    gx = lax.axis_index("gx")
    odd_x = gx % 2
    has_low = jnp.where(gx == 0, 0.0, 1.0)
    has_high = jnp.where(gx == 15, 0.0, 1.0)
    gz = lax.axis_index("gz")

    def place(src_ref, places, keep_last):
        has = has_high if keep_last else has_low
        packed = src_ref[14].astype(F32) * has
        for j, at in enumerate(places):
            for f in range(4):
                scale = (lambda v: v / 15.0) if f == 3 else (lambda v: v)
                ext = scale(unpack_ext(packed, 4 * j + f, gz))
                if j < 3:
                    main = scale(src_ref[4 * j + f].astype(F32) * has)
                elif f == 3:
                    main = scale(src_ref[12].astype(F32) * has)
                elif f == 0 and keep_last:
                    main = src_ref[13].astype(F32) * has
                else:
                    main, ext = jnp.zeros_like(packed), jnp.zeros_like(packed)
                if f == 3:
                    s_ref[0, at, 0] = main
                    s_ref[0, at, 1] = ext
                else:
                    all_ref[at, f, 0] = main
                    all_ref[at, f, 1] = ext

    @pl.when(odd_x == 0)
    def _():
        place(ro_ref, (3, 2, 1, 0), False)
        place(re_ref, (8, 9, 10, 11), True)

    @pl.when(odd_x == 1)
    def _():
        place(re_ref, (3, 2, 1, 0), False)
        place(ro_ref, (8, 9, 10, 11), True)

    for x in range(4):
        for f in range(3):
            all_ref[4 + x, f, 0] = e_ref[x, f]
            all_ref[4 + x, f, 1] = ext_ref[x, f]
        s_ref[0, 4 + x, 0] = e_ref[x, 3] / 15.0
        s_ref[0, 4 + x, 1] = ext_ref[x, 3] / 15.0

    lane = iota((40, 128), 1)

    def down(pair):
        a, b = pltpu.roll(pair[0], 1, 1), pltpu.roll(pair[1], 1, 1)
        return jnp.where(lane == 0, b, a), jnp.where(lane == 0, a, b)

    def up(pair):
        a, b = pltpu.roll(pair[0], 127, 1), pltpu.roll(pair[1], 127, 1)
        return jnp.where(lane == 127, b, a), jnp.where(lane == 127, a, b)

    for r in range(ROUNDS):
        src, dst = r % 2, (r + 1) % 2

        for x in range(r + 1, 11 - r):
            here = (s_ref[src, x, 0], s_ref[src, x, 1])
            best = list(here)
            ez = (all_ref[x, 2, 0], all_ref[x, 2, 1])
            z_low = down(here)
            z_high = up(tuple(jnp.minimum(here[i], ez[i]) for i in range(2)))
            for i in range(2):
                ey = all_ref[x, 1, i]
                value = here[i]
                value = jnp.maximum(value, jnp.minimum(s_ref[src, x - 1, i], all_ref[x, 0, i]))
                value = jnp.maximum(value, jnp.minimum(s_ref[src, x + 1, i], all_ref[x + 1, 0, i]))
                value = jnp.maximum(value, jnp.minimum(pltpu.roll(here[i], 1, 0), ey))
                value = jnp.maximum(value, pltpu.roll(jnp.minimum(here[i], ey), 39, 0))
                value = jnp.maximum(value, jnp.minimum(z_low[i], ez[i]))
                value = jnp.maximum(value, z_high[i])
                s_ref[dst, x, i] = value

    for x in range(4):
        out_ref[x] = s_ref[ROUNDS % 2, 4 + x, 0, 0:32] * ms_ref[0, x]


def stay(value):
    return pltpu.with_memory_space_constraint(value, pltpu.HBM)


def call(kernel, shapes, args, scratch=(), aliases={}, specs=None):
    return pl.pallas_call(
        kernel,
        out_shape=[jax.ShapeDtypeStruct(s, d) for s, d in shapes],
        in_specs=specs or [VMEM] * len(args),
        out_specs=[VMEM] * len(shapes),
        scratch_shapes=[pltpu.VMEM(*s) if isinstance(s[0], tuple) else s[0](*s[1:]) for s in scratch],
        input_output_aliases=aliases,
        compiler_params=PARAMS,
    )(*args)


def body(features, conv_weight, conv_bias, head_weight, head_bias, mask, seeds):
    v, zs, ms = call(
        pack_kernel,
        [((4, 46, 32, 128), BF16), ((288, 128), BF16), ((2, 4, 32, 128), F32)],
        tuple(stay(a) for a in (features, mask, seeds)),
        scratch=[
            ((4, 32, 32, 128), BF16),
            ((4, 32, 128), jnp.int32),
            ((4, 32, 128), jnp.int32),
            (pltpu.SemaphoreType.DMA, (6,)),
        ],
        specs=[HBM] * 3,
    )
    zs, conv_weight, conv_bias, head_weight, head_bias = lax.optimization_barrier(
        (zs, conv_weight, conv_bias, head_weight, head_bias)
    )
    zr = lax.ppermute(zs, "gz", [(0, 1), (1, 0)])
    taps = jnp.transpose(conv_weight, (2, 3, 4, 0, 1)).reshape(27, 32, 32)
    forms = call(
        weights_kernel,
        [
            ((96, 288), BF16),
            ((288, 96), BF16),
            ((32, 128), F32),
            ((24, 256), F32),
            ((24, 128), F32),
            ((8, 32), F32),
            ((8, 128), F32),
        ],
        tuple(stay(a) for a in (taps, conv_bias.reshape(1, 32), head_weight, head_bias)),
        scratch=[
            ((27, 32, 32), BF16),
            ((1, 32), F32),
            ((3, 32), BF16),
            (pltpu.SMEM, (3,), F32),
            (pltpu.SemaphoreType.DMA, (4,)),
        ],
        specs=[HBM] * 4,
    )
    zr, *weights = lax.optimization_barrier((zr, *forms))
    weights = tuple(weights)
    pt, ye, yo = call(
        yface_kernel,
        [((4, 2, 32, 128), BF16), ((4, 208, 128), BF16), ((4, 208, 128), BF16)],
        (v, zs, zr, ms),
        scratch=[((2, 4, 16, 128), F32)],
    )
    even, odd = swaps("gy")
    yo = lax.ppermute(yo, "gy", odd)
    ye = lax.ppermute(ye, "gy", even)
    v, xe, xo = call(
        xface_kernel,
        [((4, 46, 32, 128), BF16), ((46, 32, 128), BF16), ((46, 32, 128), BF16)],
        (v, pt, ye, yo),
    )
    even, odd = swaps("gx")
    xo = lax.ppermute(xo, "gx", odd)
    xe = lax.ppermute(xe, "gx", even)
    affinity, e, ext = call(
        inner_kernel,
        [((3, 4, 32, 128), BF16), ((4, 4, 40, 128), F32), ((4, 4, 40, 128), F32)],
        (v, ye, yo, zr, ms) + weights,
        scratch=[((2, 1280, 128), BF16), ((2, 4, 40, 128), F32), ((2, 4, 40, 128), F32)],
    )
    affinity, e, ext, se, so = call(
        border_kernel,
        [
            ((3, 4, 32, 128), BF16),
            ((4, 4, 40, 128), F32),
            ((4, 4, 40, 128), F32),
            ((15, 40, 128), BF16),
            ((15, 40, 128), BF16),
        ],
        (v, xe, xo, affinity, e, ext) + weights,
        scratch=[((46, 32, 128), BF16), ((46, 32, 128), BF16), ((2, 1280, 128), BF16)],
    )
    so = lax.ppermute(so, "gx", odd)
    se = lax.ppermute(se, "gx", even)
    (strength,) = call(
        rounds_kernel,
        [((4, 32, 128), F32)],
        (e, ext, se, so, ms),
        scratch=[((12, 3, 2, 40, 128), F32), ((2, 12, 2, 40, 128), F32)],
    )
    return (affinity, strength)


def solution(mesh):
    in_specs = (
        P(None, "gx", "gy", "gz"),
        P(),
        P(),
        P(),
        P(),
        P("gx", "gy", "gz"),
        P("gx", "gy", "gz"),
    )
    out_specs = (P(None, "gx", "gy", "gz"), P("gx", "gy", "gz"))
    return jax.shard_map(body, mesh=mesh, in_specs=in_specs, out_specs=out_specs, check_vma=False)
```

```python
import jax
import jax.numpy as jnp
from jax import lax
from jax.experimental import pallas as pl
from jax.experimental.pallas import tpu as pltpu
from jax.sharding import PartitionSpec as P

ROUNDS = 4
F32 = jnp.float32
BF16 = jnp.bfloat16
VMEM = pl.BlockSpec(memory_space=pltpu.VMEM)
HBM = pl.BlockSpec(memory_space=pltpu.HBM)
PARAMS = pltpu.CompilerParams(vmem_limit_bytes=12 * 2**20)


def swaps(axis):
    count = lax.axis_size(axis)

    def pairs(first):
        return [
            p
            for i in range(first, count + first, 2)
            for p in ((i % count, (i + 1) % count), ((i + 1) % count, i % count))
        ]

    return pairs(0), pairs(1)


def iota(shape, dim):
    return lax.broadcasted_iota(jnp.int32, shape, dim)


def pack_kernel(x_hbm, m_hbm, s_hbm, v_ref, zs_ref, ms_ref, xe_ref, xo_ref, x_ref, m_ref, s_ref, sems):
    gz = lax.axis_index("gz")
    copies = [pltpu.make_async_copy(x_hbm.at[:, x], x_ref.at[x], sems.at[x]) for x in range(4)]
    copies += [
        pltpu.make_async_copy(m_hbm, m_ref, sems.at[4]),
        pltpu.make_async_copy(s_hbm, s_ref, sems.at[5]),
    ]
    for copy in copies:
        copy.start()
    lane = iota((128, 128), 1)
    row = iota((128, 128), 0)
    base = jnp.where(gz == 0, 120, 0)
    hit = row == base + lane % 8
    sels = [jnp.where(hit & (lane // 8 == y), 1.0, 0.0).astype(BF16) for y in range(16)]
    for x in range(4):
        copies[x].wait()
        v_ref[x, 5:37] = jnp.swapaxes(x_ref[x], 0, 1)
    even_face = jnp.where(lax.axis_index("gx") % 2 == 0, 3, 0)
    xe_ref[...] = v_ref[even_face, 5:37]
    xo_ref[...] = v_ref[3 - even_face, 5:37]
    acc = jnp.zeros((256, 128), F32)
    for y in range(16):
        lhs = jnp.concatenate(
            [v_ref[x, 5 + 16 * half + y] for x in range(4) for half in range(2)], axis=0
        )
        acc = acc + jnp.dot(lhs, sels[y], preferred_element_type=F32)
    zs_ref[0:256] = acc.astype(BF16)
    copies[4].wait()
    copies[5].wait()
    lane = iota((32, 128), 1)
    edge = (lane >= jnp.where(gz == 0, 124, 0)) & (lane < jnp.where(gz == 0, 128, 4))
    packed = jnp.zeros((32, 128), F32)
    for x in range(4):
        mask = m_ref[x].astype(F32)
        seed = mask * s_ref[x].astype(F32)
        ms_ref[0, x] = mask
        ms_ref[1, x] = seed
        for slot, value in ((x, mask), (4 + x, seed)):
            value = jnp.where(edge, value, 0.0)
            packed = packed + (pltpu.roll(value, 8 * slot, 1) if slot else value)
    zs_ref[256:288] = packed.astype(BF16)


def weights_kernel(
    t_hbm, b_hbm, h_hbm, hb_hbm, w_ref, wp_ref, bias_ref, hw_ref, hbias_ref, hwp_ref, hbp_ref,
    t_ref, b_ref, h_ref, hb_ref, sems,
):
    copies = [
        pltpu.make_async_copy(src, dst, sems.at[i])
        for i, (src, dst) in enumerate(
            ((t_hbm, t_ref), (b_hbm, b_ref), (h_hbm, h_ref), (hb_hbm, hb_ref))
        )
    ]
    for copy in copies:
        copy.start()
    for copy in copies:
        copy.wait()
    for dz in range(3):
        w_ref[32 * dz : 32 * dz + 32] = jnp.concatenate(
            [t_ref[3 * k + dz] for k in range(9)], axis=1
        )
    for k in range(9):
        wp_ref[32 * k : 32 * k + 32] = jnp.concatenate(
            [t_ref[9 * dx + k] for dx in range(3)], axis=1
        )
    across = jnp.broadcast_to(b_ref[...], (32, 32))
    diagonal = iota((32, 32), 0) == iota((32, 32), 1)
    column = jnp.sum(jnp.where(diagonal, across, 0.0), axis=1, keepdims=True)
    bias_ref[...] = jnp.broadcast_to(column, (32, 128))
    same = iota((8, 256), 0) == iota((8, 256), 1) // 32
    few = iota((8, 128), 0)
    hwp = jnp.zeros((8, 32), F32)
    hbp = jnp.zeros((8, 128), F32)
    heads = h_ref[...].astype(F32)
    for c in range(3):
        line = jnp.concatenate([heads[c : c + 1]] * 8, axis=1)
        hw_ref[8 * c : 8 * c + 8] = jnp.where(same, jnp.broadcast_to(line, (8, 256)), 0.0)
        hbias_ref[8 * c : 8 * c + 8] = jnp.full((8, 128), hb_ref[c], F32)
        hwp = jnp.where(few[:, 0:32] == c, jnp.broadcast_to(heads[c : c + 1], (8, 32)), hwp)
        hbp = jnp.where(few == c, hb_ref[c], hbp)
    hwp_ref[...] = hwp
    hbp_ref[...] = hbp


def unpack_ext(packed, slot, gz):
    lane = iota(packed.shape, 1)
    inside = (lane >= jnp.where(gz == 0, 0, 124)) & (lane < jnp.where(gz == 0, 4, 128))
    value = pltpu.roll(packed, (128 - 8 * slot) % 128, 1) if slot else packed
    return jnp.where(inside, value, 0.0)


def yface_kernel(v_ref, zs_ref, zr_ref, ms_ref, pt_ref, ye_ref, yo_ref, block_ref):
    odd = lax.axis_index("gy") % 2
    gz = lax.axis_index("gz")
    lane = iota((256, 128), 1) % 8
    own = pltpu.roll(zs_ref[0:256].astype(F32), jnp.where(gz == 0, 122, 5), 1)
    other = pltpu.roll(zr_ref[0:256].astype(F32), jnp.where(gz == 0, 2, 125), 1)
    own_from = jnp.where(gz == 0, 0, 5)
    other_from = jnp.where(gz == 0, 2, 0)
    packed = jnp.where((lane >= own_from) & (lane < own_from + 2), own, 0.0)
    packed = jnp.where((lane >= other_from) & (lane < other_from + 5), other, packed)
    packed = packed.astype(BF16).reshape(4, 2, 32, 128)
    pt_ref[...] = packed
    zmask = zr_ref[256:288].astype(F32)
    for x in range(4):
        fields = (ms_ref[0, x], ms_ref[1, x], unpack_ext(zmask, x, gz), unpack_ext(zmask, 4 + x, gz))
        for f, value in enumerate(fields):
            block_ref[0, x, 4 * f : 4 * f + 4] = value[28:32]
            block_ref[1, x, 4 * f : 4 * f + 4] = value[0:4]

    def write(dst_ref, up):
        for x in range(4):
            first = 32 if up else 5
            for j in range(5):
                dst_ref[x, 32 * j : 32 * j + 32] = v_ref[x, first + j]
            dst_ref[x, 160:192] = pt_ref[x, 1 if up else 0]
            dst_ref[x, 192:208] = block_ref[0 if up else 1, x].astype(BF16)

    @pl.when(odd == 0)
    def _():
        write(ye_ref, True)
        write(yo_ref, False)

    @pl.when(odd == 1)
    def _():
        write(ye_ref, False)
        write(yo_ref, True)


def xface_kernel(v_in_ref, pt_ref, ye_ref, yo_ref, v_ref, xe_ref, xo_ref):
    odd_x = lax.axis_index("gx") % 2
    odd_y = lax.axis_index("gy") % 2

    gy = lax.axis_index("gy")
    for x in range(4):
        v_ref[x, 5:37] = v_in_ref[x, 5:37]

    def fill(low_ref, high_ref):
        for x in range(4):
            for j in range(5):
                v_ref[x, j] = low_ref[x, 32 * j : 32 * j + 32]
                v_ref[x, 37 + j] = high_ref[x, 32 * j : 32 * j + 32]
            v_ref[x, 42] = low_ref[x, 160:192]
            v_ref[x, 43] = pt_ref[x, 0]
            v_ref[x, 44] = pt_ref[x, 1]
            v_ref[x, 45] = high_ref[x, 160:192]

    @pl.when(odd_y == 0)
    def _():
        fill(yo_ref, ye_ref)

    @pl.when(odd_y == 1)
    def _():
        fill(ye_ref, yo_ref)

    zero = jnp.zeros((32, 128), BF16)

    @pl.when(gy == 0)
    def _():
        for x in range(4):
            for tile in (0, 1, 2, 3, 4, 42):
                v_ref[x, tile] = zero

    @pl.when(gy == 7)
    def _():
        for x in range(4):
            for tile in (37, 38, 39, 40, 41, 45):
                v_ref[x, tile] = zero

    even_face = jnp.where(odd_x == 0, 3, 0)
    for dst_ref, face in ((xe_ref, even_face), (xo_ref, 3 - even_face)):
        dst_ref[0:5] = v_ref[face, 0:5]
        dst_ref[5:14] = v_ref[face, 37:46]


def head(hidden, head_ref, bias_ref):
    logits = jnp.dot(head_ref[...].astype(BF16), hidden, preferred_element_type=F32)
    logits = logits + jnp.tile(bias_ref[...], (1, logits.shape[1] // 128))
    return jax.nn.sigmoid(logits).astype(BF16).astype(F32)


def tile_of(row):
    return row + 5 if row < 36 else row - 35


def spread_matrix(gz):
    k = iota((512, 128), 0) % 8
    to = iota((512, 128), 1)
    goal = jnp.where(gz == 0, (k + 126) % 128, (k + 123) % 128)
    return jnp.where((k >= 1) & (k <= 5) & (to == goal), 1.0, 0.0).astype(BF16)


INTERIOR = tuple(range(1, 31))
OTHERS = (31, 32, 33, 34, 35, 36, 37, 38, 39, 0)


def conv_main(refs, weights, hid_ref, rows):
    lane = iota((32, 128), 1)
    first, last = lane == 0, lane == 127
    w, bias = weights[0][...], weights[2][...]
    for pair in zip(rows[0::2], rows[1::2]):
        cols = []
        for row in pair:
            t = tile_of(row)
            cols.append(
                jnp.concatenate([r[t - 1 : t + 2].reshape(96, 128) for r in refs], axis=0)
            )
        part = jnp.dot(w, jnp.concatenate(cols, axis=1), preferred_element_type=F32)
        for i, row in enumerate(pair):
            one = part[:, 128 * i : 128 * i + 128]
            left = jnp.where(first, 0.0, pltpu.roll(one[0:32], 1, 1))
            right = jnp.where(last, 0.0, pltpu.roll(one[64:96], 127, 1))
            hid = jnp.maximum(one[32:64] + left + right + bias, 0.0)
            hid_ref[32 * row : 32 * row + 32] = hid.astype(BF16)


def conv_packed(refs, weights, spread):
    _, wp_ref, b_ref, _, _, hwp_ref, hbp_ref = weights
    cols = [jnp.concatenate([r[42 + q] for r in refs], axis=0) for q in range(4)]
    part = jnp.dot(wp_ref[...], jnp.concatenate(cols, axis=1), preferred_element_type=F32)
    total = jnp.tile(b_ref[...], (1, 4))
    for dy in range(3):
        for dz in range(3):
            k = 3 * dy + dz
            shift = (-(8 * (dy - 1) + dz - 1)) % 512
            one = part[32 * k : 32 * k + 32]
            total = total + (pltpu.roll(one, shift, 1) if shift else one)
    value = head(jnp.maximum(total, 0.0).astype(BF16), hwp_ref, hbp_ref)
    row = iota((40, 512), 0)
    at = iota((40, 512), 1)
    mine = at // 8 - 16 == jnp.where(row < 36, row, row - 40)
    lhs = jnp.concatenate(
        [jnp.where(mine, jnp.broadcast_to(value[c : c + 1], (40, 512)), 0.0) for c in range(3)],
        axis=0,
    ).astype(BF16)
    return jnp.dot(lhs, spread, preferred_element_type=F32)


def conv_slice(gz, refs, weights, spread, interior_ref, hid_ref):
    conv_main(refs, weights, hid_ref, OTHERS)
    border = conv_packed(refs, weights, spread)

    def hidden(row):
        return (interior_ref if row in INTERIOR else hid_ref)[32 * row : 32 * row + 32]

    hid = jnp.concatenate(
        [jnp.concatenate([hidden(8 * g + i) for i in range(8)], axis=0) for g in range(5)], axis=1
    )
    value = head(hid, weights[3], weights[4])
    fixed = iota((40, 128), 1) == jnp.where(gz == 0, 127, 0)
    out = []
    for c in range(3):
        main = jnp.concatenate(
            [value[8 * c : 8 * c + 8, 128 * g : 128 * g + 128] for g in range(5)], axis=0
        )
        one = border[40 * c : 40 * c + 40]
        out.append((jnp.where(fixed, one, main), jnp.where(fixed, 0.0, one)))
    return out


def inner_rows_kernel(v_ref, w_ref, b_ref, hid_ref):
    for x in (1, 2):
        refs = [v_ref.at[x - 1 + d] for d in range(3)]
        conv_main(refs, (w_ref, None, b_ref), hid_ref.at[x - 1], INTERIOR)


def by_side(even_ref, odd_ref, fill):
    gx = lax.axis_index("gx")

    @pl.when(gx % 2 == 0)
    def _():
        fill(odd_ref, even_ref)

    @pl.when(gx % 2 == 1)
    def _():
        fill(even_ref, odd_ref)


def border_rows_kernel(v_ref, xe_ref, xo_ref, w_ref, b_ref, hid_ref, face_ref):
    gx = lax.axis_index("gx")

    def fill(low_ref, high_ref):
        face_ref[0, 5:37] = low_ref[...]
        face_ref[1, 5:37] = high_ref[...]

    by_side(xe_ref, xo_ref, fill)

    @pl.when(gx == 0)
    def _():
        face_ref[0, 5:37] = jnp.zeros((32, 32, 128), BF16)

    @pl.when(gx == 15)
    def _():
        face_ref[1, 5:37] = jnp.zeros((32, 32, 128), BF16)

    for i, refs in enumerate(
        (
            [face_ref.at[0], v_ref.at[0], v_ref.at[1]],
            [v_ref.at[2], v_ref.at[3], face_ref.at[1]],
        )
    ):
        conv_main(refs, (w_ref, None, b_ref), hid_ref.at[i], INTERIOR)


def inner_kernel(
    v_ref, rows_ref, ye_ref, yo_ref, zr_ref, ms_ref, w_ref, wp_ref, b_ref, hw_ref, hb_ref, hwp_ref, hbp_ref,
    a_ref, e_ref, ext_ref, hid_ref, mask_ref, mext_ref,
):
    gy = lax.axis_index("gy")
    odd_y = gy % 2
    gz = lax.axis_index("gz")
    zmask = zr_ref[256:288].astype(F32)
    for x in range(4):
        for f in range(2):
            mask_ref[f, x, 0:32] = ms_ref[f, x]
            mext_ref[f, x, 0:32] = unpack_ext(zmask, 4 * f + x, gz)

    def fill(lower_ref, upper_ref):
        has_lower = jnp.where(gy == 0, 0.0, 1.0)
        has_upper = jnp.where(gy == 7, 0.0, 1.0)
        for x in range(4):
            lower = lower_ref[x, 192:208].astype(F32) * has_lower
            upper = upper_ref[x, 192:208].astype(F32) * has_upper
            for f in range(2):
                mask_ref[f, x, 32:36] = upper[4 * f : 4 * f + 4]
                mask_ref[f, x, 36:40] = lower[4 * f : 4 * f + 4]
                mext_ref[f, x, 32:36] = upper[8 + 4 * f : 12 + 4 * f]
                mext_ref[f, x, 36:40] = lower[8 + 4 * f : 12 + 4 * f]

    @pl.when(odd_y == 0)
    def _():
        fill(yo_ref, ye_ref)

    @pl.when(odd_y == 1)
    def _():
        fill(ye_ref, yo_ref)

    lane = iota((40, 128), 1)
    row = iota((40, 128), 0)

    def shift_y(value):
        return jnp.where(row == 36, 0.0, pltpu.roll(value, 1, 0))

    weights = (w_ref, wp_ref, b_ref, hw_ref, hb_ref, hwp_ref, hbp_ref)
    spread = spread_matrix(gz)
    for x in range(4):
        main, ext = mask_ref[0, x], mext_ref[0, x]
        rolled, rolled_ext = pltpu.roll(main, 1, 1), pltpu.roll(ext, 1, 1)
        z_main = main * jnp.where(lane == 0, rolled_ext, rolled)
        z_ext = ext * jnp.where(lane == 0, rolled, rolled_ext)
        y_main, y_ext = main * shift_y(main), ext * shift_y(ext)
        x_main = main * mask_ref[0, x - 1] if x else main
        x_ext = ext * mext_ref[0, x - 1] if x else ext
        keep = ((x_main, x_ext), (y_main, y_ext), (z_main, z_ext))
        if 0 < x < 3:
            refs = [v_ref.at[x - 1 + d] for d in range(3)]
            a = conv_slice(gz, refs, weights, spread, rows_ref.at[x - 1], hid_ref.at[x - 1])
            for f in range(3):
                a_ref[f, x] = a[f][0][0:32].astype(BF16)
                e_ref[x, f] = a[f][0] * keep[f][0]
                ext_ref[x, f] = a[f][1] * keep[f][1]
        else:
            for f in range(3):
                e_ref[x, f] = keep[f][0]
                ext_ref[x, f] = keep[f][1]
        e_ref[x, 3] = mask_ref[1, x]
        ext_ref[x, 3] = mext_ref[1, x]


def border_kernel(
    v_ref, face_ref, rows_ref, xe_ref, xo_ref, a_in, e_in, ext_in, w_ref, wp_ref, b_ref, hw_ref, hb_ref, hwp_ref, hbp_ref,
    a_ref, e_ref, ext_ref, se_ref, so_ref, side_ref, hid_ref,
):
    gx = lax.axis_index("gx")
    odd_x = gx % 2
    gz = lax.axis_index("gz")

    def fill(low_ref, high_ref):
        for i, ref in enumerate((low_ref, high_ref)):
            side_ref[i, 0:5] = ref[0:5]
            side_ref[i, 37:46] = ref[5:14]

    by_side(xe_ref, xo_ref, fill)
    for i, end in ((0, 0), (1, 15)):
        for at in (5, 6, 35, 36):
            side_ref[i, at] = face_ref[i, at]

        @pl.when(gx == end)
        def _():
            side_ref[i, 0:5] = jnp.zeros((5, 32, 128), BF16)
            side_ref[i, 37:46] = jnp.zeros((9, 32, 128), BF16)

    for x in (1, 2):
        a_ref[:, x] = a_in[:, x]
        e_ref[x] = e_in[x]
        ext_ref[x] = ext_in[x]
    for x in (0, 3):
        e_ref[x, 3] = e_in[x, 3]
        ext_ref[x, 3] = ext_in[x, 3]

    weights = (w_ref, wp_ref, b_ref, hw_ref, hb_ref, hwp_ref, hbp_ref)
    spread = spread_matrix(gz)
    for x, refs in (
        (0, [side_ref.at[0], v_ref.at[0], v_ref.at[1]]),
        (3, [v_ref.at[2], v_ref.at[3], side_ref.at[1]]),
    ):
        a = conv_slice(gz, refs, weights, spread, rows_ref.at[x // 3], hid_ref.at[x // 3])
        for f in range(3):
            a_ref[f, x] = a[f][0][0:32].astype(BF16)
            e_ref[x, f] = a[f][0] * e_in[x, f]
            ext_ref[x, f] = a[f][1] * ext_in[x, f]

    def send(dst_ref, order):
        packed = jnp.zeros((40, 128), F32)
        for j, x in enumerate(order):
            for f in range(4 if j < 3 else 0):
                value = ext_ref[x, f]
                slot = 4 * j + f
                packed = packed + (pltpu.roll(value, 8 * slot, 1) if slot else value)
                dst_ref[slot] = e_ref[x, f].astype(BF16)
        dst_ref[12] = e_ref[order[3], 3].astype(BF16)
        dst_ref[13] = e_ref[order[3], 0].astype(BF16)
        dst_ref[14] = packed.astype(BF16)

    @pl.when(odd_x == 0)
    def _():
        send(se_ref, (3, 2, 1, 0))
        send(so_ref, (0, 1, 2, 3))

    @pl.when(odd_x == 1)
    def _():
        send(se_ref, (0, 1, 2, 3))
        send(so_ref, (3, 2, 1, 0))


def rounds_kernel(a_ref, e_ref, ext_ref, re_ref, ro_ref, ms_ref, a_hbm, out_hbm, all_ref, s_ref, out_ref, sems):
    affinity_copy = pltpu.make_async_copy(a_ref, a_hbm, sems.at[4])
    affinity_copy.start()
    gx = lax.axis_index("gx")
    odd_x = gx % 2
    has_low = jnp.where(gx == 0, 0.0, 1.0)
    has_high = jnp.where(gx == 15, 0.0, 1.0)
    gz = lax.axis_index("gz")

    def place(src_ref, places, keep_last):
        has = has_high if keep_last else has_low
        packed = src_ref[14].astype(F32) * has
        for j, at in enumerate(places):
            for f in range(4):
                scale = (lambda v: v / 15.0) if f == 3 else (lambda v: v)
                ext = scale(unpack_ext(packed, 4 * j + f, gz)) if j < 3 else jnp.zeros_like(packed)
                if j < 3:
                    main = scale(src_ref[4 * j + f].astype(F32) * has)
                elif f == 3:
                    main = scale(src_ref[12].astype(F32) * has)
                elif f == 0 and keep_last:
                    main = src_ref[13].astype(F32) * has
                else:
                    main = jnp.zeros_like(packed)
                if f == 3:
                    s_ref[0, at, 0] = main
                    s_ref[0, at, 1] = ext
                else:
                    all_ref[at, f, 0] = main
                    all_ref[at, f, 1] = ext

    @pl.when(odd_x == 0)
    def _():
        place(ro_ref, (3, 2, 1, 0), False)
        place(re_ref, (8, 9, 10, 11), True)

    @pl.when(odd_x == 1)
    def _():
        place(re_ref, (3, 2, 1, 0), False)
        place(ro_ref, (8, 9, 10, 11), True)

    for x in range(4):
        for f in range(3):
            all_ref[4 + x, f, 0] = e_ref[x, f]
            all_ref[4 + x, f, 1] = ext_ref[x, f]
        s_ref[0, 4 + x, 0] = e_ref[x, 3] / 15.0
        s_ref[0, 4 + x, 1] = ext_ref[x, 3] / 15.0

    lane = iota((40, 128), 1)

    def down(pair):
        a, b = pltpu.roll(pair[0], 1, 1), pltpu.roll(pair[1], 1, 1)
        return jnp.where(lane == 0, b, a), jnp.where(lane == 0, a, b)

    def up(pair):
        a, b = pltpu.roll(pair[0], 127, 1), pltpu.roll(pair[1], 127, 1)
        return jnp.where(lane == 127, b, a), jnp.where(lane == 127, a, b)

    for r in range(ROUNDS):
        src, dst = r % 2, (r + 1) % 2

        for x in range(r + 1, 11 - r):
            here = (s_ref[src, x, 0], s_ref[src, x, 1])
            best = list(here)
            ez = (all_ref[x, 2, 0], all_ref[x, 2, 1])
            z_low = down(here)
            z_high = up(tuple(jnp.minimum(here[i], ez[i]) for i in range(2)))
            for i in range(2):
                ey = all_ref[x, 1, i]
                value = here[i]
                value = jnp.maximum(value, jnp.minimum(s_ref[src, x - 1, i], all_ref[x, 0, i]))
                value = jnp.maximum(value, jnp.minimum(s_ref[src, x + 1, i], all_ref[x + 1, 0, i]))
                value = jnp.maximum(value, jnp.minimum(pltpu.roll(here[i], 1, 0), ey))
                value = jnp.maximum(value, pltpu.roll(jnp.minimum(here[i], ey), 39, 0))
                value = jnp.maximum(value, jnp.minimum(z_low[i], ez[i]))
                value = jnp.maximum(value, z_high[i])
                s_ref[dst, x, i] = value

    copies = [affinity_copy]
    for x in range(4):
        out_ref[x] = s_ref[ROUNDS % 2, 4 + x, 0, 0:32] * ms_ref[0, x]
        copies.append(pltpu.make_async_copy(out_ref.at[x], out_hbm.at[x], sems.at[x]))
        copies[-1].start()
    for copy in copies:
        copy.wait()


def stay(value):
    return pltpu.with_memory_space_constraint(value, pltpu.HBM)


def call(kernel, shapes, args, scratch=(), specs=None, out_specs=None):
    return pl.pallas_call(
        kernel,
        out_shape=[jax.ShapeDtypeStruct(s, d) for s, d in shapes],
        in_specs=specs or [VMEM] * len(args),
        out_specs=out_specs or [VMEM] * len(shapes),
        scratch_shapes=[pltpu.VMEM(*s) if isinstance(s[0], tuple) else s[0](*s[1:]) for s in scratch],
        compiler_params=PARAMS,
    )(*args)


def body(features, conv_weight, conv_bias, head_weight, head_bias, mask, seeds):
    v, zs, ms, fe, fo = call(
        pack_kernel,
        [
            ((4, 46, 32, 128), BF16),
            ((288, 128), BF16),
            ((2, 4, 32, 128), F32),
            ((32, 32, 128), BF16),
            ((32, 32, 128), BF16),
        ],
        tuple(stay(a) for a in (features, mask, seeds)),
        scratch=[
            ((4, 32, 32, 128), BF16),
            ((4, 32, 128), jnp.int32),
            ((4, 32, 128), jnp.int32),
            (pltpu.SemaphoreType.DMA, (6,)),
        ],
        specs=[HBM] * 3,
    )
    zr = lax.ppermute(zs, "gz", [(0, 1), (1, 0)])
    even_x, odd_x = swaps("gx")
    fo = lax.ppermute(fo, "gx", odd_x)
    fe = lax.ppermute(fe, "gx", even_x)
    pt, ye, yo = call(
        yface_kernel,
        [((4, 2, 32, 128), BF16), ((4, 208, 128), BF16), ((4, 208, 128), BF16)],
        (v, zs, zr, ms),
        scratch=[((2, 4, 16, 128), F32)],
    )
    ye, yo, vy, conv_weight, conv_bias, head_weight, head_bias = lax.optimization_barrier(
        (ye, yo, v, conv_weight, conv_bias, head_weight, head_bias)
    )
    taps = jnp.transpose(conv_weight, (2, 3, 4, 0, 1)).reshape(27, 32, 32)
    forms = call(
        weights_kernel,
        [
            ((96, 288), BF16),
            ((288, 96), BF16),
            ((32, 128), F32),
            ((24, 256), F32),
            ((24, 128), F32),
            ((8, 32), F32),
            ((8, 128), F32),
        ],
        tuple(stay(a) for a in (taps, conv_bias.reshape(1, 32), head_weight, head_bias)),
        scratch=[
            ((27, 32, 32), BF16),
            ((1, 32), F32),
            ((3, 32), BF16),
            (pltpu.SMEM, (3,), F32),
            (pltpu.SemaphoreType.DMA, (4,)),
        ],
        specs=[HBM] * 4,
    )
    weights = tuple(forms)
    rows_shape = [((2, 1280, 128), BF16)]
    (inner_rows,) = call(inner_rows_kernel, rows_shape, (vy, weights[0], weights[2]))
    even, odd = swaps("gy")
    yo = lax.ppermute(yo, "gy", odd)
    ye = lax.ppermute(ye, "gy", even)
    ye, yo, inner_rows = lax.optimization_barrier((ye, yo, inner_rows))
    v, xe, xo = call(
        xface_kernel,
        [((4, 46, 32, 128), BF16), ((14, 32, 128), BF16), ((14, 32, 128), BF16)],
        (v, pt, ye, yo),
    )
    xe, xo, v, fe, fo = lax.optimization_barrier((xe, xo, v, fe, fo))
    xo = lax.ppermute(xo, "gx", odd_x)
    xe = lax.ppermute(xe, "gx", even_x)
    affinity, e, ext = call(
        inner_kernel,
        [((3, 4, 32, 128), BF16), ((4, 4, 40, 128), F32), ((4, 4, 40, 128), F32)],
        (v, inner_rows, ye, yo, zr, ms) + weights,
        scratch=[((2, 1280, 128), BF16), ((2, 4, 40, 128), F32), ((2, 4, 40, 128), F32)],
    )
    border_rows, faces = call(
        border_rows_kernel,
        rows_shape + [((2, 46, 32, 128), BF16)],
        (v, fe, fo, weights[0], weights[2]),
    )
    xe, xo, affinity, e, ext, border_rows, faces = lax.optimization_barrier(
        (xe, xo, affinity, e, ext, border_rows, faces)
    )
    affinity, e, ext, se, so = call(
        border_kernel,
        [
            ((3, 4, 32, 128), BF16),
            ((4, 4, 40, 128), F32),
            ((4, 4, 40, 128), F32),
            ((15, 40, 128), BF16),
            ((15, 40, 128), BF16),
        ],
        (v, faces, border_rows, xe, xo, affinity, e, ext) + weights,
        scratch=[((2, 46, 32, 128), BF16), ((2, 1280, 128), BF16)],
    )
    so = lax.ppermute(so, "gx", odd_x)
    se = lax.ppermute(se, "gx", even_x)
    affinity, strength = call(
        rounds_kernel,
        [((3, 4, 32, 128), BF16), ((4, 32, 128), F32)],
        (affinity, e, ext, se, so, ms),
        scratch=[
            ((12, 3, 2, 40, 128), F32),
            ((2, 12, 2, 40, 128), F32),
            ((4, 32, 128), F32),
            (pltpu.SemaphoreType.DMA, (5,)),
        ],
        out_specs=[HBM, HBM],
    )
    return (affinity, strength)


def solution(mesh):
    in_specs = (
        P(None, "gx", "gy", "gz"),
        P(),
        P(),
        P(),
        P(),
        P("gx", "gy", "gz"),
        P("gx", "gy", "gz"),
    )
    out_specs = (P(None, "gx", "gy", "gz"), P("gx", "gy", "gz"))
    return jax.shard_map(body, mesh=mesh, in_specs=in_specs, out_specs=out_specs, check_vma=False)
```

```python
import jax
import jax.numpy as jnp
from jax import lax
from jax.experimental import pallas as pl
from jax.experimental.pallas import tpu as pltpu
from jax.sharding import PartitionSpec as P

ROUNDS = 4
F32 = jnp.float32
BF16 = jnp.bfloat16
VMEM = pl.BlockSpec(memory_space=pltpu.VMEM)
HBM = pl.BlockSpec(memory_space=pltpu.HBM)
PARAMS = pltpu.CompilerParams(vmem_limit_bytes=12 * 2**20)


def swaps(count):
    def pairs(first):
        return [
            p
            for i in range(first, count + first, 2)
            for p in ((i % count, (i + 1) % count), ((i + 1) % count, i % count))
        ]

    return pairs(0), pairs(1)


def swaps_gx():
    nx, ny = lax.axis_size("gx"), lax.axis_size("gy")

    def partner(x, y, first):
        other = x + 1 if x % 2 == first else x - 1
        return (other, y) if 0 <= other < nx else (x, y ^ 1)

    def pairs(first):
        out = []
        for x in range(nx):
            for y in range(ny):
                px, py = partner(x, y, first)
                out.append((x * ny + y, px * ny + py))
        return out

    return pairs(0), pairs(1)


def iota(shape, dim):
    return lax.broadcasted_iota(jnp.int32, shape, dim)


def pack_kernel(x_hbm, m_hbm, s_hbm, v_ref, zs_ref, ms_ref, xe_ref, xo_ref, x_ref, m_ref, s_ref, sems):
    gz = lax.axis_index("gz")
    copies = [pltpu.make_async_copy(x_hbm.at[:, x], x_ref.at[x], sems.at[x]) for x in range(4)]
    small = [
        pltpu.make_async_copy(m_hbm, m_ref, sems.at[4]),
        pltpu.make_async_copy(s_hbm, s_ref, sems.at[5]),
    ]
    for copy in small + copies:
        copy.start()
    lane = iota((128, 128), 1)
    row = iota((128, 128), 0)
    base = jnp.where(gz == 0, 120, 0)
    hit = row == base + lane % 8
    sels = [jnp.where(hit & (lane // 8 == y), 1.0, 0.0).astype(BF16) for y in range(16)]
    for copy in small:
        copy.wait()
    lane = iota((32, 128), 1)
    edge = (lane >= jnp.where(gz == 0, 124, 0)) & (lane < jnp.where(gz == 0, 128, 4))
    packed = jnp.zeros((32, 128), F32)
    for x in range(4):
        mask = m_ref[x].astype(F32)
        seed = mask * s_ref[x].astype(F32)
        ms_ref[0, x] = mask
        ms_ref[1, x] = seed
        xe_ref[32 + x] = seed.astype(BF16)
        xo_ref[32 + x] = seed.astype(BF16)
        for slot, value in ((x, mask), (4 + x, seed)):
            value = jnp.where(edge, value, 0.0)
            packed = packed + (pltpu.roll(value, 8 * slot, 1) if slot else value)
    zs_ref[256:288] = packed.astype(BF16)
    for x in range(4):
        copies[x].wait()
        v_ref[x, 5:37] = jnp.swapaxes(x_ref[x], 0, 1)
    acc = jnp.zeros((256, 128), F32)
    for y in range(16):
        lhs = jnp.concatenate(
            [v_ref[x, 5 + 16 * half + y] for x in range(4) for half in range(2)], axis=0
        )
        acc = acc + jnp.dot(lhs, sels[y], preferred_element_type=F32)
    zs_ref[0:256] = acc.astype(BF16)
    zs_ref[288:320] = jnp.zeros((32, 128), BF16)
    even_face = jnp.where(lax.axis_index("gx") % 2 == 0, 3, 0)
    xe_ref[0:32] = v_ref[even_face, 5:37]
    xo_ref[0:32] = v_ref[3 - even_face, 5:37]


def weights_kernel(
    t_hbm, b_hbm, h_hbm, hb_hbm, w_ref, wp_ref, bias_ref, hw_ref, hbias_ref, hwp_ref, hbp_ref,
    t_ref, b_ref, h_ref, hb_ref, sems,
):
    copies = [
        pltpu.make_async_copy(src, dst, sems.at[i])
        for i, (src, dst) in enumerate(
            ((t_hbm, t_ref), (b_hbm, b_ref), (h_hbm, h_ref), (hb_hbm, hb_ref))
        )
    ]
    for copy in copies:
        copy.start()
    for copy in copies:
        copy.wait()
    for dz in range(3):
        w_ref[32 * dz : 32 * dz + 32] = jnp.concatenate(
            [t_ref[3 * k + dz] for k in range(9)], axis=1
        )
    for k in range(9):
        wp_ref[32 * k : 32 * k + 32] = jnp.concatenate(
            [t_ref[9 * dx + k] for dx in range(3)], axis=1
        )
    across = jnp.broadcast_to(b_ref[...], (32, 32))
    diagonal = iota((32, 32), 0) == iota((32, 32), 1)
    column = jnp.sum(jnp.where(diagonal, across, 0.0), axis=1, keepdims=True)
    bias_ref[...] = jnp.broadcast_to(column, (32, 128))
    same = iota((8, 256), 0) == iota((8, 256), 1) // 32
    few = iota((8, 128), 0)
    hwp = jnp.zeros((8, 32), F32)
    hbp = jnp.zeros((8, 128), F32)
    heads = h_ref[...].astype(F32)
    for c in range(3):
        line = jnp.concatenate([heads[c : c + 1]] * 8, axis=1)
        hw_ref[8 * c : 8 * c + 8] = jnp.where(same, jnp.broadcast_to(line, (8, 256)), 0.0)
        hbias_ref[8 * c : 8 * c + 8] = jnp.full((8, 128), hb_ref[c], F32)
        hwp = jnp.where(few[:, 0:32] == c, jnp.broadcast_to(heads[c : c + 1], (8, 32)), hwp)
        hbp = jnp.where(few == c, hb_ref[c], hbp)
    hwp_ref[...] = hwp
    hbp_ref[...] = hbp


def unpack_ext(packed, slot, gz):
    lane = iota(packed.shape, 1)
    inside = (lane >= jnp.where(gz == 0, 0, 124)) & (lane < jnp.where(gz == 0, 4, 128))
    value = pltpu.roll(packed, (128 - 8 * slot) % 128, 1) if slot else packed
    return jnp.where(inside, value, 0.0)


def yface_kernel(v_ref, zs_ref, zr_ref, ms_ref, pt_ref, ye_ref, yo_ref, block_ref):
    odd = lax.axis_index("gy") % 2
    gz = lax.axis_index("gz")
    lane = iota((256, 128), 1) % 8
    own = pltpu.roll(zs_ref[0:256].astype(F32), jnp.where(gz == 0, 122, 5), 1)
    other = pltpu.roll(zr_ref[0:256].astype(F32), jnp.where(gz == 0, 2, 125), 1)
    own_from = jnp.where(gz == 0, 0, 5)
    other_from = jnp.where(gz == 0, 2, 0)
    packed = jnp.where((lane >= own_from) & (lane < own_from + 2), own, 0.0)
    packed = jnp.where((lane >= other_from) & (lane < other_from + 5), other, packed)
    packed = packed.astype(BF16).reshape(4, 2, 32, 128)
    pt_ref[...] = packed
    zmask = zr_ref[256:288].astype(F32)
    for x in range(4):
        fields = (ms_ref[0, x], ms_ref[1, x], unpack_ext(zmask, x, gz), unpack_ext(zmask, 4 + x, gz))
        for f, value in enumerate(fields):
            block_ref[0, x, 4 * f : 4 * f + 4] = value[28:32]
            block_ref[1, x, 4 * f : 4 * f + 4] = value[0:4]

    def write(dst_ref, up):
        for x in range(4):
            first = 32 if up else 5
            for j in range(5):
                dst_ref[x, 32 * j : 32 * j + 32] = v_ref[x, first + j]
            dst_ref[x, 160:192] = pt_ref[x, 1 if up else 0]
            dst_ref[x, 192:208] = block_ref[0 if up else 1, x].astype(BF16)

    @pl.when(odd == 0)
    def _():
        write(ye_ref, True)
        write(yo_ref, False)

    @pl.when(odd == 1)
    def _():
        write(ye_ref, False)
        write(yo_ref, True)


def xface_kernel(v_in_ref, pt_ref, ye_ref, yo_ref, v_ref, xe_ref, xo_ref):
    odd_x = lax.axis_index("gx") % 2
    odd_y = lax.axis_index("gy") % 2

    gy = lax.axis_index("gy")
    for x in range(4):
        v_ref[x, 5:37] = v_in_ref[x, 5:37]

    def fill(low_ref, high_ref):
        for x in range(4):
            for j in range(5):
                v_ref[x, j] = low_ref[x, 32 * j : 32 * j + 32]
                v_ref[x, 37 + j] = high_ref[x, 32 * j : 32 * j + 32]
            v_ref[x, 42] = low_ref[x, 160:192]
            v_ref[x, 43] = pt_ref[x, 0]
            v_ref[x, 44] = pt_ref[x, 1]
            v_ref[x, 45] = high_ref[x, 160:192]

    @pl.when(odd_y == 0)
    def _():
        fill(yo_ref, ye_ref)

    @pl.when(odd_y == 1)
    def _():
        fill(ye_ref, yo_ref)

    zero = jnp.zeros((32, 128), BF16)

    @pl.when(gy == 0)
    def _():
        for x in range(4):
            for tile in (0, 1, 2, 3, 4, 42):
                v_ref[x, tile] = zero

    @pl.when(gy == 7)
    def _():
        for x in range(4):
            for tile in (37, 38, 39, 40, 41, 45):
                v_ref[x, tile] = zero

    even_face = jnp.where(odd_x == 0, 3, 0)
    for dst_ref, face in ((xe_ref, even_face), (xo_ref, 3 - even_face)):
        dst_ref[0:4] = v_ref[face, 1:5]
        dst_ref[4:13] = v_ref[face, 37:46]


def head(hidden, head_ref, bias_ref):
    logits = jnp.dot(head_ref[...].astype(BF16), hidden, preferred_element_type=F32)
    logits = logits + jnp.tile(bias_ref[...], (1, logits.shape[1] // 128))
    return jax.nn.sigmoid(logits).astype(BF16).astype(F32)


def tile_of(row):
    return row + 5 if row < 36 else row - 35


def spread_matrix(gz):
    k = iota((512, 128), 0) % 8
    to = iota((512, 128), 1)
    goal = jnp.where(gz == 0, (k + 126) % 128, (k + 123) % 128)
    return jnp.where((k >= 1) & (k <= 5) & (to == goal), 1.0, 0.0).astype(BF16)


INTERIOR = tuple(range(1, 31))
OTHERS = (31, 32, 33, 34, 35, 36, 37, 38, 39, 0)


def conv_main(refs, weights, hid_ref, rows):
    lane = iota((32, 128), 1)
    first, last = lane == 0, lane == 127
    w, bias = weights[0][...], weights[2][...]
    for pair in zip(rows[0::2], rows[1::2]):
        cols = []
        for row in pair:
            t = tile_of(row)
            cols.append(
                jnp.concatenate([r[t - 1 : t + 2].reshape(96, 128) for r in refs], axis=0)
            )
        part = jnp.dot(w, jnp.concatenate(cols, axis=1), preferred_element_type=F32)
        for i, row in enumerate(pair):
            one = part[:, 128 * i : 128 * i + 128]
            left = jnp.where(first, 0.0, pltpu.roll(one[0:32], 1, 1))
            right = jnp.where(last, 0.0, pltpu.roll(one[64:96], 127, 1))
            hid = jnp.maximum(one[32:64] + left + right + bias, 0.0)
            hid_ref[32 * row : 32 * row + 32] = hid.astype(BF16)


def conv_packed(refs, weights, spread):
    _, wp_ref, b_ref, _, _, hwp_ref, hbp_ref = weights
    cols = [jnp.concatenate([r[42 + q] for r in refs], axis=0) for q in range(4)]
    part = jnp.dot(wp_ref[...], jnp.concatenate(cols, axis=1), preferred_element_type=F32)
    total = jnp.tile(b_ref[...], (1, 4))
    for dy in range(3):
        for dz in range(3):
            k = 3 * dy + dz
            shift = (-(8 * (dy - 1) + dz - 1)) % 512
            one = part[32 * k : 32 * k + 32]
            total = total + (pltpu.roll(one, shift, 1) if shift else one)
    value = head(jnp.maximum(total, 0.0).astype(BF16), hwp_ref, hbp_ref)
    row = iota((40, 512), 0)
    at = iota((40, 512), 1)
    mine = at // 8 - 16 == jnp.where(row < 36, row, row - 40)
    lhs = jnp.concatenate(
        [jnp.where(mine, jnp.broadcast_to(value[c : c + 1], (40, 512)), 0.0) for c in range(3)],
        axis=0,
    ).astype(BF16)
    return jnp.dot(lhs, spread, preferred_element_type=F32)


def conv_slice(gz, refs, weights, spread, interior_ref, hid_ref):
    conv_main(refs, weights, hid_ref, OTHERS)
    border = conv_packed(refs, weights, spread)

    def hidden(row):
        return (interior_ref if row in INTERIOR else hid_ref)[32 * row : 32 * row + 32]

    hid = jnp.concatenate(
        [jnp.concatenate([hidden(8 * g + i) for i in range(8)], axis=0) for g in range(5)], axis=1
    )
    value = head(hid, weights[3], weights[4])
    fixed = iota((40, 128), 1) == jnp.where(gz == 0, 127, 0)
    out = []
    for c in range(3):
        main = jnp.concatenate(
            [value[8 * c : 8 * c + 8, 128 * g : 128 * g + 128] for g in range(5)], axis=0
        )
        one = border[40 * c : 40 * c + 40]
        out.append((jnp.where(fixed, one, main), jnp.where(fixed, 0.0, one)))
    return out


def inner_rows_kernel(v_ref, w_ref, b_ref, hid_ref):
    for x in (1, 2):
        refs = [v_ref.at[x - 1 + d] for d in range(3)]
        conv_main(refs, (w_ref, None, b_ref), hid_ref.at[x - 1], INTERIOR)


def by_side(even_ref, odd_ref, fill):
    gx = lax.axis_index("gx")

    @pl.when(gx % 2 == 0)
    def _():
        fill(odd_ref, even_ref)

    @pl.when(gx % 2 == 1)
    def _():
        fill(even_ref, odd_ref)


def border_rows_kernel(v_ref, xe_ref, xo_ref, w_ref, b_ref, hid_ref, face_ref, seeds_ref):
    gx = lax.axis_index("gx")

    def fill(low_ref, high_ref):
        face_ref[0, 5:37] = low_ref[0:32]
        face_ref[1, 5:37] = high_ref[0:32]
        seeds_ref[0] = low_ref[32:36]
        seeds_ref[1] = high_ref[32:36]

    by_side(xe_ref, xo_ref, fill)

    @pl.when(gx == 0)
    def _():
        face_ref[0, 5:37] = jnp.zeros((32, 32, 128), BF16)

    @pl.when(gx == 15)
    def _():
        face_ref[1, 5:37] = jnp.zeros((32, 32, 128), BF16)

    for i, refs in enumerate(
        (
            [face_ref.at[0], v_ref.at[0], v_ref.at[1]],
            [v_ref.at[2], v_ref.at[3], face_ref.at[1]],
        )
    ):
        conv_main(refs, (w_ref, None, b_ref), hid_ref.at[i], INTERIOR)


def inner_kernel(
    v_ref, rows_ref, ye_ref, yo_ref, zr_ref, ms_ref, w_ref, wp_ref, b_ref, hw_ref, hb_ref, hwp_ref, hbp_ref,
    a_ref, e_ref, ext_ref, tile_ref, slots_ref, hid_ref, mask_ref, mext_ref,
):
    gy = lax.axis_index("gy")
    odd_y = gy % 2
    gz = lax.axis_index("gz")
    zmask = zr_ref[256:288].astype(F32)
    for x in range(4):
        for f in range(2):
            mask_ref[f, x, 0:32] = ms_ref[f, x]
            mext_ref[f, x, 0:32] = unpack_ext(zmask, 4 * f + x, gz)

    def fill(lower_ref, upper_ref):
        has_lower = jnp.where(gy == 0, 0.0, 1.0)
        has_upper = jnp.where(gy == 7, 0.0, 1.0)
        for x in range(4):
            lower = lower_ref[x, 192:208].astype(F32) * has_lower
            upper = upper_ref[x, 192:208].astype(F32) * has_upper
            for f in range(2):
                mask_ref[f, x, 32:36] = upper[4 * f : 4 * f + 4]
                mask_ref[f, x, 36:40] = lower[4 * f : 4 * f + 4]
                mext_ref[f, x, 32:36] = upper[8 + 4 * f : 12 + 4 * f]
                mext_ref[f, x, 36:40] = lower[8 + 4 * f : 12 + 4 * f]

    @pl.when(odd_y == 0)
    def _():
        fill(yo_ref, ye_ref)

    @pl.when(odd_y == 1)
    def _():
        fill(ye_ref, yo_ref)

    lane = iota((40, 128), 1)
    row = iota((40, 128), 0)

    def shift_y(value):
        return jnp.where(row == 36, 0.0, pltpu.roll(value, 1, 0))

    weights = (w_ref, wp_ref, b_ref, hw_ref, hb_ref, hwp_ref, hbp_ref)
    spread = spread_matrix(gz)
    for x in range(4):
        main, ext = mask_ref[0, x], mext_ref[0, x]
        rolled, rolled_ext = pltpu.roll(main, 1, 1), pltpu.roll(ext, 1, 1)
        z_main = main * jnp.where(lane == 0, rolled_ext, rolled)
        z_ext = ext * jnp.where(lane == 0, rolled, rolled_ext)
        y_main, y_ext = main * shift_y(main), ext * shift_y(ext)
        x_main = main * mask_ref[0, x - 1] if x else main
        x_ext = ext * mext_ref[0, x - 1] if x else ext
        keep = ((x_main, x_ext), (y_main, y_ext), (z_main, z_ext))
        if 0 < x < 3:
            refs = [v_ref.at[x - 1 + d] for d in range(3)]
            a = conv_slice(gz, refs, weights, spread, rows_ref.at[x - 1], hid_ref.at[x - 1])
            for f in range(3):
                a_ref[f, x - 1] = a[f][0][0:32].astype(BF16)
                e_ref[x, f] = a[f][0] * keep[f][0]
                ext_ref[x, f] = a[f][1] * keep[f][1]
                tile_ref[x - 1, f] = e_ref[x, f].astype(BF16)
        else:
            for f in range(3):
                e_ref[x, f] = keep[f][0]
                ext_ref[x, f] = keep[f][1]
        e_ref[x, 3] = mask_ref[1, x]
        ext_ref[x, 3] = mext_ref[1, x]
    for way, order in enumerate(((2, 1), (1, 2))):
        packed = jnp.zeros((40, 128), F32)
        for j, x in enumerate(order):
            for f in range(4):
                packed = packed + pltpu.roll(ext_ref[x, f], 8 * (4 * (j + 1) + f), 1)
        slots_ref[way] = packed


def border_kernel(
    v_ref, face_ref, rows_ref, xe_ref, xo_ref, e_in, ext_in, tile_ref, slots_ref, w_ref, wp_ref, b_ref, hw_ref, hb_ref, hwp_ref, hbp_ref,
    a_ref, e_ref, ext_ref, se_ref, so_ref, side_ref, hid_ref,
):
    gx = lax.axis_index("gx")
    odd_x = gx % 2
    gz = lax.axis_index("gz")

    def fill(low_ref, high_ref):
        for i, ref in enumerate((low_ref, high_ref)):
            side_ref[i, 0] = jnp.zeros((32, 128), BF16)
            side_ref[i, 1:5] = ref[0:4]
            side_ref[i, 37:46] = ref[4:13]

    by_side(xe_ref, xo_ref, fill)
    for i, end in ((0, 0), (1, 15)):
        for at in (5, 6, 35, 36):
            side_ref[i, at] = face_ref[i, at]

        @pl.when(gx == end)
        def _():
            side_ref[i, 0:5] = jnp.zeros((5, 32, 128), BF16)
            side_ref[i, 37:46] = jnp.zeros((9, 32, 128), BF16)

    weights = (w_ref, wp_ref, b_ref, hw_ref, hb_ref, hwp_ref, hbp_ref)
    spread = spread_matrix(gz)
    for x, refs in (
        (0, [side_ref.at[0], v_ref.at[0], v_ref.at[1]]),
        (3, [v_ref.at[2], v_ref.at[3], side_ref.at[1]]),
    ):
        a = conv_slice(gz, refs, weights, spread, rows_ref.at[x // 3], hid_ref.at[x // 3])
        for f in range(3):
            a_ref[f, x // 3] = a[f][0][0:32].astype(BF16)
            e_ref[x // 3, f] = a[f][0] * e_in[x, f]
            ext_ref[x // 3, f] = a[f][1] * ext_in[x, f]

    def send(dst_ref, way, order):
        packed = slots_ref[way]
        for f in range(4):
            x = order[0]
            value = ext_ref[x // 3, f] if f < 3 else ext_in[x, 3]
            packed = packed + (pltpu.roll(value, 8 * f, 1) if f else value)
        for f in range(3):
            dst_ref[f] = e_ref[order[0] // 3, f].astype(BF16)
            dst_ref[3 + f] = tile_ref[order[1] - 1, f]
            dst_ref[6 + f] = tile_ref[order[2] - 1, f]
            dst_ref[11, 8 * f : 8 * f + 8] = e_in[order[f], 3, 32:40].astype(BF16)
        dst_ref[9] = e_ref[order[3] // 3, 0].astype(BF16)
        dst_ref[10] = packed.astype(BF16)

    up, down = (0, (3, 2, 1, 0)), (1, (0, 1, 2, 3))

    @pl.when(odd_x == 0)
    def _():
        send(se_ref, *up)
        send(so_ref, *down)

    @pl.when(odd_x == 1)
    def _():
        send(se_ref, *down)
        send(so_ref, *up)


def rounds_kernel(
    ai_ref, ab_ref, ei_ref, exti_ref, eb_ref, extb_ref, seeds_ref, re_ref, ro_ref, ms_ref,
    a_hbm, out_hbm, all_ref, s_ref, out_ref, sems,
):
    gx = lax.axis_index("gx")
    gz = lax.axis_index("gz")
    copies = [
        pltpu.make_async_copy(ai_ref, a_hbm.at[:, 1:3], sems.at[4]),
        pltpu.make_async_copy(ab_ref.at[:, 0:1], a_hbm.at[:, 0:1], sems.at[5]),
        pltpu.make_async_copy(ab_ref.at[:, 1:2], a_hbm.at[:, 3:4], sems.at[6]),
    ]
    for copy in copies:
        copy.start()
    has_low = jnp.where(gx == 0, 0.0, 1.0)
    has_high = jnp.where(gx == 15, 0.0, 1.0)
    zero = jnp.zeros((40, 128), F32)

    def place(src_ref, places, has):
        packed = src_ref[10].astype(F32) * has
        high = places[0] == 8
        for j, at in enumerate(places):
            seeds = seeds_ref[1, j] if high else seeds_ref[0, 3 - j]
            s_ref[0, at, 0, 0:32] = seeds.astype(F32) * has / 15.0
            if j == 3:
                s_ref[0, at, 0, 32:40] = zero[0:8]
                s_ref[0, at, 1] = zero
                all_ref[at % 8 if high else 4 + at, 0, 0] = src_ref[9].astype(F32) * has
                all_ref[at % 8 if high else 4 + at, 0, 1] = zero
                continue
            s_ref[0, at, 0, 32:40] = src_ref[11, 8 * j : 8 * j + 8].astype(F32) * has / 15.0
            s_ref[0, at, 1] = unpack_ext(packed, 4 * j + 3, gz) / 15.0
            for f in range(3):
                where = at % 8 if high else 4 + at
                all_ref[where, f, 0] = src_ref[3 * j + f].astype(F32) * has
                all_ref[where, f, 1] = unpack_ext(packed, 4 * j + f, gz)

    def fill(low_ref, high_ref):
        place(low_ref, (3, 2, 1, 0), has_low)
        place(high_ref, (8, 9, 10, 11), has_high)

    by_side(re_ref, ro_ref, fill)

    for x in range(4):
        s_ref[0, 4 + x, 0] = ei_ref[x, 3] / 15.0
        s_ref[0, 4 + x, 1] = exti_ref[x, 3] / 15.0

    def edge(at, f, i):
        if at < 4 or at > 7:
            return all_ref[4 + at if at < 4 else at - 8, f, i]
        if at in (5, 6):
            return (ei_ref, exti_ref)[i][at - 4, f]
        return (eb_ref, extb_ref)[i][(at - 4) // 3, f]

    lane = iota((40, 128), 1)

    def down(pair):
        a, b = pltpu.roll(pair[0], 1, 1), pltpu.roll(pair[1], 1, 1)
        return jnp.where(lane == 0, b, a), jnp.where(lane == 0, a, b)

    def up(pair):
        a, b = pltpu.roll(pair[0], 127, 1), pltpu.roll(pair[1], 127, 1)
        return jnp.where(lane == 127, b, a), jnp.where(lane == 127, a, b)

    for r in range(ROUNDS):
        src, dst = r % 2, (r + 1) % 2
        for x in range(r + 1, 11 - r):
            here = (s_ref[src, x, 0], s_ref[src, x, 1])
            ez = (edge(x, 2, 0), edge(x, 2, 1))
            z_low = down(here)
            z_high = up(tuple(jnp.minimum(here[i], ez[i]) for i in range(2)))
            for i in range(1 if r == ROUNDS - 1 else 2):
                ey = edge(x, 1, i)
                value = here[i]
                value = jnp.maximum(value, jnp.minimum(s_ref[src, x - 1, i], edge(x, 0, i)))
                value = jnp.maximum(value, jnp.minimum(s_ref[src, x + 1, i], edge(x + 1, 0, i)))
                value = jnp.maximum(value, jnp.minimum(pltpu.roll(here[i], 1, 0), ey))
                value = jnp.maximum(value, pltpu.roll(jnp.minimum(here[i], ey), 39, 0))
                value = jnp.maximum(value, jnp.minimum(z_low[i], ez[i]))
                value = jnp.maximum(value, z_high[i])
                if r < ROUNDS - 1:
                    s_ref[dst, x, i] = value
                else:
                    out_ref[x - 4] = value[0:32] * ms_ref[0, x - 4]
                    copies.append(
                        pltpu.make_async_copy(out_ref.at[x - 4], out_hbm.at[x - 4], sems.at[x - 4])
                    )
                    copies[-1].start()
    for copy in copies:
        copy.wait()


def stay(value):
    return pltpu.with_memory_space_constraint(value, pltpu.HBM)


def call(kernel, shapes, args, scratch=(), specs=None, out_specs=None):
    return pl.pallas_call(
        kernel,
        out_shape=[jax.ShapeDtypeStruct(s, d) for s, d in shapes],
        in_specs=specs or [VMEM] * len(args),
        out_specs=out_specs or [VMEM] * len(shapes),
        scratch_shapes=[pltpu.VMEM(*s) if isinstance(s[0], tuple) else s[0](*s[1:]) for s in scratch],
        compiler_params=PARAMS,
    )(*args)


def body(features, conv_weight, conv_bias, head_weight, head_bias, mask, seeds):
    v, zs, ms, fe, fo = call(
        pack_kernel,
        [
            ((4, 46, 32, 128), BF16),
            ((320, 128), BF16),
            ((2, 4, 32, 128), F32),
            ((36, 32, 128), BF16),
            ((36, 32, 128), BF16),
        ],
        tuple(stay(a) for a in (features, mask, seeds)),
        scratch=[
            ((4, 32, 32, 128), BF16),
            ((4, 32, 128), jnp.int32),
            ((4, 32, 128), jnp.int32),
            (pltpu.SemaphoreType.DMA, (6,)),
        ],
        specs=[HBM] * 3,
    )
    zr = lax.ppermute(zs, "gz", [(0, 1), (1, 0)])
    even_x, odd_x = swaps_gx()
    axes = ("gx", "gy")
    fo = lax.ppermute(fo, axes, odd_x)
    fe = lax.ppermute(fe, axes, even_x)
    pt, ye, yo = call(
        yface_kernel,
        [((4, 2, 32, 128), BF16), ((4, 208, 128), BF16), ((4, 208, 128), BF16)],
        (v, zs, zr, ms),
        scratch=[((2, 4, 16, 128), F32)],
    )
    ye, yo, vy, conv_weight, conv_bias, head_weight, head_bias = lax.optimization_barrier(
        (ye, yo, v, conv_weight, conv_bias, head_weight, head_bias)
    )
    taps = jnp.transpose(conv_weight, (2, 3, 4, 0, 1)).reshape(27, 32, 32)
    forms = call(
        weights_kernel,
        [
            ((96, 288), BF16),
            ((288, 96), BF16),
            ((32, 128), F32),
            ((24, 256), F32),
            ((24, 128), F32),
            ((8, 32), F32),
            ((8, 128), F32),
        ],
        tuple(stay(a) for a in (taps, conv_bias.reshape(1, 32), head_weight, head_bias)),
        scratch=[
            ((27, 32, 32), BF16),
            ((1, 32), F32),
            ((3, 32), BF16),
            (pltpu.SMEM, (3,), F32),
            (pltpu.SemaphoreType.DMA, (4,)),
        ],
        specs=[HBM] * 4,
    )
    weights = tuple(forms)
    rows_shape = [((2, 1280, 128), BF16)]
    (inner_rows,) = call(inner_rows_kernel, rows_shape, (vy, weights[0], weights[2]))
    even, odd = swaps(lax.axis_size("gy"))
    yo = lax.ppermute(yo, "gy", odd)
    ye = lax.ppermute(ye, "gy", even)
    ye, yo, inner_rows = lax.optimization_barrier((ye, yo, inner_rows))
    v, xe, xo = call(
        xface_kernel,
        [((4, 46, 32, 128), BF16), ((13, 32, 128), BF16), ((13, 32, 128), BF16)],
        (v, pt, ye, yo),
    )
    xe, xo, v, fe, fo = lax.optimization_barrier((xe, xo, v, fe, fo))
    xo = lax.ppermute(xo, axes, odd_x)
    xe = lax.ppermute(xe, axes, even_x)
    inner_a, e, ext, tiles, slots = call(
        inner_kernel,
        [
            ((3, 2, 32, 128), BF16),
            ((4, 4, 40, 128), F32),
            ((4, 4, 40, 128), F32),
            ((2, 3, 40, 128), BF16),
            ((2, 40, 128), F32),
        ],
        (v, inner_rows, ye, yo, zr, ms) + weights,
        scratch=[((2, 1280, 128), BF16), ((2, 4, 40, 128), F32), ((2, 4, 40, 128), F32)],
    )
    border_rows, faces, side_seeds = call(
        border_rows_kernel,
        rows_shape + [((2, 46, 32, 128), BF16), ((2, 4, 32, 128), BF16)],
        (v, fe, fo, weights[0], weights[2]),
    )
    xe, xo, e, ext, border_rows, faces = lax.optimization_barrier(
        (xe, xo, e, ext, border_rows, faces)
    )
    border_a, border_e, border_ext, se, so = call(
        border_kernel,
        [
            ((3, 2, 32, 128), BF16),
            ((2, 3, 40, 128), F32),
            ((2, 3, 40, 128), F32),
            ((12, 40, 128), BF16),
            ((12, 40, 128), BF16),
        ],
        (v, faces, border_rows, xe, xo, e, ext, tiles, slots) + weights,
        scratch=[((2, 46, 32, 128), BF16), ((2, 1280, 128), BF16)],
    )
    so = lax.ppermute(so, axes, odd_x)
    se = lax.ppermute(se, axes, even_x)
    affinity, strength = call(
        rounds_kernel,
        [((3, 4, 32, 128), BF16), ((4, 32, 128), F32)],
        (inner_a, border_a, e, ext, border_e, border_ext, side_seeds, se, so, ms),
        scratch=[
            ((8, 3, 2, 40, 128), F32),
            ((2, 12, 2, 40, 128), F32),
            ((4, 32, 128), F32),
            (pltpu.SemaphoreType.DMA, (7,)),
        ],
        out_specs=[HBM, HBM],
    )
    return (affinity, strength)


def solution(mesh):
    in_specs = (
        P(None, "gx", "gy", "gz"),
        P(),
        P(),
        P(),
        P(),
        P("gx", "gy", "gz"),
        P("gx", "gy", "gz"),
    )
    out_specs = (P(None, "gx", "gy", "gz"), P("gx", "gy", "gz"))
    return jax.shard_map(body, mesh=mesh, in_specs=in_specs, out_specs=out_specs, check_vma=False)
```

```python
import jax
import jax.numpy as jnp
from jax import lax
from jax.experimental import pallas as pl
from jax.experimental.pallas import tpu as pltpu
from jax.sharding import PartitionSpec as P

ROUNDS = 4
F32 = jnp.float32
BF16 = jnp.bfloat16
VMEM = pl.BlockSpec(memory_space=pltpu.VMEM)
HBM = pl.BlockSpec(memory_space=pltpu.HBM)
PARAMS = pltpu.CompilerParams(vmem_limit_bytes=12 * 2**20)


def swaps(axis):
    nx, ny = lax.axis_size("gx"), lax.axis_size("gy")

    def partner(x, y, first):
        at, count = (x, nx) if axis == "gx" else (y, ny)
        other = at + 1 if at % 2 == first else at - 1
        inside = 0 <= other < count
        if axis == "gx":
            return (other, y) if inside else (x, y ^ 1)
        return (x, other) if inside else (x ^ 1, y)

    def pairs(first):
        out = []
        for x in range(nx):
            for y in range(ny):
                px, py = partner(x, y, first)
                out.append((x * ny + y, px * ny + py))
        return out

    return pairs(0), pairs(1)


def iota(shape, dim):
    return lax.broadcasted_iota(jnp.int32, shape, dim)


def pack_kernel(x_hbm, m_hbm, s_hbm, v_ref, zs_ref, ms_ref, xe_ref, xo_ref, x_ref, m_ref, s_ref, sems):
    gz = lax.axis_index("gz")
    copies = [pltpu.make_async_copy(x_hbm.at[:, x], x_ref.at[x], sems.at[x]) for x in range(4)]
    small = [
        pltpu.make_async_copy(m_hbm, m_ref, sems.at[4]),
        pltpu.make_async_copy(s_hbm, s_ref, sems.at[5]),
    ]
    for copy in small + copies:
        copy.start()
    lane = iota((128, 128), 1)
    row = iota((128, 128), 0)
    base = jnp.where(gz == 0, 120, 0)
    hit = row == base + lane % 8
    sels = [jnp.where(hit & (lane // 8 == y), 1.0, 0.0).astype(BF16) for y in range(16)]
    for copy in small:
        copy.wait()
    lane = iota((32, 128), 1)
    edge = (lane >= jnp.where(gz == 0, 124, 0)) & (lane < jnp.where(gz == 0, 128, 4))
    packed = jnp.zeros((32, 128), F32)
    for x in range(4):
        mask = m_ref[x].astype(F32)
        seed = mask * s_ref[x].astype(F32)
        ms_ref[0, x] = mask
        ms_ref[1, x] = seed
        xe_ref[32 + x] = seed.astype(BF16)
        xo_ref[32 + x] = seed.astype(BF16)
        for slot, value in ((x, mask), (4 + x, seed)):
            value = jnp.where(edge, value, 0.0)
            packed = packed + (pltpu.roll(value, 8 * slot, 1) if slot else value)
    zs_ref[256:288] = packed.astype(BF16)
    for x in range(4):
        copies[x].wait()
        v_ref[x, 5:37] = jnp.swapaxes(x_ref[x], 0, 1)
    lhs = jnp.concatenate(
        [
            jnp.concatenate(
                [v_ref[x, 5 + 16 * half + y] for x in range(4) for half in range(2)], axis=0
            )
            for y in range(16)
        ],
        axis=1,
    )
    edges = jnp.dot(lhs, jnp.concatenate(sels, axis=0), preferred_element_type=F32)
    zs_ref[0:256] = edges.astype(BF16)
    zs_ref[288:320] = jnp.zeros((32, 128), BF16)
    even_face = jnp.where(lax.axis_index("gx") % 2 == 0, 3, 0)
    xe_ref[0:32] = v_ref[even_face, 5:37]
    xo_ref[0:32] = v_ref[3 - even_face, 5:37]


def weights_kernel(
    t_hbm, b_hbm, h_hbm, hb_hbm, w_ref, wp_ref, bias_ref, hw_ref, hbias_ref, hwp_ref, hbp_ref,
    t_ref, b_ref, h_ref, hb_ref, sems,
):
    copies = [
        pltpu.make_async_copy(src, dst, sems.at[i])
        for i, (src, dst) in enumerate(
            ((t_hbm, t_ref), (b_hbm, b_ref), (h_hbm, h_ref), (hb_hbm, hb_ref))
        )
    ]
    for copy in copies:
        copy.start()
    for copy in copies:
        copy.wait()
    for dz in range(3):
        w_ref[32 * dz : 32 * dz + 32] = jnp.concatenate(
            [t_ref[3 * k + dz] for k in range(9)], axis=1
        )
    for k in range(9):
        wp_ref[32 * k : 32 * k + 32] = jnp.concatenate(
            [t_ref[9 * dx + k] for dx in range(3)], axis=1
        )
    across = jnp.broadcast_to(b_ref[...], (32, 32))
    diagonal = iota((32, 32), 0) == iota((32, 32), 1)
    column = jnp.sum(jnp.where(diagonal, across, 0.0), axis=1, keepdims=True)
    bias_ref[...] = jnp.broadcast_to(column, (32, 128))
    same = iota((8, 256), 0) == iota((8, 256), 1) // 32
    few = iota((8, 128), 0)
    hwp = jnp.zeros((8, 32), F32)
    hbp = jnp.zeros((8, 128), F32)
    heads = h_ref[...].astype(F32)
    for c in range(3):
        line = jnp.concatenate([heads[c : c + 1]] * 8, axis=1)
        hw_ref[8 * c : 8 * c + 8] = jnp.where(same, jnp.broadcast_to(line, (8, 256)), 0.0)
        hbias_ref[8 * c : 8 * c + 8] = jnp.full((8, 128), hb_ref[c], F32)
        hwp = jnp.where(few[:, 0:32] == c, jnp.broadcast_to(heads[c : c + 1], (8, 32)), hwp)
        hbp = jnp.where(few == c, hb_ref[c], hbp)
    hwp_ref[...] = hwp
    hbp_ref[...] = hbp


def unpack_ext(packed, slot, gz):
    lane = iota(packed.shape, 1)
    inside = (lane >= jnp.where(gz == 0, 0, 124)) & (lane < jnp.where(gz == 0, 4, 128))
    value = pltpu.roll(packed, (128 - 8 * slot) % 128, 1) if slot else packed
    return jnp.where(inside, value, 0.0)


def yface_kernel(v_ref, zs_ref, zr_ref, ms_ref, pt_ref, ye_ref, yo_ref, block_ref):
    odd = lax.axis_index("gy") % 2
    gz = lax.axis_index("gz")
    lane = iota((256, 128), 1) % 8
    own = pltpu.roll(zs_ref[0:256].astype(F32), jnp.where(gz == 0, 122, 5), 1)
    other = pltpu.roll(zr_ref[0:256].astype(F32), jnp.where(gz == 0, 2, 125), 1)
    own_from = jnp.where(gz == 0, 0, 5)
    other_from = jnp.where(gz == 0, 2, 0)
    packed = jnp.where((lane >= own_from) & (lane < own_from + 2), own, 0.0)
    packed = jnp.where((lane >= other_from) & (lane < other_from + 5), other, packed)
    packed = packed.astype(BF16).reshape(4, 2, 32, 128)
    pt_ref[...] = packed
    zmask = zr_ref[256:288].astype(F32)
    for x in range(4):
        fields = (ms_ref[0, x], ms_ref[1, x], unpack_ext(zmask, x, gz), unpack_ext(zmask, 4 + x, gz))
        for f, value in enumerate(fields):
            block_ref[0, x, 4 * f : 4 * f + 4] = value[28:32]
            block_ref[1, x, 4 * f : 4 * f + 4] = value[0:4]

    def write(dst_ref, up):
        for x in range(4):
            first = 32 if up else 5
            for j in range(5):
                dst_ref[x, 32 * j : 32 * j + 32] = v_ref[x, first + j]
            dst_ref[x, 160:192] = pt_ref[x, 1 if up else 0]
            dst_ref[x, 192:208] = block_ref[0 if up else 1, x].astype(BF16)

    @pl.when(odd == 0)
    def _():
        write(ye_ref, True)
        write(yo_ref, False)

    @pl.when(odd == 1)
    def _():
        write(ye_ref, False)
        write(yo_ref, True)


def xface_kernel(v_in_ref, pt_ref, ye_ref, yo_ref, v_ref, xe_ref, xo_ref):
    odd_x = lax.axis_index("gx") % 2
    odd_y = lax.axis_index("gy") % 2

    gy = lax.axis_index("gy")
    for x in range(4):
        v_ref[x, 5:37] = v_in_ref[x, 5:37]

    def fill(low_ref, high_ref):
        for x in range(4):
            for j in range(5):
                v_ref[x, j] = low_ref[x, 32 * j : 32 * j + 32]
                v_ref[x, 37 + j] = high_ref[x, 32 * j : 32 * j + 32]
            v_ref[x, 42] = low_ref[x, 160:192]
            v_ref[x, 43] = pt_ref[x, 0]
            v_ref[x, 44] = pt_ref[x, 1]
            v_ref[x, 45] = high_ref[x, 160:192]

    @pl.when(odd_y == 0)
    def _():
        fill(yo_ref, ye_ref)

    @pl.when(odd_y == 1)
    def _():
        fill(ye_ref, yo_ref)

    zero = jnp.zeros((32, 128), BF16)

    @pl.when(gy == 0)
    def _():
        for x in range(4):
            for tile in (0, 1, 2, 3, 4, 42):
                v_ref[x, tile] = zero

    @pl.when(gy == 7)
    def _():
        for x in range(4):
            for tile in (37, 38, 39, 40, 41, 45):
                v_ref[x, tile] = zero

    even_face = jnp.where(odd_x == 0, 3, 0)
    for dst_ref, face in ((xe_ref, even_face), (xo_ref, 3 - even_face)):
        dst_ref[0:4] = v_ref[face, 1:5]
        dst_ref[4:13] = v_ref[face, 37:46]


def head(hidden, head_ref, bias_ref):
    logits = jnp.dot(head_ref[...].astype(BF16), hidden, preferred_element_type=F32)
    logits = logits + jnp.tile(bias_ref[...], (1, logits.shape[1] // 128))
    return jax.nn.sigmoid(logits).astype(BF16).astype(F32)


def tile_of(row):
    return row + 5 if row < 36 else row - 35


def spread_matrix(gz):
    k = iota((512, 128), 0) % 8
    to = iota((512, 128), 1)
    goal = jnp.where(gz == 0, (k + 126) % 128, (k + 123) % 128)
    return jnp.where((k >= 1) & (k <= 5) & (to == goal), 1.0, 0.0).astype(BF16)


INTERIOR = tuple(range(1, 31))
OTHERS = (31, 32, 33, 34, 35, 36, 37, 38, 39, 0)


def conv_main(refs, weights, hid_ref, rows):
    lane = iota((32, 128), 1)
    first, last = lane == 0, lane == 127
    w, bias = weights[0][...], weights[2][...]
    for pair in zip(rows[0::2], rows[1::2]):
        cols = []
        for row in pair:
            t = tile_of(row)
            cols.append(
                jnp.concatenate([r[t - 1 : t + 2].reshape(96, 128) for r in refs], axis=0)
            )
        part = jnp.dot(w, jnp.concatenate(cols, axis=1), preferred_element_type=F32)
        for i, row in enumerate(pair):
            one = part[:, 128 * i : 128 * i + 128]
            left = jnp.where(first, 0.0, pltpu.roll(one[0:32], 1, 1))
            right = jnp.where(last, 0.0, pltpu.roll(one[64:96], 127, 1))
            hid = jnp.maximum(one[32:64] + left + right + bias, 0.0)
            hid_ref[32 * row : 32 * row + 32] = hid.astype(BF16)


def conv_packed(refs, weights, spread):
    _, wp_ref, b_ref, _, _, hwp_ref, hbp_ref = weights
    cols = [jnp.concatenate([r[42 + q] for r in refs], axis=0) for q in range(4)]
    part = jnp.dot(wp_ref[...], jnp.concatenate(cols, axis=1), preferred_element_type=F32)
    total = jnp.tile(b_ref[...], (1, 4))
    for dy in range(3):
        for dz in range(3):
            k = 3 * dy + dz
            shift = (-(8 * (dy - 1) + dz - 1)) % 512
            one = part[32 * k : 32 * k + 32]
            total = total + (pltpu.roll(one, shift, 1) if shift else one)
    value = head(jnp.maximum(total, 0.0).astype(BF16), hwp_ref, hbp_ref)
    row = iota((40, 512), 0)
    at = iota((40, 512), 1)
    mine = at // 8 - 16 == jnp.where(row < 36, row, row - 40)
    lhs = jnp.concatenate(
        [jnp.where(mine, jnp.broadcast_to(value[c : c + 1], (40, 512)), 0.0) for c in range(3)],
        axis=0,
    ).astype(BF16)
    return jnp.dot(lhs, spread, preferred_element_type=F32)


def conv_slice(gz, refs, weights, spread, interior_ref, hid_ref):
    conv_main(refs, weights, hid_ref, OTHERS)
    border = conv_packed(refs, weights, spread)

    def hidden(row):
        return (interior_ref if row in INTERIOR else hid_ref)[32 * row : 32 * row + 32]

    hid = jnp.concatenate(
        [jnp.concatenate([hidden(8 * g + i) for i in range(8)], axis=0) for g in range(5)], axis=1
    )
    value = head(hid, weights[3], weights[4])
    fixed = iota((40, 128), 1) == jnp.where(gz == 0, 127, 0)
    out = []
    for c in range(3):
        main = jnp.concatenate(
            [value[8 * c : 8 * c + 8, 128 * g : 128 * g + 128] for g in range(5)], axis=0
        )
        one = border[40 * c : 40 * c + 40]
        out.append((jnp.where(fixed, one, main), jnp.where(fixed, 0.0, one)))
    return out


def inner_rows_kernel(v_ref, w_ref, b_ref, hid_ref):
    for x in (1, 2):
        refs = [v_ref.at[x - 1 + d] for d in range(3)]
        conv_main(refs, (w_ref, None, b_ref), hid_ref.at[x - 1], INTERIOR)


def by_side(even_ref, odd_ref, fill):
    gx = lax.axis_index("gx")

    @pl.when(gx % 2 == 0)
    def _():
        fill(odd_ref, even_ref)

    @pl.when(gx % 2 == 1)
    def _():
        fill(even_ref, odd_ref)


def border_rows_kernel(v_ref, xe_ref, xo_ref, w_ref, b_ref, hid_ref, face_ref, seeds_ref):
    gx = lax.axis_index("gx")

    def fill(low_ref, high_ref):
        face_ref[0, 5:37] = low_ref[0:32]
        face_ref[1, 5:37] = high_ref[0:32]
        seeds_ref[0] = low_ref[32:36].astype(F32) / 15.0
        seeds_ref[1] = high_ref[32:36].astype(F32) / 15.0

    by_side(xe_ref, xo_ref, fill)

    @pl.when(gx == 0)
    def _():
        face_ref[0, 5:37] = jnp.zeros((32, 32, 128), BF16)

    @pl.when(gx == 15)
    def _():
        face_ref[1, 5:37] = jnp.zeros((32, 32, 128), BF16)

    for i, refs in enumerate(
        (
            [face_ref.at[0], v_ref.at[0], v_ref.at[1]],
            [v_ref.at[2], v_ref.at[3], face_ref.at[1]],
        )
    ):
        conv_main(refs, (w_ref, None, b_ref), hid_ref.at[i], INTERIOR)


def inner_kernel(
    v_ref, rows_ref, ye_ref, yo_ref, zr_ref, ms_ref, w_ref, wp_ref, b_ref, hw_ref, hb_ref, hwp_ref, hbp_ref,
    a_ref, e_ref, ext_ref, tile_ref, slots_ref, start_ref, hid_ref, mask_ref, mext_ref,
):
    gy = lax.axis_index("gy")
    odd_y = gy % 2
    gz = lax.axis_index("gz")
    zmask = zr_ref[256:288].astype(F32)
    for x in range(4):
        for f in range(2):
            mask_ref[f, x, 0:32] = ms_ref[f, x]
            mext_ref[f, x, 0:32] = unpack_ext(zmask, 4 * f + x, gz)

    def fill(lower_ref, upper_ref):
        has_lower = jnp.where(gy == 0, 0.0, 1.0)
        has_upper = jnp.where(gy == 7, 0.0, 1.0)
        for x in range(4):
            lower = lower_ref[x, 192:208].astype(F32) * has_lower
            upper = upper_ref[x, 192:208].astype(F32) * has_upper
            for f in range(2):
                mask_ref[f, x, 32:36] = upper[4 * f : 4 * f + 4]
                mask_ref[f, x, 36:40] = lower[4 * f : 4 * f + 4]
                mext_ref[f, x, 32:36] = upper[8 + 4 * f : 12 + 4 * f]
                mext_ref[f, x, 36:40] = lower[8 + 4 * f : 12 + 4 * f]

    @pl.when(odd_y == 0)
    def _():
        fill(yo_ref, ye_ref)

    @pl.when(odd_y == 1)
    def _():
        fill(ye_ref, yo_ref)

    lane = iota((40, 128), 1)
    row = iota((40, 128), 0)

    def shift_y(value):
        return jnp.where(row == 36, 0.0, pltpu.roll(value, 1, 0))

    weights = (w_ref, wp_ref, b_ref, hw_ref, hb_ref, hwp_ref, hbp_ref)
    spread = spread_matrix(gz)
    for x in range(4):
        main, ext = mask_ref[0, x], mext_ref[0, x]
        rolled, rolled_ext = pltpu.roll(main, 1, 1), pltpu.roll(ext, 1, 1)
        z_main = main * jnp.where(lane == 0, rolled_ext, rolled)
        z_ext = ext * jnp.where(lane == 0, rolled, rolled_ext)
        y_main, y_ext = main * shift_y(main), ext * shift_y(ext)
        x_main = main * mask_ref[0, x - 1] if x else main
        x_ext = ext * mext_ref[0, x - 1] if x else ext
        keep = ((x_main, x_ext), (y_main, y_ext), (z_main, z_ext))
        if 0 < x < 3:
            refs = [v_ref.at[x - 1 + d] for d in range(3)]
            a = conv_slice(gz, refs, weights, spread, rows_ref.at[x - 1], hid_ref.at[x - 1])
            for f in range(3):
                a_ref[f, x - 1] = a[f][0][0:32].astype(BF16)
                e_ref[x, f] = a[f][0] * keep[f][0]
                ext_ref[x, f] = a[f][1] * keep[f][1]
                tile_ref[x - 1, f] = e_ref[x, f].astype(BF16)
        else:
            for f in range(3):
                e_ref[x, f] = keep[f][0]
                ext_ref[x, f] = keep[f][1]
        e_ref[x, 3] = mask_ref[1, x]
        ext_ref[x, 3] = mext_ref[1, x]
        start_ref[x, 0] = mask_ref[1, x] / 15.0
        start_ref[x, 1] = mext_ref[1, x] / 15.0
    for way, order in enumerate(((2, 1), (1, 2))):
        packed = jnp.zeros((40, 128), F32)
        for j, x in enumerate(order):
            for f in range(4):
                packed = packed + pltpu.roll(ext_ref[x, f], 8 * (4 * (j + 1) + f), 1)
        slots_ref[way] = packed


def border_kernel(
    v_ref, face_ref, rows_ref, xe_ref, xo_ref, e_in, ext_in, tile_ref, slots_ref, w_ref, wp_ref, b_ref, hw_ref, hb_ref, hwp_ref, hbp_ref,
    a_ref, e_ref, ext_ref, se_ref, so_ref, side_ref, hid_ref,
):
    gx = lax.axis_index("gx")
    odd_x = gx % 2
    gz = lax.axis_index("gz")

    def fill(low_ref, high_ref):
        for i, ref in enumerate((low_ref, high_ref)):
            side_ref[i, 0] = jnp.zeros((32, 128), BF16)
            side_ref[i, 1:5] = ref[0:4]
            side_ref[i, 37:46] = ref[4:13]

    by_side(xe_ref, xo_ref, fill)
    for i, end in ((0, 0), (1, 15)):
        for at in (5, 6, 35, 36):
            side_ref[i, at] = face_ref[i, at]

        @pl.when(gx == end)
        def _():
            side_ref[i, 0:5] = jnp.zeros((5, 32, 128), BF16)
            side_ref[i, 37:46] = jnp.zeros((9, 32, 128), BF16)

    weights = (w_ref, wp_ref, b_ref, hw_ref, hb_ref, hwp_ref, hbp_ref)
    spread = spread_matrix(gz)
    for x, refs in (
        (0, [side_ref.at[0], v_ref.at[0], v_ref.at[1]]),
        (3, [v_ref.at[2], v_ref.at[3], side_ref.at[1]]),
    ):
        a = conv_slice(gz, refs, weights, spread, rows_ref.at[x // 3], hid_ref.at[x // 3])
        for f in range(3):
            a_ref[f, x // 3] = a[f][0][0:32].astype(BF16)
            e_ref[x // 3, f] = a[f][0] * e_in[x, f]
            ext_ref[x // 3, f] = a[f][1] * ext_in[x, f]

    def send(dst_ref, way, order):
        packed = slots_ref[way]
        for f in range(4):
            x = order[0]
            value = ext_ref[x // 3, f] if f < 3 else ext_in[x, 3]
            packed = packed + (pltpu.roll(value, 8 * f, 1) if f else value)
        for f in range(3):
            dst_ref[f] = e_ref[order[0] // 3, f].astype(BF16)
            dst_ref[3 + f] = tile_ref[order[1] - 1, f]
            dst_ref[6 + f] = tile_ref[order[2] - 1, f]
            dst_ref[11, 8 * f : 8 * f + 8] = e_in[order[f], 3, 32:40].astype(BF16)
        dst_ref[9] = e_ref[order[3] // 3, 0].astype(BF16)
        dst_ref[10] = packed.astype(BF16)

    up, down = (0, (3, 2, 1, 0)), (1, (0, 1, 2, 3))

    @pl.when(odd_x == 0)
    def _():
        send(se_ref, *up)
        send(so_ref, *down)

    @pl.when(odd_x == 1)
    def _():
        send(se_ref, *down)
        send(so_ref, *up)


def rounds_kernel(
    ai_ref, ab_ref, ei_ref, exti_ref, eb_ref, extb_ref, start_ref, seeds_ref, re_ref, ro_ref, ms_ref,
    a_hbm, out_hbm, all_ref, s_ref, out_ref, sems,
):
    gx = lax.axis_index("gx")
    gz = lax.axis_index("gz")
    copies = [
        pltpu.make_async_copy(ai_ref, a_hbm.at[:, 1:3], sems.at[4]),
        pltpu.make_async_copy(ab_ref.at[:, 0:1], a_hbm.at[:, 0:1], sems.at[5]),
        pltpu.make_async_copy(ab_ref.at[:, 1:2], a_hbm.at[:, 3:4], sems.at[6]),
    ]
    for copy in copies:
        copy.start()
    has_low = jnp.where(gx == 0, 0.0, 1.0)
    has_high = jnp.where(gx == 15, 0.0, 1.0)
    zero = jnp.zeros((40, 128), F32)

    def place(src_ref, places, has):
        packed = src_ref[10].astype(F32) * has
        high = places[0] == 8
        for j, at in enumerate(places):
            seeds = seeds_ref[1, j] if high else seeds_ref[0, 3 - j]
            s_ref[0, at, 0, 0:32] = seeds * has
            if j == 3:
                s_ref[0, at, 0, 32:40] = zero[0:8]
                s_ref[0, at, 1] = zero
                all_ref[at % 8 if high else 4 + at, 0, 0] = src_ref[9].astype(F32) * has
                all_ref[at % 8 if high else 4 + at, 0, 1] = zero
                continue
            s_ref[0, at, 0, 32:40] = src_ref[11, 8 * j : 8 * j + 8].astype(F32) * has / 15.0
            s_ref[0, at, 1] = unpack_ext(packed, 4 * j + 3, gz) / 15.0
            for f in range(3):
                where = at % 8 if high else 4 + at
                all_ref[where, f, 0] = src_ref[3 * j + f].astype(F32) * has
                all_ref[where, f, 1] = unpack_ext(packed, 4 * j + f, gz)

    def fill(low_ref, high_ref):
        place(low_ref, (3, 2, 1, 0), has_low)
        place(high_ref, (8, 9, 10, 11), has_high)

    by_side(re_ref, ro_ref, fill)

    for x in range(4):
        s_ref[0, 4 + x] = start_ref[x]

    def edge(at, f, i):
        if at < 4 or at > 7:
            return all_ref[4 + at if at < 4 else at - 8, f, i]
        if at in (5, 6):
            return (ei_ref, exti_ref)[i][at - 4, f]
        return (eb_ref, extb_ref)[i][(at - 4) // 3, f]

    lane = iota((40, 128), 1)

    def down(pair):
        a, b = pltpu.roll(pair[0], 1, 1), pltpu.roll(pair[1], 1, 1)
        return jnp.where(lane == 0, b, a), jnp.where(lane == 0, a, b)

    def up(pair):
        a, b = pltpu.roll(pair[0], 127, 1), pltpu.roll(pair[1], 127, 1)
        return jnp.where(lane == 127, b, a), jnp.where(lane == 127, a, b)

    for r in range(ROUNDS):
        src, dst = r % 2, (r + 1) % 2
        for x in range(r + 1, 11 - r):
            here = (s_ref[src, x, 0], s_ref[src, x, 1])
            ez = (edge(x, 2, 0), edge(x, 2, 1))
            z_low = down(here)
            z_high = up(tuple(jnp.minimum(here[i], ez[i]) for i in range(2)))
            for i in range(1 if r == ROUNDS - 1 else 2):
                ey = edge(x, 1, i)
                value = here[i]
                value = jnp.maximum(value, jnp.minimum(s_ref[src, x - 1, i], edge(x, 0, i)))
                value = jnp.maximum(value, jnp.minimum(s_ref[src, x + 1, i], edge(x + 1, 0, i)))
                value = jnp.maximum(value, jnp.minimum(pltpu.roll(here[i], 1, 0), ey))
                value = jnp.maximum(value, pltpu.roll(jnp.minimum(here[i], ey), 39, 0))
                value = jnp.maximum(value, jnp.minimum(z_low[i], ez[i]))
                value = jnp.maximum(value, z_high[i])
                if r < ROUNDS - 1:
                    s_ref[dst, x, i] = value
                else:
                    out_ref[x - 4] = value[0:32] * ms_ref[0, x - 4]
                    copies.append(
                        pltpu.make_async_copy(out_ref.at[x - 4], out_hbm.at[x - 4], sems.at[x - 4])
                    )
                    copies[-1].start()
    for copy in copies:
        copy.wait()


def stay(value):
    return pltpu.with_memory_space_constraint(value, pltpu.HBM)


def call(kernel, shapes, args, scratch=(), specs=None, out_specs=None):
    return pl.pallas_call(
        kernel,
        out_shape=[jax.ShapeDtypeStruct(s, d) for s, d in shapes],
        in_specs=specs or [VMEM] * len(args),
        out_specs=out_specs or [VMEM] * len(shapes),
        scratch_shapes=[pltpu.VMEM(*s) if isinstance(s[0], tuple) else s[0](*s[1:]) for s in scratch],
        compiler_params=PARAMS,
    )(*args)


def body(features, conv_weight, conv_bias, head_weight, head_bias, mask, seeds):
    v, zs, ms, fe, fo = call(
        pack_kernel,
        [
            ((4, 46, 32, 128), BF16),
            ((320, 128), BF16),
            ((2, 4, 32, 128), F32),
            ((36, 32, 128), BF16),
            ((36, 32, 128), BF16),
        ],
        tuple(stay(a) for a in (features, mask, seeds)),
        scratch=[
            ((4, 32, 32, 128), BF16),
            ((4, 32, 128), jnp.int32),
            ((4, 32, 128), jnp.int32),
            (pltpu.SemaphoreType.DMA, (6,)),
        ],
        specs=[HBM] * 3,
    )
    zr = lax.ppermute(zs, "gz", [(0, 1), (1, 0)])
    even_x, odd_x = swaps("gx")
    axes = ("gx", "gy")
    fo = lax.ppermute(fo, axes, odd_x)
    fe = lax.ppermute(fe, axes, even_x)
    pt, ye, yo = call(
        yface_kernel,
        [((4, 2, 32, 128), BF16), ((4, 208, 128), BF16), ((4, 208, 128), BF16)],
        (v, zs, zr, ms),
        scratch=[((2, 4, 16, 128), F32)],
    )
    ye, yo, vy, conv_weight, conv_bias, head_weight, head_bias = lax.optimization_barrier(
        (ye, yo, v, conv_weight, conv_bias, head_weight, head_bias)
    )
    taps = jnp.transpose(conv_weight, (2, 3, 4, 0, 1)).reshape(27, 32, 32)
    forms = call(
        weights_kernel,
        [
            ((96, 288), BF16),
            ((288, 96), BF16),
            ((32, 128), F32),
            ((24, 256), F32),
            ((24, 128), F32),
            ((8, 32), F32),
            ((8, 128), F32),
        ],
        tuple(stay(a) for a in (taps, conv_bias.reshape(1, 32), head_weight, head_bias)),
        scratch=[
            ((27, 32, 32), BF16),
            ((1, 32), F32),
            ((3, 32), BF16),
            (pltpu.SMEM, (3,), F32),
            (pltpu.SemaphoreType.DMA, (4,)),
        ],
        specs=[HBM] * 4,
    )
    weights = tuple(forms)
    rows_shape = [((2, 1280, 128), BF16)]
    (inner_rows,) = call(inner_rows_kernel, rows_shape, (vy, weights[0], weights[2]))
    even, odd = swaps("gy")
    yo = lax.ppermute(yo, axes, odd)
    ye = lax.ppermute(ye, axes, even)
    ye, yo, inner_rows = lax.optimization_barrier((ye, yo, inner_rows))
    v, xe, xo = call(
        xface_kernel,
        [((4, 46, 32, 128), BF16), ((13, 32, 128), BF16), ((13, 32, 128), BF16)],
        (v, pt, ye, yo),
    )
    xe, xo, v, fe, fo = lax.optimization_barrier((xe, xo, v, fe, fo))
    xo = lax.ppermute(xo, axes, odd_x)
    xe = lax.ppermute(xe, axes, even_x)
    inner_a, e, ext, tiles, slots, start = call(
        inner_kernel,
        [
            ((3, 2, 32, 128), BF16),
            ((4, 4, 40, 128), F32),
            ((4, 4, 40, 128), F32),
            ((2, 3, 40, 128), BF16),
            ((2, 40, 128), F32),
            ((4, 2, 40, 128), F32),
        ],
        (v, inner_rows, ye, yo, zr, ms) + weights,
        scratch=[((2, 1280, 128), BF16), ((2, 4, 40, 128), F32), ((2, 4, 40, 128), F32)],
    )
    border_rows, faces, side_seeds = call(
        border_rows_kernel,
        rows_shape + [((2, 46, 32, 128), BF16), ((2, 4, 32, 128), F32)],
        (v, fe, fo, weights[0], weights[2]),
    )
    xe, xo, e, ext, border_rows, faces = lax.optimization_barrier(
        (xe, xo, e, ext, border_rows, faces)
    )
    border_a, border_e, border_ext, se, so = call(
        border_kernel,
        [
            ((3, 2, 32, 128), BF16),
            ((2, 3, 40, 128), F32),
            ((2, 3, 40, 128), F32),
            ((12, 40, 128), BF16),
            ((12, 40, 128), BF16),
        ],
        (v, faces, border_rows, xe, xo, e, ext, tiles, slots) + weights,
        scratch=[((2, 46, 32, 128), BF16), ((2, 1280, 128), BF16)],
    )
    so = lax.ppermute(so, axes, odd_x)
    se = lax.ppermute(se, axes, even_x)
    affinity, strength = call(
        rounds_kernel,
        [((3, 4, 32, 128), BF16), ((4, 32, 128), F32)],
        (inner_a, border_a, e, ext, border_e, border_ext, start, side_seeds, se, so, ms),
        scratch=[
            ((8, 3, 2, 40, 128), F32),
            ((2, 12, 2, 40, 128), F32),
            ((4, 32, 128), F32),
            (pltpu.SemaphoreType.DMA, (7,)),
        ],
        out_specs=[HBM, HBM],
    )
    return (affinity, strength)


def solution(mesh):
    in_specs = (
        P(None, "gx", "gy", "gz"),
        P(),
        P(),
        P(),
        P(),
        P("gx", "gy", "gz"),
        P("gx", "gy", "gz"),
    )
    out_specs = (P(None, "gx", "gy", "gz"), P("gx", "gy", "gz"))
    return jax.shard_map(body, mesh=mesh, in_specs=in_specs, out_specs=out_specs, check_vma=False)
```

```python
import jax
import jax.numpy as jnp
from jax import lax
from jax.experimental import pallas as pl
from jax.experimental.pallas import tpu as pltpu
from jax.sharding import PartitionSpec as P

ROUNDS = 4
F32 = jnp.float32
BF16 = jnp.bfloat16
VMEM = pl.BlockSpec(memory_space=pltpu.VMEM)
HBM = pl.BlockSpec(memory_space=pltpu.HBM)
PARAMS = pltpu.CompilerParams(vmem_limit_bytes=12 * 2**20)


def swaps(axis):
    nx, ny = lax.axis_size("gx"), lax.axis_size("gy")

    def partner(x, y, first):
        at, count = (x, nx) if axis == "gx" else (y, ny)
        other = at + 1 if at % 2 == first else at - 1
        inside = 0 <= other < count
        if axis == "gx":
            return (other, y) if inside else (x, y ^ 1)
        return (x, other) if inside else (x ^ 1, y)

    def pairs(first):
        out = []
        for x in range(nx):
            for y in range(ny):
                px, py = partner(x, y, first)
                out.append((x * ny + y, px * ny + py))
        return out

    return pairs(0), pairs(1)


def iota(shape, dim):
    return lax.broadcasted_iota(jnp.int32, shape, dim)


def pack_kernel(x_hbm, m_hbm, s_hbm, v_ref, zs_ref, ms_ref, xe_ref, xo_ref, x_ref, m_ref, s_ref, sems):
    gz = lax.axis_index("gz")
    copies = [pltpu.make_async_copy(x_hbm.at[:, x], x_ref.at[x], sems.at[x]) for x in range(4)]
    small = [
        pltpu.make_async_copy(m_hbm, m_ref, sems.at[4]),
        pltpu.make_async_copy(s_hbm, s_ref, sems.at[5]),
    ]
    for copy in copies[:1] + small + copies[1:]:
        copy.start()
    lane = iota((128, 128), 1)
    row = iota((128, 128), 0)
    base = jnp.where(gz == 0, 120, 0)
    hit = row == base + lane % 8
    sels = [jnp.where(hit & (lane // 8 == y), 1.0, 0.0).astype(BF16) for y in range(16)]
    copies[0].wait()
    v_ref[0, 5:37] = jnp.swapaxes(x_ref[0], 0, 1)
    for copy in small:
        copy.wait()
    lane = iota((32, 128), 1)
    edge = (lane >= jnp.where(gz == 0, 124, 0)) & (lane < jnp.where(gz == 0, 128, 4))
    packed = jnp.zeros((32, 128), F32)
    for x in range(4):
        mask = m_ref[x].astype(F32)
        seed = mask * s_ref[x].astype(F32)
        ms_ref[0, x] = mask
        ms_ref[1, x] = seed
        xe_ref[32 + x] = seed.astype(BF16)
        xo_ref[32 + x] = seed.astype(BF16)
        for slot, value in ((x, mask), (4 + x, seed)):
            value = jnp.where(edge, value, 0.0)
            packed = packed + (pltpu.roll(value, 8 * slot, 1) if slot else value)
    zs_ref[256:288] = packed.astype(BF16)
    for x in range(1, 4):
        copies[x].wait()
        v_ref[x, 5:37] = jnp.swapaxes(x_ref[x], 0, 1)
    lhs = jnp.concatenate(
        [
            jnp.concatenate(
                [v_ref[x, 5 + 16 * half + y] for x in range(4) for half in range(2)], axis=0
            )
            for y in range(16)
        ],
        axis=1,
    )
    edges = jnp.dot(lhs, jnp.concatenate(sels, axis=0), preferred_element_type=F32)
    zs_ref[0:256] = edges.astype(BF16)
    zs_ref[288:320] = jnp.zeros((32, 128), BF16)
    even_face = jnp.where(lax.axis_index("gx") % 2 == 0, 3, 0)
    xe_ref[0:32] = v_ref[even_face, 5:37]
    xo_ref[0:32] = v_ref[3 - even_face, 5:37]


def weights_kernel(
    t_hbm, b_hbm, h_hbm, hb_hbm, w_ref, wp_ref, bias_ref, hw_ref, hbias_ref, hwp_ref, hbp_ref,
    t_ref, b_ref, h_ref, hb_ref, sems,
):
    copies = [
        pltpu.make_async_copy(src, dst, sems.at[i])
        for i, (src, dst) in enumerate(
            ((t_hbm, t_ref), (b_hbm, b_ref), (h_hbm, h_ref), (hb_hbm, hb_ref))
        )
    ]
    for copy in copies:
        copy.start()
    for copy in copies:
        copy.wait()
    for dz in range(3):
        w_ref[32 * dz : 32 * dz + 32] = jnp.concatenate(
            [t_ref[3 * k + dz] for k in range(9)], axis=1
        )
    for k in range(9):
        wp_ref[32 * k : 32 * k + 32] = jnp.concatenate(
            [t_ref[9 * dx + k] for dx in range(3)], axis=1
        )
    across = jnp.broadcast_to(b_ref[...], (32, 32))
    diagonal = iota((32, 32), 0) == iota((32, 32), 1)
    column = jnp.sum(jnp.where(diagonal, across, 0.0), axis=1, keepdims=True)
    bias_ref[...] = jnp.broadcast_to(column, (32, 128))
    same = iota((8, 256), 0) == iota((8, 256), 1) // 32
    few = iota((8, 128), 0)
    hwp = jnp.zeros((8, 32), F32)
    hbp = jnp.zeros((8, 128), F32)
    heads = h_ref[...].astype(F32)
    for c in range(3):
        line = jnp.concatenate([heads[c : c + 1]] * 8, axis=1)
        hw_ref[8 * c : 8 * c + 8] = jnp.where(same, jnp.broadcast_to(line, (8, 256)), 0.0)
        hbias_ref[8 * c : 8 * c + 8] = jnp.full((8, 128), hb_ref[c], F32)
        hwp = jnp.where(few[:, 0:32] == c, jnp.broadcast_to(heads[c : c + 1], (8, 32)), hwp)
        hbp = jnp.where(few == c, hb_ref[c], hbp)
    hwp_ref[...] = hwp
    hbp_ref[...] = hbp


def unpack_ext(packed, slot, gz):
    lane = iota(packed.shape, 1)
    inside = (lane >= jnp.where(gz == 0, 0, 124)) & (lane < jnp.where(gz == 0, 4, 128))
    value = pltpu.roll(packed, (128 - 8 * slot) % 128, 1) if slot else packed
    return jnp.where(inside, value, 0.0)


def yface_kernel(v_ref, zs_ref, zr_ref, ms_ref, pt_ref, ye_ref, yo_ref, block_ref):
    odd = lax.axis_index("gy") % 2
    gz = lax.axis_index("gz")
    lane = iota((256, 128), 1) % 8
    own = pltpu.roll(zs_ref[0:256].astype(F32), jnp.where(gz == 0, 122, 5), 1)
    other = pltpu.roll(zr_ref[0:256].astype(F32), jnp.where(gz == 0, 2, 125), 1)
    own_from = jnp.where(gz == 0, 0, 5)
    other_from = jnp.where(gz == 0, 2, 0)
    packed = jnp.where((lane >= own_from) & (lane < own_from + 2), own, 0.0)
    packed = jnp.where((lane >= other_from) & (lane < other_from + 5), other, packed)
    packed = packed.astype(BF16).reshape(4, 2, 32, 128)
    pt_ref[...] = packed
    zmask = zr_ref[256:288].astype(F32)
    for x in range(4):
        fields = (ms_ref[0, x], ms_ref[1, x], unpack_ext(zmask, x, gz), unpack_ext(zmask, 4 + x, gz))
        for f, value in enumerate(fields):
            block_ref[0, x, 4 * f : 4 * f + 4] = value[28:32]
            block_ref[1, x, 4 * f : 4 * f + 4] = value[0:4]

    def write(dst_ref, up):
        for x in range(4):
            first = 32 if up else 5
            for j in range(5):
                dst_ref[x, 32 * j : 32 * j + 32] = v_ref[x, first + j]
            dst_ref[x, 160:192] = pt_ref[x, 1 if up else 0]
            dst_ref[x, 192:208] = block_ref[0 if up else 1, x].astype(BF16)

    @pl.when(odd == 0)
    def _():
        write(ye_ref, True)
        write(yo_ref, False)

    @pl.when(odd == 1)
    def _():
        write(ye_ref, False)
        write(yo_ref, True)


def xface_kernel(v_in_ref, pt_ref, ye_ref, yo_ref, v_ref, xe_ref, xo_ref):
    odd_x = lax.axis_index("gx") % 2
    odd_y = lax.axis_index("gy") % 2

    gy = lax.axis_index("gy")
    for x in range(4):
        v_ref[x, 5:37] = v_in_ref[x, 5:37]

    def fill(low_ref, high_ref):
        for x in range(4):
            for j in range(5):
                v_ref[x, j] = low_ref[x, 32 * j : 32 * j + 32]
                v_ref[x, 37 + j] = high_ref[x, 32 * j : 32 * j + 32]
            v_ref[x, 42] = low_ref[x, 160:192]
            v_ref[x, 43] = pt_ref[x, 0]
            v_ref[x, 44] = pt_ref[x, 1]
            v_ref[x, 45] = high_ref[x, 160:192]

    @pl.when(odd_y == 0)
    def _():
        fill(yo_ref, ye_ref)

    @pl.when(odd_y == 1)
    def _():
        fill(ye_ref, yo_ref)

    zero = jnp.zeros((32, 128), BF16)

    @pl.when(gy == 0)
    def _():
        for x in range(4):
            for tile in (0, 1, 2, 3, 4, 42):
                v_ref[x, tile] = zero

    @pl.when(gy == 7)
    def _():
        for x in range(4):
            for tile in (37, 38, 39, 40, 41, 45):
                v_ref[x, tile] = zero

    even_face = jnp.where(odd_x == 0, 3, 0)
    for dst_ref, face in ((xe_ref, even_face), (xo_ref, 3 - even_face)):
        dst_ref[0:4] = v_ref[face, 1:5]
        dst_ref[4:13] = v_ref[face, 37:46]


def head(hidden, head_ref, bias_ref):
    logits = jnp.dot(head_ref[...].astype(BF16), hidden, preferred_element_type=F32)
    logits = logits + jnp.tile(bias_ref[...], (1, logits.shape[1] // 128))
    return jax.nn.sigmoid(logits).astype(BF16).astype(F32)


def tile_of(row):
    return row + 5 if row < 36 else row - 35


def spread_matrix(gz):
    k = iota((512, 128), 0) % 8
    to = iota((512, 128), 1)
    goal = jnp.where(gz == 0, (k + 126) % 128, (k + 123) % 128)
    return jnp.where((k >= 1) & (k <= 5) & (to == goal), 1.0, 0.0).astype(BF16)


INTERIOR = tuple(range(1, 31))
OTHERS = (31, 32, 33, 34, 35, 36, 37, 38, 39, 0)


def conv_main(refs, weights, hid_ref, rows):
    lane = iota((32, 128), 1)
    first, last = lane == 0, lane == 127
    w, bias = weights[0][...], weights[2][...]
    for pair in zip(rows[0::2], rows[1::2]):
        cols = []
        for row in pair:
            t = tile_of(row)
            cols.append(
                jnp.concatenate([r[t - 1 : t + 2].reshape(96, 128) for r in refs], axis=0)
            )
        part = jnp.dot(w, jnp.concatenate(cols, axis=1), preferred_element_type=F32)
        for i, row in enumerate(pair):
            one = part[:, 128 * i : 128 * i + 128]
            left = jnp.where(first, 0.0, pltpu.roll(one[0:32], 1, 1))
            right = jnp.where(last, 0.0, pltpu.roll(one[64:96], 127, 1))
            hid = jnp.maximum(one[32:64] + left + right + bias, 0.0)
            hid_ref[32 * row : 32 * row + 32] = hid.astype(BF16)


def conv_packed(refs, weights, spread):
    _, wp_ref, b_ref, _, _, hwp_ref, hbp_ref = weights
    cols = [jnp.concatenate([r[42 + q] for r in refs], axis=0) for q in range(4)]
    part = jnp.dot(wp_ref[...], jnp.concatenate(cols, axis=1), preferred_element_type=F32)
    total = jnp.tile(b_ref[...], (1, 4))
    for dy in range(3):
        for dz in range(3):
            k = 3 * dy + dz
            shift = (-(8 * (dy - 1) + dz - 1)) % 512
            one = part[32 * k : 32 * k + 32]
            total = total + (pltpu.roll(one, shift, 1) if shift else one)
    value = head(jnp.maximum(total, 0.0).astype(BF16), hwp_ref, hbp_ref)
    row = iota((40, 512), 0)
    at = iota((40, 512), 1)
    mine = at // 8 - 16 == jnp.where(row < 36, row, row - 40)
    lhs = jnp.concatenate(
        [jnp.where(mine, jnp.broadcast_to(value[c : c + 1], (40, 512)), 0.0) for c in range(3)],
        axis=0,
    ).astype(BF16)
    return jnp.dot(lhs, spread, preferred_element_type=F32)


def conv_slice(gz, refs, weights, spread, interior_ref, hid_ref):
    conv_main(refs, weights, hid_ref, OTHERS)
    border = conv_packed(refs, weights, spread)

    def hidden(row):
        return (interior_ref if row in INTERIOR else hid_ref)[32 * row : 32 * row + 32]

    hid = jnp.concatenate(
        [jnp.concatenate([hidden(8 * g + i) for i in range(8)], axis=0) for g in range(5)], axis=1
    )
    value = head(hid, weights[3], weights[4])
    fixed = iota((40, 128), 1) == jnp.where(gz == 0, 127, 0)
    out = []
    for c in range(3):
        main = jnp.concatenate(
            [value[8 * c : 8 * c + 8, 128 * g : 128 * g + 128] for g in range(5)], axis=0
        )
        one = border[40 * c : 40 * c + 40]
        out.append((jnp.where(fixed, one, main), jnp.where(fixed, 0.0, one)))
    return out


def inner_rows_kernel(v_ref, w_ref, b_ref, hid_ref):
    for x in (1, 2):
        refs = [v_ref.at[x - 1 + d] for d in range(3)]
        conv_main(refs, (w_ref, None, b_ref), hid_ref.at[x - 1], INTERIOR)


def by_side(even_ref, odd_ref, fill):
    gx = lax.axis_index("gx")

    @pl.when(gx % 2 == 0)
    def _():
        fill(odd_ref, even_ref)

    @pl.when(gx % 2 == 1)
    def _():
        fill(even_ref, odd_ref)


def border_rows_kernel(v_ref, xe_ref, xo_ref, w_ref, b_ref, hid_ref, face_ref, seeds_ref):
    gx = lax.axis_index("gx")

    def fill(low_ref, high_ref):
        face_ref[0, 5:37] = low_ref[0:32]
        face_ref[1, 5:37] = high_ref[0:32]
        seeds_ref[0] = low_ref[32:36].astype(F32) / 15.0
        seeds_ref[1] = high_ref[32:36].astype(F32) / 15.0

    by_side(xe_ref, xo_ref, fill)

    @pl.when(gx == 0)
    def _():
        face_ref[0, 5:37] = jnp.zeros((32, 32, 128), BF16)

    @pl.when(gx == 15)
    def _():
        face_ref[1, 5:37] = jnp.zeros((32, 32, 128), BF16)

    for i, refs in enumerate(
        (
            [face_ref.at[0], v_ref.at[0], v_ref.at[1]],
            [v_ref.at[2], v_ref.at[3], face_ref.at[1]],
        )
    ):
        conv_main(refs, (w_ref, None, b_ref), hid_ref.at[i], INTERIOR)


def inner_kernel(
    v_ref, rows_ref, ye_ref, yo_ref, zr_ref, ms_ref, w_ref, wp_ref, b_ref, hw_ref, hb_ref, hwp_ref, hbp_ref,
    a_ref, e_ref, ext_ref, tile_ref, slots_ref, start_ref, hid_ref, mask_ref, mext_ref,
):
    gy = lax.axis_index("gy")
    odd_y = gy % 2
    gz = lax.axis_index("gz")
    zmask = zr_ref[256:288].astype(F32)
    for x in range(4):
        for f in range(2):
            mask_ref[f, x, 0:32] = ms_ref[f, x]
            mext_ref[f, x, 0:32] = unpack_ext(zmask, 4 * f + x, gz)

    def fill(lower_ref, upper_ref):
        has_lower = jnp.where(gy == 0, 0.0, 1.0)
        has_upper = jnp.where(gy == 7, 0.0, 1.0)
        for x in range(4):
            lower = lower_ref[x, 192:208].astype(F32) * has_lower
            upper = upper_ref[x, 192:208].astype(F32) * has_upper
            for f in range(2):
                mask_ref[f, x, 32:36] = upper[4 * f : 4 * f + 4]
                mask_ref[f, x, 36:40] = lower[4 * f : 4 * f + 4]
                mext_ref[f, x, 32:36] = upper[8 + 4 * f : 12 + 4 * f]
                mext_ref[f, x, 36:40] = lower[8 + 4 * f : 12 + 4 * f]

    @pl.when(odd_y == 0)
    def _():
        fill(yo_ref, ye_ref)

    @pl.when(odd_y == 1)
    def _():
        fill(ye_ref, yo_ref)

    lane = iota((40, 128), 1)
    row = iota((40, 128), 0)

    def shift_y(value):
        return jnp.where(row == 36, 0.0, pltpu.roll(value, 1, 0))

    weights = (w_ref, wp_ref, b_ref, hw_ref, hb_ref, hwp_ref, hbp_ref)
    spread = spread_matrix(gz)
    for x in range(4):
        main, ext = mask_ref[0, x], mext_ref[0, x]
        rolled, rolled_ext = pltpu.roll(main, 1, 1), pltpu.roll(ext, 1, 1)
        z_main = main * jnp.where(lane == 0, rolled_ext, rolled)
        z_ext = ext * jnp.where(lane == 0, rolled, rolled_ext)
        y_main, y_ext = main * shift_y(main), ext * shift_y(ext)
        x_main = main * mask_ref[0, x - 1] if x else main
        x_ext = ext * mext_ref[0, x - 1] if x else ext
        keep = ((x_main, x_ext), (y_main, y_ext), (z_main, z_ext))
        if 0 < x < 3:
            refs = [v_ref.at[x - 1 + d] for d in range(3)]
            a = conv_slice(gz, refs, weights, spread, rows_ref.at[x - 1], hid_ref.at[x - 1])
            for f in range(3):
                a_ref[f, x - 1] = a[f][0][0:32].astype(BF16)
                e_ref[x, f] = a[f][0] * keep[f][0]
                ext_ref[x, f] = a[f][1] * keep[f][1]
                tile_ref[x - 1, f] = e_ref[x, f].astype(BF16)
        else:
            for f in range(3):
                e_ref[x, f] = keep[f][0]
                ext_ref[x, f] = keep[f][1]
        e_ref[x, 3] = mask_ref[1, x]
        ext_ref[x, 3] = mext_ref[1, x]
        start_ref[x, 0] = mask_ref[1, x] / 15.0
        start_ref[x, 1] = mext_ref[1, x] / 15.0
    for way, order in enumerate(((2, 1), (1, 2))):
        packed = jnp.zeros((40, 128), F32)
        for j, x in enumerate(order):
            for f in range(4):
                packed = packed + pltpu.roll(ext_ref[x, f], 8 * (4 * (j + 1) + f), 1)
        slots_ref[way] = packed


def border_kernel(
    v_ref, face_ref, rows_ref, xe_ref, xo_ref, e_in, ext_in, tile_ref, slots_ref, w_ref, wp_ref, b_ref, hw_ref, hb_ref, hwp_ref, hbp_ref,
    a_ref, e_ref, ext_ref, se_ref, so_ref, side_ref, hid_ref,
):
    gx = lax.axis_index("gx")
    odd_x = gx % 2
    gz = lax.axis_index("gz")

    def fill(low_ref, high_ref):
        for i, ref in enumerate((low_ref, high_ref)):
            side_ref[i, 0] = jnp.zeros((32, 128), BF16)
            side_ref[i, 1:5] = ref[0:4]
            side_ref[i, 37:46] = ref[4:13]

    by_side(xe_ref, xo_ref, fill)
    for i, end in ((0, 0), (1, 15)):
        for at in (5, 6, 35, 36):
            side_ref[i, at] = face_ref[i, at]

        @pl.when(gx == end)
        def _():
            side_ref[i, 0:5] = jnp.zeros((5, 32, 128), BF16)
            side_ref[i, 37:46] = jnp.zeros((9, 32, 128), BF16)

    weights = (w_ref, wp_ref, b_ref, hw_ref, hb_ref, hwp_ref, hbp_ref)
    spread = spread_matrix(gz)
    for x, refs in (
        (0, [side_ref.at[0], v_ref.at[0], v_ref.at[1]]),
        (3, [v_ref.at[2], v_ref.at[3], side_ref.at[1]]),
    ):
        a = conv_slice(gz, refs, weights, spread, rows_ref.at[x // 3], hid_ref.at[x // 3])
        for f in range(3):
            a_ref[f, x // 3] = a[f][0][0:32].astype(BF16)
            e_ref[x // 3, f] = a[f][0] * e_in[x, f]
            ext_ref[x // 3, f] = a[f][1] * ext_in[x, f]

    def send(dst_ref, way, order):
        packed = slots_ref[way]
        for f in range(4):
            x = order[0]
            value = ext_ref[x // 3, f] if f < 3 else ext_in[x, 3]
            packed = packed + (pltpu.roll(value, 8 * f, 1) if f else value)
        for f in range(3):
            dst_ref[f] = e_ref[order[0] // 3, f].astype(BF16)
            dst_ref[3 + f] = tile_ref[order[1] - 1, f]
            dst_ref[6 + f] = tile_ref[order[2] - 1, f]
            dst_ref[11, 8 * f : 8 * f + 8] = e_in[order[f], 3, 32:40].astype(BF16)
        dst_ref[9] = e_ref[order[3] // 3, 0].astype(BF16)
        dst_ref[10] = packed.astype(BF16)

    up, down = (0, (3, 2, 1, 0)), (1, (0, 1, 2, 3))

    @pl.when(odd_x == 0)
    def _():
        send(se_ref, *up)
        send(so_ref, *down)

    @pl.when(odd_x == 1)
    def _():
        send(se_ref, *down)
        send(so_ref, *up)


def rounds_kernel(
    ai_ref, ab_ref, ei_ref, exti_ref, eb_ref, extb_ref, start_ref, seeds_ref, re_ref, ro_ref, ms_ref,
    a_hbm, out_hbm, all_ref, s_ref, out_ref, sems,
):
    gx = lax.axis_index("gx")
    gz = lax.axis_index("gz")
    copies = [
        pltpu.make_async_copy(ai_ref, a_hbm.at[:, 1:3], sems.at[4]),
        pltpu.make_async_copy(ab_ref.at[:, 0:1], a_hbm.at[:, 0:1], sems.at[5]),
        pltpu.make_async_copy(ab_ref.at[:, 1:2], a_hbm.at[:, 3:4], sems.at[6]),
    ]
    for copy in copies:
        copy.start()
    has_low = jnp.where(gx == 0, 0.0, 1.0)
    has_high = jnp.where(gx == 15, 0.0, 1.0)
    zero = jnp.zeros((40, 128), F32)

    def place(src_ref, places, has):
        packed = src_ref[10].astype(F32) * has
        high = places[0] == 8
        for j, at in enumerate(places):
            seeds = seeds_ref[1, j] if high else seeds_ref[0, 3 - j]
            s_ref[0, at, 0, 0:32] = seeds * has
            if j == 3:
                s_ref[0, at, 0, 32:40] = zero[0:8]
                s_ref[0, at, 1] = zero
                all_ref[at % 8 if high else 4 + at, 0, 0] = src_ref[9].astype(F32) * has
                all_ref[at % 8 if high else 4 + at, 0, 1] = zero
                continue
            s_ref[0, at, 0, 32:40] = src_ref[11, 8 * j : 8 * j + 8].astype(F32) * has / 15.0
            s_ref[0, at, 1] = unpack_ext(packed, 4 * j + 3, gz) / 15.0
            for f in range(3):
                where = at % 8 if high else 4 + at
                all_ref[where, f, 0] = src_ref[3 * j + f].astype(F32) * has
                all_ref[where, f, 1] = unpack_ext(packed, 4 * j + f, gz)

    def fill(low_ref, high_ref):
        place(low_ref, (3, 2, 1, 0), has_low)
        place(high_ref, (8, 9, 10, 11), has_high)

    by_side(re_ref, ro_ref, fill)

    for x in range(4):
        s_ref[0, 4 + x] = start_ref[x]

    def edge(at, f, i):
        if at < 4 or at > 7:
            return all_ref[4 + at if at < 4 else at - 8, f, i]
        if at in (5, 6):
            return (ei_ref, exti_ref)[i][at - 4, f]
        return (eb_ref, extb_ref)[i][(at - 4) // 3, f]

    lane = iota((40, 128), 1)

    def down(pair):
        a, b = pltpu.roll(pair[0], 1, 1), pltpu.roll(pair[1], 1, 1)
        return jnp.where(lane == 0, b, a), jnp.where(lane == 0, a, b)

    def up(pair):
        a, b = pltpu.roll(pair[0], 127, 1), pltpu.roll(pair[1], 127, 1)
        return jnp.where(lane == 127, b, a), jnp.where(lane == 127, a, b)

    for r in range(ROUNDS):
        src, dst = r % 2, (r + 1) % 2
        for x in range(r + 1, 11 - r):
            here = (s_ref[src, x, 0], s_ref[src, x, 1])
            ez = (edge(x, 2, 0), edge(x, 2, 1))
            z_low = down(here)
            z_high = up(tuple(jnp.minimum(here[i], ez[i]) for i in range(2)))
            for i in range(1 if r == ROUNDS - 1 else 2):
                ey = edge(x, 1, i)
                value = here[i]
                value = jnp.maximum(value, jnp.minimum(s_ref[src, x - 1, i], edge(x, 0, i)))
                value = jnp.maximum(value, jnp.minimum(s_ref[src, x + 1, i], edge(x + 1, 0, i)))
                value = jnp.maximum(value, jnp.minimum(pltpu.roll(here[i], 1, 0), ey))
                value = jnp.maximum(value, pltpu.roll(jnp.minimum(here[i], ey), 39, 0))
                value = jnp.maximum(value, jnp.minimum(z_low[i], ez[i]))
                value = jnp.maximum(value, z_high[i])
                if r < ROUNDS - 1:
                    s_ref[dst, x, i] = value
                else:
                    out_ref[x - 4] = value[0:32] * ms_ref[0, x - 4]
                    copies.append(
                        pltpu.make_async_copy(out_ref.at[x - 4], out_hbm.at[x - 4], sems.at[x - 4])
                    )
                    copies[-1].start()
    for copy in copies:
        copy.wait()


def stay(value):
    return pltpu.with_memory_space_constraint(value, pltpu.HBM)


def call(kernel, shapes, args, scratch=(), specs=None, out_specs=None):
    return pl.pallas_call(
        kernel,
        out_shape=[jax.ShapeDtypeStruct(s, d) for s, d in shapes],
        in_specs=specs or [VMEM] * len(args),
        out_specs=out_specs or [VMEM] * len(shapes),
        scratch_shapes=[pltpu.VMEM(*s) if isinstance(s[0], tuple) else s[0](*s[1:]) for s in scratch],
        compiler_params=PARAMS,
    )(*args)


def body(features, conv_weight, conv_bias, head_weight, head_bias, mask, seeds):
    v, zs, ms, fe, fo = call(
        pack_kernel,
        [
            ((4, 46, 32, 128), BF16),
            ((320, 128), BF16),
            ((2, 4, 32, 128), F32),
            ((36, 32, 128), BF16),
            ((36, 32, 128), BF16),
        ],
        tuple(stay(a) for a in (features, mask, seeds)),
        scratch=[
            ((4, 32, 32, 128), BF16),
            ((4, 32, 128), jnp.int32),
            ((4, 32, 128), jnp.int32),
            (pltpu.SemaphoreType.DMA, (6,)),
        ],
        specs=[HBM] * 3,
    )
    zr = lax.ppermute(zs, "gz", [(0, 1), (1, 0)])
    even_x, odd_x = swaps("gx")
    axes = ("gx", "gy")
    fo = lax.ppermute(fo, axes, odd_x)
    fe = lax.ppermute(fe, axes, even_x)
    pt, ye, yo = call(
        yface_kernel,
        [((4, 2, 32, 128), BF16), ((4, 208, 128), BF16), ((4, 208, 128), BF16)],
        (v, zs, zr, ms),
        scratch=[((2, 4, 16, 128), F32)],
    )
    ye, yo, vy, conv_weight, conv_bias, head_weight, head_bias = lax.optimization_barrier(
        (ye, yo, v, conv_weight, conv_bias, head_weight, head_bias)
    )
    taps = jnp.transpose(conv_weight, (2, 3, 4, 0, 1)).reshape(27, 32, 32)
    forms = call(
        weights_kernel,
        [
            ((96, 288), BF16),
            ((288, 96), BF16),
            ((32, 128), F32),
            ((24, 256), F32),
            ((24, 128), F32),
            ((8, 32), F32),
            ((8, 128), F32),
        ],
        tuple(stay(a) for a in (taps, conv_bias.reshape(1, 32), head_weight, head_bias)),
        scratch=[
            ((27, 32, 32), BF16),
            ((1, 32), F32),
            ((3, 32), BF16),
            (pltpu.SMEM, (3,), F32),
            (pltpu.SemaphoreType.DMA, (4,)),
        ],
        specs=[HBM] * 4,
    )
    weights = tuple(forms)
    rows_shape = [((2, 1280, 128), BF16)]
    (inner_rows,) = call(inner_rows_kernel, rows_shape, (vy, weights[0], weights[2]))
    even, odd = swaps("gy")
    yo = lax.ppermute(yo, axes, odd)
    ye = lax.ppermute(ye, axes, even)
    ye, yo, inner_rows = lax.optimization_barrier((ye, yo, inner_rows))
    v, xe, xo = call(
        xface_kernel,
        [((4, 46, 32, 128), BF16), ((13, 32, 128), BF16), ((13, 32, 128), BF16)],
        (v, pt, ye, yo),
    )
    xe, xo, v, fe, fo = lax.optimization_barrier((xe, xo, v, fe, fo))
    xo = lax.ppermute(xo, axes, odd_x)
    xe = lax.ppermute(xe, axes, even_x)
    inner_a, e, ext, tiles, slots, start = call(
        inner_kernel,
        [
            ((3, 2, 32, 128), BF16),
            ((4, 4, 40, 128), F32),
            ((4, 4, 40, 128), F32),
            ((2, 3, 40, 128), BF16),
            ((2, 40, 128), F32),
            ((4, 2, 40, 128), F32),
        ],
        (v, inner_rows, ye, yo, zr, ms) + weights,
        scratch=[((2, 1280, 128), BF16), ((2, 4, 40, 128), F32), ((2, 4, 40, 128), F32)],
    )
    border_rows, faces, side_seeds = call(
        border_rows_kernel,
        rows_shape + [((2, 46, 32, 128), BF16), ((2, 4, 32, 128), F32)],
        (v, fe, fo, weights[0], weights[2]),
    )
    xe, xo, e, ext, border_rows, faces = lax.optimization_barrier(
        (xe, xo, e, ext, border_rows, faces)
    )
    border_a, border_e, border_ext, se, so = call(
        border_kernel,
        [
            ((3, 2, 32, 128), BF16),
            ((2, 3, 40, 128), F32),
            ((2, 3, 40, 128), F32),
            ((12, 40, 128), BF16),
            ((12, 40, 128), BF16),
        ],
        (v, faces, border_rows, xe, xo, e, ext, tiles, slots) + weights,
        scratch=[((2, 46, 32, 128), BF16), ((2, 1280, 128), BF16)],
    )
    so = lax.ppermute(so, axes, odd_x)
    se = lax.ppermute(se, axes, even_x)
    affinity, strength = call(
        rounds_kernel,
        [((3, 4, 32, 128), BF16), ((4, 32, 128), F32)],
        (inner_a, border_a, e, ext, border_e, border_ext, start, side_seeds, se, so, ms),
        scratch=[
            ((8, 3, 2, 40, 128), F32),
            ((2, 12, 2, 40, 128), F32),
            ((4, 32, 128), F32),
            (pltpu.SemaphoreType.DMA, (7,)),
        ],
        out_specs=[HBM, HBM],
    )
    return (affinity, strength)


def solution(mesh):
    in_specs = (
        P(None, "gx", "gy", "gz"),
        P(),
        P(),
        P(),
        P(),
        P("gx", "gy", "gz"),
        P("gx", "gy", "gz"),
    )
    out_specs = (P(None, "gx", "gy", "gz"), P("gx", "gy", "gz"))
    return jax.shard_map(body, mesh=mesh, in_specs=in_specs, out_specs=out_specs, check_vma=False)
```
